32 devices in a mesh: groups: 2 (over x), seq: 16 (over z, y, core).
Axes of the slice: x: 2, y: 2, z: 4, core: 2. Of those that a mesh axis runs over, the one named last changes fastest.
Arguments:
- features: bfloat16 [3, 4096, 4096], P(None, ('groups', 'seq')), parts along dimension 1, may hold values from -6 to 6
- kernel: float32 [3, 3, 4096], replicated, may hold values from -3.5 to 3.5
- skip: float32 [4096], replicated, may hold values from -4 to 4
- residues: float32 [2, 16, 4096], replicated, may hold values from -3 to 3
- decay: float32 [16, 4096], replicated, may hold values from 9.765625e-05 to 0.041666667
- freq: float32 [16, 4096], replicated, may hold values from 0.001 to 0.5
- lengths: int32 [12], P('groups'), parts along dimension 0, may hold values from 1 to 1024, 2048 in all
Outputs:
- mixed: bfloat16 [4096, 4096], P(('groups', 'seq')), parts along dimension 0
The draws below stay inside these ranges and needn't reach their ends.
There are 2 independent parts, one for each index of `groups`. The reference program is written for one: setup_inputs(seed, part) draws one part's arguments, and reference() takes and returns one part's arrays. A program takes and returns all parts, laid end to end along the dimension named above; an argument that names none is the same for every part. Nothing has to cross between parts.
Inputs may be any that keep to these rules, and one draw needn't show every extreme that they name: The lengths sum to 2048; the longest is exactly 1024.
All inputs are finite; a program needn't handle non-finite values.
Results may differ from the reference program's by a relative error of at most 0.0065.
Values may be sent and summed in bfloat16 or wider, within the bound.
No kernel may reach another device: no remote copies, remote signals or barrier semaphores. Data moves between devices by JAX's collectives and lax.ppermute only.
A program may use at most 192 MiB of HBM per device.

```python
import math
import jax
import jax.numpy as jnp
import numpy as np
from jax import lax

C = 4096
M = 16
BLK = 16
NSEQ = 6
TOKENS = 2048
MOST = 1024


def draw_decay(key, part):
    pick_key, slow_key, fast_key = jax.random.split(key, 3)
    share = 0.5
    chooser = jax.random.uniform(pick_key, (M, C), jnp.float32)
    slow_lo = math.log(0.2 / TOKENS)
    slow_hi = math.log(2.0 / TOKENS)
    fast_lo = math.log(2.0 / TOKENS)
    fast_hi = math.log(1.0 / 24)
    slow_u = jax.random.uniform(slow_key, (M, C), jnp.float32)
    fast_u = jax.random.uniform(fast_key, (M, C), jnp.float32)
    slow_rate = jnp.exp(slow_lo + slow_u * (slow_hi - slow_lo))
    fast_rate = jnp.exp(fast_lo + fast_u * (fast_hi - fast_lo))
    return jnp.where(chooser < share, slow_rate, fast_rate).astype(jnp.float32)


def levels(rng, shape, pieces, low, high):
    def one(position, parts):
        draws = jax.random.uniform(jax.random.fold_in(jax.random.fold_in(rng, 6), position), (parts,), jnp.float32, low / len(pieces), high / len(pieces))
        return jnp.repeat(jnp.exp(draws), shape[position] // parts).reshape((-1,) + (1,) * (len(shape) - position - 1))

    level = one(*pieces[0])
    for cut in pieces[1:]:
        level = level * one(*cut)
    return level


def split_up(count, total, bound, lean):
    portions = [(1 << 20) // math.isqrt(grade ** lean) + 1 for grade in range(2, count + 1)]
    spare, given = total - bound - (count - 1), [1] * (count - 1)
    while spare > 0:
        candidates = [i for i in range(count - 1) if given[i] < bound]
        mass, budget = sum([portions[i] for i in candidates]), spare
        for i in candidates:
            extra = min(bound - given[i], max(1, budget * portions[i] // mass), spare)
            given[i] = given[i] + extra
            spare = spare - extra
    return np.array([bound] + given)


def ragged(own_key, number_of, total, most, skew):
    if number_of == 2:
        one = jax.random.randint(own_key, (), max(1, total - most), min(most, total - 1) + 1)
        return jnp.stack([one, total - one])
    sizes = jnp.asarray(split_up(number_of, total, most, skew), jnp.int32)
    twos = (number_of - 1) // 2
    giver, sink = sizes[1:1 + 2 * twos:2], sizes[2:2 + 2 * twos:2]
    slack = jnp.minimum(giver - 1, most - sink)
    moved = jax.random.randint(jax.random.fold_in(own_key, 1), (twos,), 0, 1 << 20) % (slack + 1)
    sizes = sizes.at[1:1 + 2 * twos:2].set(giver - moved).at[2:2 + 2 * twos:2].set(sink + moved)
    return sizes[jax.random.permutation(jax.random.fold_in(own_key, 2), number_of)]


def scatter_about(own_key, shape, scale, most, cuts=(), kind=jnp.bfloat16):
    gain = levels(own_key, shape, cuts, -0.22, 0.18) if cuts else 1.0
    array = jax.random.normal(own_key, shape, jnp.float32) * scale * gain
    return jnp.minimum(jnp.maximum(array, -most), most).astype(kind)


def setup_inputs(seed: int = 0, part: int = 0) -> dict:
    seeds = jax.random.split(jax.random.key(seed), 8)
    part_splits = jax.random.split(jax.random.fold_in(seeds[7], part), 8)
    features = scatter_about(part_splits[0], (3, TOKENS, C), 1.0, 6.0, ((1, 16),))
    kernel = scatter_about(seeds[1], (3, 3, C), 3 ** -0.5, 3.5, (), jnp.float32)
    skip = scatter_about(seeds[2], (C,), 1.0, 4.0, (), jnp.float32)
    residues = scatter_about(seeds[3], (2, M, C), 0.5, 3.0, (), jnp.float32)
    decay = draw_decay(jax.random.fold_in(seeds[7], 71), part)
    freq = jnp.clip(jnp.exp(jax.random.uniform(seeds[5], (M, C), jnp.float32, math.log(0.001), math.log(0.5))), 0.001, 0.5)
    lengths = ragged(part_splits[6], NSEQ, TOKENS, MOST, 2).astype(jnp.int32)
    return {"features": features, "kernel": kernel, "skip": skip, "residues": residues, "decay": decay, "freq": freq, "lengths": lengths}


HI = lax.Precision.HIGHEST

def segment_ids(lengths, index):
    starts = jnp.cumsum(lengths, dtype=jnp.int32) - lengths
    return lax.optimization_barrier(jnp.sum((starts[None, :] <= index[:, None]).astype(jnp.int32), axis=1)) - 1

def short_conv(extended, seg_ext, kernel):
    values = extended.astype(jnp.float32)
    mask_one = (seg_ext[2:] == seg_ext[1:-1]).astype(jnp.float32)[None, :, None]
    mask_two = (seg_ext[2:] == seg_ext[:-2]).astype(jnp.float32)[None, :, None]
    conv = kernel[:, 0][:, None, :] * values[:, 2:]
    conv = conv + kernel[:, 1][:, None, :] * values[:, 1:-1] * mask_one
    conv = conv + kernel[:, 2][:, None, :] * values[:, :-2] * mask_two
    return ((conv[0] * conv[2]).astype(jnp.bfloat16), conv[1])

def mode_tables(decay, freq, residues):
    steps = jnp.arange(BLK + 1, dtype=jnp.float32)[:, None, None]
    magnitude = jnp.exp(-decay[None] * steps)
    angle = freq[None] * steps
    pow_re = magnitude * jnp.cos(angle)
    pow_im = magnitude * jnp.sin(angle)
    scale = jnp.sqrt(-jnp.expm1(-2.0 * decay))
    coef_re = residues[0] * scale
    coef_im = residues[1] * scale
    filt = lax.optimization_barrier(jnp.sum(coef_re[None] * pow_re[:BLK] - coef_im[None] * pow_im[:BLK], axis=1)).astype(jnp.bfloat16)
    lag = jnp.arange(BLK, dtype=jnp.int32)[:, None] - jnp.arange(BLK, dtype=jnp.int32)[None, :]
    toeplitz = jnp.where((lag >= 0)[:, :, None], filt[jnp.clip(lag, 0, BLK - 1)], jnp.zeros((), jnp.bfloat16))
    return (pow_re, pow_im, coef_re, coef_im, toeplitz)

def local_blocks(gated, seg_with_prev, tables):
    pow_re, pow_im, coef_re, coef_im, toeplitz = tables
    count = gated.shape[0] // BLK
    blocks = gated.reshape(count, BLK, gated.shape[1])
    seg_blocks = seg_with_prev[1:].reshape(count, BLK)
    seg_before = seg_with_prev[:-1].reshape(count, BLK)[:, 0]

    def one_block(pair):
        values, segs = pair
        same = (segs[:, None] == segs[None, :]).astype(jnp.float32)
        masked = toeplitz.astype(jnp.float32) * same[:, :, None]
        return jnp.einsum('tsc,sc->tc', masked, values.astype(jnp.float32), precision=HI)
    intra = lax.map(one_block, (blocks, seg_blocks))
    last_mask = (seg_blocks == seg_blocks[:, -1:]).astype(jnp.float32)
    weighted = blocks.astype(jnp.float32) * last_mask[:, :, None]
    e_re = jnp.einsum('smc,bsc->bmc', pow_re[:BLK][::-1], weighted, precision=HI)
    e_im = jnp.einsum('smc,bsc->bmc', pow_im[:BLK][::-1], weighted, precision=HI)
    flags = (seg_blocks[:, -1] == seg_before).astype(jnp.float32)
    g_re = flags[:, None, None] * pow_re[BLK][None]
    g_im = flags[:, None, None] * pow_im[BLK][None]
    first_mask = (seg_blocks == seg_before[:, None]).astype(jnp.float32)
    return (intra, e_re, e_im, g_re, g_im, first_mask, flags)

def run_chain(start_re, start_im, g_re, g_im, e_re, e_im):

    def advance(carry, item):
        s_re, s_im = carry
        a_re, a_im, b_re, b_im = item
        n_re = a_re * s_re - a_im * s_im + b_re
        n_im = a_re * s_im + a_im * s_re + b_im
        return ((n_re, n_im), (s_re, s_im))
    final, states = lax.scan(advance, (start_re, start_im), (g_re, g_im, e_re, e_im))
    return (states[0], states[1], final[0], final[1])

def finish(intra, states_re, states_im, tables, first_mask, gated, other, skip):
    pow_re, pow_im, coef_re, coef_im, toeplitz = tables
    amp_re = coef_re[None] * states_re - coef_im[None] * states_im
    amp_im = coef_re[None] * states_im + coef_im[None] * states_re
    carried = jnp.einsum('jmc,bmc->bjc', pow_re[1:], amp_re, precision=HI)
    carried = carried - jnp.einsum('jmc,bmc->bjc', pow_im[1:], amp_im, precision=HI)
    total = intra + carried * first_mask[:, :, None]
    total = total.reshape(gated.shape)
    return (other * (total + skip[None, :] * gated.astype(jnp.float32))).astype(jnp.bfloat16)

def reference(features, kernel, skip, residues, decay, freq, lengths):
    index = jnp.arange(TOKENS + 2, dtype=jnp.int32) - 2
    seg_ext = segment_ids(lengths, index)
    pad = jnp.zeros((3, 2, C), jnp.bfloat16)
    extended = jnp.concatenate([pad, features], axis=1)
    gated, other = short_conv(extended, seg_ext, kernel)
    tables = mode_tables(decay, freq, residues)
    intra, e_re, e_im, g_re, g_im, first_mask, flags = local_blocks(gated, seg_ext[1:], tables)
    zero = jnp.zeros((M, C), jnp.float32)
    states_re, states_im, _, _ = run_chain(zero, zero, g_re, g_im, e_re, e_im)
    return finish(intra, states_re, states_im, tables, first_mask, gated, other, skip)
```

```python
import jax
import jax.numpy as jnp
from jax import lax
from jax.experimental import pallas as pl
from jax.experimental.pallas import tpu as pltpu
from jax.sharding import PartitionSpec as P

BLK = 16
LANE = 128
SUB = 8
TILE = 512
F32 = jnp.float32
BF16 = jnp.bfloat16


def exchange(block, distance):
    devices = range(lax.axis_size("seq"))
    return lax.ppermute(block, "seq", [(i, i ^ distance) for i in devices])


def row_iota(rows):
    return lax.broadcasted_iota(jnp.int32, (rows, LANE), 0)


def short_filter(rows, halo, taps, pad, mask_one, mask_two):
    tokens = rows.shape[0]
    values = rows.astype(F32)
    pad[pl.ds(SUB, tokens), :] = values
    pad[pl.ds(SUB - 2, 2), :] = halo.astype(F32)
    conv = taps[0:1, :] * values
    conv = conv + taps[1:2, :] * pad[pl.ds(SUB - 1, tokens), :] * mask_one
    return conv + taps[2:3, :] * pad[pl.ds(SUB - 2, tokens), :] * mask_two


def tap_masks(starts_ref, tokens):
    t = row_iota(tokens)
    here = jnp.zeros((tokens, LANE), jnp.bool_)
    before = jnp.zeros((tokens, LANE), jnp.bool_)
    for i in range(starts_ref.shape[0]):
        here = here | (t == starts_ref[i])
        before = before | (t - 1 == starts_ref[i])
    mask_one = jnp.where(here, 0.0, 1.0)
    return mask_one, jnp.where(here | before, 0.0, 1.0)


def block_flags(starts_ref, count):
    flags = []
    for b in range(count):
        hit = jnp.int32(0)
        for i in range(starts_ref.shape[0]):
            s = starts_ref[i]
            hit = hit | ((s >= b * BLK) & (s < (b + 1) * BLK)).astype(jnp.int32)
        flags.append((1 - hit).astype(F32))
    return flags


def cmul(a_re, a_im, b_re, b_im):
    return a_re * b_re - a_im * b_im, a_re * b_im + a_im * b_re


def column_sums(parts):
    row = lax.broadcasted_iota(jnp.int32, (SUB, LANE), 0)
    low = row < 4
    level = []
    for b in range(4):
        keep = jnp.where(low, parts[b], parts[b + 4])
        move = jnp.where(low, parts[b + 4], parts[b])
        level.append(keep + pltpu.roll(move, 4, 0))
    for step in (2, 1):
        clear = (row & step) == 0
        level = [
            jnp.where(
                clear,
                level[b] + pltpu.roll(level[b], SUB - step, 0),
                level[b + step] + pltpu.roll(level[b + step], step, 0),
            )
            for b in range(step)
        ]
    return level[0]


def front_kernel(starts_ref, f0_ref, f2_ref, halo_ref, taps_ref, pre_ref, pim_ref,
                 z_ref, e_ref, end_ref, one_s, two_s, last_s, pad_s, z_s):
    tokens, width = z_ref.shape
    count = tokens // BLK
    modes = pre_ref.shape[0]
    halves = modes // SUB

    @pl.when(pl.program_id(0) == 0)
    def _():
        mask_one, mask_two = tap_masks(starts_ref, tokens)
        one_s[...] = mask_one
        two_s[...] = mask_two
        t = row_iota(tokens)
        last = jnp.full((tokens, LANE), -1, jnp.int32)
        for i in range(starts_ref.shape[0]):
            s = starts_ref[i]
            last = jnp.maximum(last, jnp.where(s <= (t | (BLK - 1)), s, -1))
        last_s[...] = jnp.where(t >= last, 1.0, 0.0)

    flags = block_flags(starts_ref, count)

    @pl.loop(0, width // LANE)
    def _(tile):
        lanes = pl.ds(pl.multiple_of(tile * LANE, LANE), LANE)
        mask_one, mask_two = one_s[...], two_s[...]
        conv0 = short_filter(f0_ref[0, :, lanes], halo_ref[0, :, lanes], taps_ref[0, :, lanes],
                             pad_s.at[0], mask_one, mask_two)
        conv2 = short_filter(f2_ref[0, :, lanes], halo_ref[2, :, lanes], taps_ref[2, :, lanes],
                             pad_s.at[1], mask_one, mask_two)
        z = (conv0 * conv2).astype(BF16)
        z_ref[:, lanes] = z
        z_s[...] = z.astype(F32) * last_s[...]
        p_re = [pre_ref[pl.ds(h * SUB, SUB), lanes] for h in range(halves)]
        p_im = [pim_ref[pl.ds(h * SUB, SUB), lanes] for h in range(halves)]
        pow_re, pow_im = list(p_re), list(p_im)
        e_re, e_im = [], []
        for b in range(count):
            here = z_s[pl.ds(b * BLK + BLK - 1, SUB, stride=0), :]
            prev = z_s[pl.ds(b * BLK + BLK - 2, SUB, stride=0), :]
            e_re.append([here + p_re[h] * prev for h in range(halves)])
            e_im.append([p_im[h] * prev for h in range(halves)])
        for k in range(2, BLK):
            for h in range(halves):
                pow_re[h], pow_im[h] = cmul(pow_re[h], pow_im[h], p_re[h], p_im[h])
            for b in range(count):
                here = z_s[pl.ds(b * BLK + BLK - 1 - k, SUB, stride=0), :]
                for h in range(halves):
                    e_re[b][h] = e_re[b][h] + pow_re[h] * here
                    e_im[b][h] = e_im[b][h] + pow_im[h] * here
        for h in range(halves):
            g_re, g_im = cmul(pow_re[h], pow_im[h], p_re[h], p_im[h])
            end_re, end_im = e_re[0][h], e_im[0][h]
            for b in range(count):
                if b:
                    move_re, move_im = cmul(g_re, g_im, end_re, end_im)
                    end_re = flags[b] * move_re + e_re[b][h]
                    end_im = flags[b] * move_im + e_im[b][h]
                e_ref[b, pl.ds(h * SUB, SUB), lanes] = e_re[b][h]
                e_ref[b, pl.ds(modes + h * SUB, SUB), lanes] = e_im[b][h]
            end_ref[0, pl.ds(h * SUB, SUB), lanes] = end_re.astype(BF16)
            end_ref[0, pl.ds(modes + h * SUB, SUB), lanes] = end_im.astype(BF16)


def middle_kernel(starts_ref, f1_ref, halo_ref, taps_ref, z_ref, skip_ref, pre_ref, pim_ref,
                  cre_ref, cim_ref, base_ref, gain_ref,
                  one_s, two_s, first_s, part_s, pad_s, z_s, filt_s, acc_s):
    tokens, width = z_ref.shape
    count = tokens // BLK
    modes = pre_ref.shape[0]
    halves = modes // SUB
    nseq = starts_ref.shape[0]

    @pl.when(pl.program_id(0) == 0)
    def _():
        mask_one, mask_two = tap_masks(starts_ref, tokens)
        one_s[...] = mask_one
        two_s[...] = mask_two
        t = row_iota(tokens)
        t0 = t & (-BLK)
        piece = jnp.zeros((tokens, LANE), jnp.int32)
        opened = jnp.zeros((tokens, LANE), jnp.bool_)
        for i in range(nseq):
            s = starts_ref[i]
            piece = piece + jnp.where((s > t0) & (s <= t), 1, 0)
            opened = opened | ((s >= t0) & (s <= t))
        part_s[...] = piece.astype(F32)
        first_s[...] = jnp.where(opened, 0.0, 1.0)

    pieces = jnp.int32(1)
    for b in range(count):
        inside = jnp.int32(1)
        for i in range(nseq):
            s = starts_ref[i]
            inside = inside + ((s > b * BLK) & (s < (b + 1) * BLK)).astype(jnp.int32)
        pieces = jnp.maximum(pieces, inside)

    @pl.loop(0, width // LANE)
    def _(tile):
        lanes = pl.ds(pl.multiple_of(tile * LANE, LANE), LANE)
        q_re = [cre_ref[pl.ds(h * SUB, SUB), lanes] for h in range(halves)]
        q_im = [cim_ref[pl.ds(h * SUB, SUB), lanes] for h in range(halves)]
        p_re = [pre_ref[pl.ds(h * SUB, SUB), lanes] for h in range(halves)]
        p_im = [pim_ref[pl.ds(h * SUB, SUB), lanes] for h in range(halves)]
        filt_s[pl.ds(0, BLK), :] = jnp.zeros((BLK, LANE), F32)
        for group in range(BLK // SUB):
            parts = []
            for k in range(SUB):
                parts.append(sum(q_re[1:], q_re[0]))
                for h in range(halves):
                    q_re[h], q_im[h] = cmul(q_re[h], q_im[h], p_re[h], p_im[h])
            filt_s[pl.ds(BLK + group * SUB, SUB), :] = column_sums(parts).astype(BF16).astype(F32)
        z = z_ref[:, lanes].astype(F32)
        acc_s[...] = skip_ref[:, lanes] * z

        def one_piece(q, carry):
            mask = jnp.where(part_s[...] == q.astype(F32), 1.0, 0.0)
            z_s[...] = z_ref[:, lanes].astype(F32) * mask
            sums = [[None] * 2 for _ in range(count)]
            for s in range(BLK):
                for r in range(BLK // SUB):
                    if s >= (r + 1) * SUB:
                        continue
                    column = filt_s[pl.ds(BLK - s + r * SUB, SUB), :]
                    for b in range(count):
                        term = column * z_s[pl.ds(b * BLK + s, SUB, stride=0), :]
                        sums[b][r] = term if s == 0 else sums[b][r] + term
            for b in range(count):
                for r in range(BLK // SUB):
                    rows = pl.ds(b * BLK + r * SUB, SUB)
                    here = jnp.where(part_s[rows, :] == q.astype(F32), sums[b][r], 0.0)
                    acc_s[rows, :] = acc_s[rows, :] + here
            return carry

        lax.fori_loop(0, pieces, one_piece, 0)
        conv1 = short_filter(f1_ref[0, :, lanes], halo_ref[1, :, lanes], taps_ref[1, :, lanes],
                             pad_s, one_s[...], two_s[...])
        base_ref[:, lanes] = conv1 * acc_s[...]
        gain_ref[:, lanes] = conv1 * first_s[...]


def back_kernel(starts_ref, core_ref, own_ref, other_ref, e_ref, pre_ref, pim_ref, cre_ref, cim_ref,
                base_ref, gain_ref, out_ref, y_s):
    tokens, width = out_ref.shape
    count = tokens // BLK
    modes = pre_ref.shape[0]
    halves = modes // SUB
    flags = block_flags(starts_ref, count)
    mine = (pl.program_id(0) * 2 >= pl.num_programs(0)).astype(jnp.int32) == core_ref[0]

    @pl.loop(0, width // LANE)
    def _(tile):
        lanes = pl.ds(pl.multiple_of(tile * LANE, LANE), LANE)

        def rows(ref, h):
            return ref[pl.ds(h * SUB, SUB), lanes]

        entry = [
            jnp.where(mine, rows(own_ref, h).astype(F32), rows(other_ref, h).astype(F32))
            for h in range(2 * halves)
        ]
        p_re = [rows(pre_ref, h) for h in range(halves)]
        p_im = [rows(pim_ref, h) for h in range(halves)]
        q_re = [rows(cre_ref, h) for h in range(halves)]
        q_im = [rows(cim_ref, h) for h in range(halves)]
        s_re, s_im = [entry[:halves]], [entry[halves:]]
        gate = [(p_re[h], p_im[h]) for h in range(halves)]
        for _ in range(4):
            gate = [cmul(*g, *g) for g in gate]
        for b in range(count - 1):
            new_re, new_im = [], []
            for h in range(halves):
                move_re, move_im = cmul(*gate[h], s_re[b][h], s_im[b][h])
                new_re.append(flags[b] * move_re + e_ref[b, pl.ds(h * SUB, SUB), lanes])
                new_im.append(flags[b] * move_im + e_ref[b, pl.ds(modes + h * SUB, SUB), lanes])
            s_re.append(new_re)
            s_im.append(new_im)
        for k in range(BLK):
            for h in range(halves):
                q_re[h], q_im[h] = cmul(q_re[h], q_im[h], p_re[h], p_im[h])
            parts = []
            for b in range(count):
                part = q_re[0] * s_re[b][0] - q_im[0] * s_im[b][0]
                for h in range(1, halves):
                    part = part + q_re[h] * s_re[b][h] - q_im[h] * s_im[b][h]
                parts.append(part)
            y_s[pl.ds(k, SUB, stride=BLK), :] = column_sums(parts)
        out_ref[:, lanes] = (base_ref[:, lanes] + gain_ref[:, lanes] * y_s[...]).astype(BF16)


def per_device(features, kernel, skip, residues, decay, freq, lengths):
    tokens = features.shape[1]
    modes, width = decay.shape
    half = width // 2
    count = tokens // BLK
    n = lax.axis_size("seq")
    place = lax.axis_index("seq")
    core = place % 2
    tiles = width // TILE

    rim = features[:, tokens - 2 :, :]
    inner = exchange(rim, 1)
    link = [(i, i + 1) for i in range(1, n - 1, 2)]
    outer = lax.ppermute(rim, "seq", link + [(b, a) for a, b in link])
    halo = jnp.where(core == 1, inner, outer)

    order = jnp.arange(lengths.shape[0])
    starts = jnp.sum(jnp.where(order[None, :] < order[:, None], lengths[None, :], 0), axis=1)
    base = place * tokens
    local_starts = (starts - base).astype(jnp.int32)

    def same(first, last):
        hit = (starts >= first * tokens) & (starts < (last + 1) * tokens)
        return jnp.where(jnp.any(hit), 0.0, 1.0).astype(F32)

    magnitude = jnp.exp(-decay)
    p_re = magnitude * jnp.cos(freq)
    p_im = magnitude * jnp.sin(freq)
    scale = jnp.sqrt(-jnp.expm1(-2.0 * decay))
    c_re = residues[0] * scale
    c_im = residues[1] * scale

    def smem(shape):
        return pl.BlockSpec(shape, lambda *_: (0,) * len(shape), memory_space=pltpu.SMEM)

    def stream(r):
        return pl.BlockSpec((1, tokens, TILE), lambda i, *_: (r, 0, i))

    def columns(*lead):
        return pl.BlockSpec((*lead, TILE), lambda i, *_: (0,) * len(lead) + (i,))

    params = pltpu.CompilerParams(
        dimension_semantics=("arbitrary",), vmem_limit_bytes=32 * 1024 * 1024
    )
    table = columns(modes)
    plane = pltpu.VMEM((tokens, LANE), F32)
    pad = pltpu.VMEM((tokens + SUB, LANE), F32)
    z, e, end = pl.pallas_call(
        front_kernel,
        grid_spec=pltpu.PrefetchScalarGridSpec(
            num_scalar_prefetch=1,
            grid=(tiles,),
            in_specs=[stream(0), stream(2), columns(3, 2), columns(3, 3), table, table],
            out_specs=[
                columns(tokens),
                columns(count, 2 * modes),
                pl.BlockSpec((1, 2 * modes, TILE), lambda i, *_: (i * 2 // tiles, 0, i % (tiles // 2))),
            ],
            scratch_shapes=[plane, plane, plane, pltpu.VMEM((2, tokens + SUB, LANE), F32), plane],
        ),
        out_shape=[
            jax.ShapeDtypeStruct((tokens, width), BF16),
            jax.ShapeDtypeStruct((count, 2 * modes, width), F32),
            jax.ShapeDtypeStruct((2, 2 * modes, half), BF16),
        ],
        compiler_params=params,
        name="front",
    )(local_starts, features, features, halo, kernel, p_re, p_im)

    base_out, gain = pl.pallas_call(
        middle_kernel,
        grid_spec=pltpu.PrefetchScalarGridSpec(
            num_scalar_prefetch=1,
            grid=(tiles,),
            in_specs=[stream(1), columns(3, 2), columns(3, 3), columns(tokens), columns(1),
                      table, table, table, table],
            out_specs=[columns(tokens), columns(tokens)],
            scratch_shapes=[plane, plane, plane, plane, pad, plane,
                            pltpu.VMEM((2 * BLK, LANE), F32), plane],
        ),
        out_shape=[jax.ShapeDtypeStruct((tokens, width), F32)] * 2,
        compiler_params=params,
        cost_estimate=pl.CostEstimate(flops=10 * 1000 * 1000, bytes_accessed=8 << 20, transcendentals=0),
        name="middle",
    )(local_starts, features, halo, kernel, z, skip[None], p_re, p_im, c_re, c_im)

    span = lax.dynamic_slice_in_dim(decay, core * half, half, 1) * float(tokens)
    turn = lax.dynamic_slice_in_dim(freq, core * half, half, 1) * float(tokens)
    fade = jnp.exp(-span)
    one = (fade * jnp.cos(turn), fade * jnp.sin(turn))

    def split(packed):
        return packed[:modes].astype(F32), packed[modes:].astype(F32)

    def pack(pair):
        return jnp.concatenate([pair[0].astype(BF16), pair[1].astype(BF16)], axis=0)

    def advance(gate, flag, state, addend):
        re, im = cmul(*gate, *state)
        return addend[0] + flag * re, addend[1] + flag * im

    def choose(flag, a, b):
        return tuple(jnp.where(flag, x, y) for x, y in zip(a, b))

    kept = split(lax.dynamic_index_in_dim(end, core, 0, False))
    came = split(exchange(lax.dynamic_index_in_dim(end, 1 - core, 0, False), 1))
    odd = core == 1
    even_end, odd_end = choose(odd, came, kept), choose(odd, kept, came)
    even = place - core
    total = advance(one, same(even + 1, even + 1), even_end, odd_end)
    zero = jnp.zeros((modes, half), F32)
    prefix = (zero, zero)
    before = (zero + 1.0, zero)
    power = cmul(*one, *one)
    distance = 2
    while distance < n:
        upper = (place & distance) != 0
        group = place - place % distance
        met = split(exchange(pack(total), distance))
        added = advance(before, same(group, even - 1), met, prefix)
        prefix = choose(upper, added, prefix)
        early, late = choose(upper, met, total), choose(upper, total, met)
        later = group | distance
        total = advance(power, same(later, later + distance - 1), early, late)
        before = choose(upper, cmul(*before, *power), before)
        power = cmul(*power, *power)
        distance *= 2
    beyond = advance(one, same(even, even), prefix, even_end)
    own = pack(choose(odd, beyond, prefix))
    other = exchange(pack(choose(odd, prefix, beyond)), 1)

    entry = pl.BlockSpec((2 * modes, TILE), lambda i, *_: (0, i % (tiles // 2)))
    return pl.pallas_call(
        back_kernel,
        grid_spec=pltpu.PrefetchScalarGridSpec(
            num_scalar_prefetch=2,
            grid=(tiles,),
            in_specs=[entry, entry, columns(count, 2 * modes), table, table, table, table,
                      columns(tokens), columns(tokens)],
            out_specs=columns(tokens),
            scratch_shapes=[plane],
        ),
        out_shape=jax.ShapeDtypeStruct((tokens, width), BF16),
        compiler_params=params,
        name="back",
    )(local_starts, core[None].astype(jnp.int32), own, other, e, p_re, p_im, c_re, c_im, base_out, gain)


def solution(mesh):
    return jax.shard_map(
        per_device,
        mesh=mesh,
        in_specs=(P(None, ("groups", "seq"), None), P(), P(), P(), P(), P(), P("groups")),
        out_specs=P(("groups", "seq"), None),
        check_vma=False,
    )
```

```python
import functools

import jax
import jax.numpy as jnp
from jax import lax
from jax.experimental import pallas as pl
from jax.experimental.pallas import tpu as pltpu
from jax.sharding import PartitionSpec as P

BLK = 16
LANE = 128
SUB = 8
TILE = 512
F32 = jnp.float32
BF16 = jnp.bfloat16


def exchange(block, distance):
    devices = range(lax.axis_size("seq"))
    return lax.ppermute(block, "seq", [(i, i ^ distance) for i in devices])


def row_iota(rows):
    return lax.broadcasted_iota(jnp.int32, (rows, LANE), 0)


def starts_of(lengths_ref, origin):
    starts, at = [], -origin
    for i in range(lengths_ref.shape[0]):
        starts.append(at)
        at = at + lengths_ref[i]
    return starts


def none_in(starts, first, beyond):
    hit = jnp.int32(0)
    for s in starts:
        hit = hit | ((s >= first) & (s < beyond)).astype(jnp.int32)
    return (1 - hit).astype(F32)


def block_flags(starts, count):
    return [none_in(starts, b * BLK, (b + 1) * BLK) for b in range(count)]


def tap_masks(starts, tokens):
    t = row_iota(tokens)
    here = jnp.zeros((tokens, LANE), jnp.bool_)
    before = jnp.zeros((tokens, LANE), jnp.bool_)
    for s in starts:
        here = here | (t == s)
        before = before | (t - 1 == s)
    mask_one = jnp.where(here, 0.0, 1.0)
    return mask_one, jnp.where(here | before, 0.0, 1.0)


def short_filter(rows, halo, taps, mask_one, mask_two):
    values = rows.astype(F32)
    edge = halo.astype(F32)
    first, second = edge[0:1, :], edge[1:2, :]
    row = row_iota(values.shape[0])
    behind = jnp.where(row == 0, second, pltpu.roll(values, 1, 0))
    further = jnp.where(row == 0, first, jnp.where(row == 1, second, pltpu.roll(values, 2, 0)))
    conv = taps[0:1, :] * values
    conv = conv + taps[1:2, :] * behind * mask_one
    return conv + taps[2:3, :] * further * mask_two


def lane_tile(tile):
    return pl.ds(pl.multiple_of(tile * LANE, LANE), LANE)


def cmul(a_re, a_im, b_re, b_im):
    return a_re * b_re - a_im * b_im, a_re * b_im + a_im * b_re


def column_sums(parts):
    row = lax.broadcasted_iota(jnp.int32, (SUB, LANE), 0)
    low = row < 4
    level = []
    for b in range(4):
        keep = jnp.where(low, parts[b], parts[b + 4])
        move = jnp.where(low, parts[b + 4], parts[b])
        level.append(keep + pltpu.roll(move, 4, 0))
    for step in (2, 1):
        clear = (row & step) == 0
        level = [
            jnp.where(
                clear,
                level[b] + pltpu.roll(level[b], SUB - step, 0),
                level[b + step] + pltpu.roll(level[b + step], step, 0),
            )
            for b in range(step)
        ]
    return level[0]


def rows_of(ref, h, lanes):
    return ref[pl.ds(h * SUB, SUB), lanes]


def tables_kernel(place_ref, decay_ref, freq_ref, residues_ref, pole_ref, coef_ref, gate_ref, before_ref,
                  *, tokens):
    modes, width = decay_ref.shape
    half = width // 2
    place = place_ref[0]
    rounds = gate_ref.shape[0]

    @pl.loop(0, width // LANE)
    def _(tile):
        lanes = lane_tile(tile)
        decay, x = decay_ref[:, lanes], freq_ref[:, lanes]
        fade = jnp.exp(-decay)
        s = x * x
        sine = x * (1 + s * (-1 / 6 + s * (1 / 120 + s * (-1 / 5040 + s * (1 / 362880)))))
        cosine = 1 + s * (-1 / 2 + s * (1 / 24 + s * (-1 / 720 + s * (1 / 40320 - s * (1 / 3628800)))))
        pole_ref[0:modes, lanes] = fade * cosine
        pole_ref[modes : 2 * modes, lanes] = fade * sine
        d = 2 * decay
        scale = jnp.sqrt(d * (1 - d * (1 / 2 - d * (1 / 6 - d * (1 / 24 - d * (1 / 120 - d * (1 / 720)))))))
        coef_ref[0:modes, lanes] = residues_ref[0, :, lanes] * scale
        coef_ref[modes : 2 * modes, lanes] = residues_ref[1, :, lanes] * scale

    @pl.loop(0, half // LANE)
    def _(tile):
        lanes = lane_tile(tile)
        from_lane = pl.ds(pl.multiple_of((place & 1) * half + tile * LANE, LANE), LANE)
        gate = pole_ref[0:modes, from_lane], pole_ref[modes : 2 * modes, from_lane]
        reach = 1
        while reach < tokens:
            gate = cmul(*gate, *gate)
            reach *= 2
        before = jnp.ones_like(gate[0]), jnp.zeros_like(gate[0])
        for k in range(rounds):
            gate_ref[k, 0:modes, lanes], gate_ref[k, modes : 2 * modes, lanes] = gate
            before_ref[k, 0:modes, lanes], before_ref[k, modes : 2 * modes, lanes] = before
            if k:
                upper = (place & (1 << k)) != 0
                moved = cmul(*before, *gate)
                before = tuple(jnp.where(upper, a, b) for a, b in zip(moved, before))
            gate = cmul(*gate, *gate)


def front_kernel(lengths_ref, place_ref, f0_ref, f2_ref, halo_ref, taps_ref, pole_ref,
                 z_ref, e_ref, end_ref, one_s, two_s, last_s, z_s):
    tokens, width = z_ref.shape
    count = tokens // BLK
    modes = pole_ref.shape[0] // 2
    halves = modes // SUB
    starts = starts_of(lengths_ref, place_ref[0] * tokens)

    @pl.when(pl.program_id(0) == 0)
    def _():
        mask_one, mask_two = tap_masks(starts, tokens)
        one_s[...] = mask_one
        two_s[...] = mask_two
        t = row_iota(tokens)
        last = jnp.full((tokens, LANE), -1, jnp.int32)
        for s in starts:
            last = jnp.maximum(last, jnp.where(s <= (t | (BLK - 1)), s, -1))
        last_s[...] = jnp.where(t >= last, 1.0, 0.0)

    flags = block_flags(starts, count)

    @pl.loop(0, width // LANE)
    def _(tile):
        lanes = lane_tile(tile)
        mask_one, mask_two = one_s[...], two_s[...]
        conv0 = short_filter(f0_ref[0, :, lanes], halo_ref[0, :, lanes], taps_ref[0, :, lanes], mask_one, mask_two)
        conv2 = short_filter(f2_ref[0, :, lanes], halo_ref[2, :, lanes], taps_ref[2, :, lanes], mask_one, mask_two)
        z = (conv0 * conv2).astype(BF16)
        z_ref[:, lanes] = z
        z_s[...] = z.astype(F32) * last_s[...]
        p_re = [rows_of(pole_ref, h, lanes) for h in range(halves)]
        p_im = [rows_of(pole_ref, halves + h, lanes) for h in range(halves)]
        pow_re, pow_im = list(p_re), list(p_im)
        e_re, e_im = [], []
        for b in range(count):
            here = z_s[pl.ds(b * BLK + BLK - 1, SUB, stride=0), :]
            prev = z_s[pl.ds(b * BLK + BLK - 2, SUB, stride=0), :]
            e_re.append([here + p_re[h] * prev for h in range(halves)])
            e_im.append([p_im[h] * prev for h in range(halves)])
        for k in range(2, BLK):
            for h in range(halves):
                pow_re[h], pow_im[h] = cmul(pow_re[h], pow_im[h], p_re[h], p_im[h])
            for b in range(count):
                here = z_s[pl.ds(b * BLK + BLK - 1 - k, SUB, stride=0), :]
                for h in range(halves):
                    e_re[b][h] = e_re[b][h] + pow_re[h] * here
                    e_im[b][h] = e_im[b][h] + pow_im[h] * here
        for h in range(halves):
            g_re, g_im = cmul(pow_re[h], pow_im[h], p_re[h], p_im[h])
            end_re, end_im = e_re[0][h], e_im[0][h]
            for b in range(count):
                if b:
                    move_re, move_im = cmul(g_re, g_im, end_re, end_im)
                    end_re = flags[b] * move_re + e_re[b][h]
                    end_im = flags[b] * move_im + e_im[b][h]
                e_ref[b, pl.ds(h * SUB, SUB), lanes] = e_re[b][h]
                e_ref[b, pl.ds(modes + h * SUB, SUB), lanes] = e_im[b][h]
            end_ref[pl.ds(h * SUB, SUB), lanes] = end_re.astype(BF16)
            end_ref[pl.ds(modes + h * SUB, SUB), lanes] = end_im.astype(BF16)


def middle_kernel(lengths_ref, place_ref, f1_ref, halo_ref, taps_ref, z_ref, skip_ref, pole_ref, coef_ref,
                  base_ref, gain_ref, one_s, two_s, first_s, part_s, z_s, filt_s, acc_s):
    tokens, width = z_ref.shape
    count = tokens // BLK
    modes = pole_ref.shape[0] // 2
    halves = modes // SUB
    starts = starts_of(lengths_ref, place_ref[0] * tokens)

    @pl.when(pl.program_id(0) == 0)
    def _():
        mask_one, mask_two = tap_masks(starts, tokens)
        one_s[...] = mask_one
        two_s[...] = mask_two
        t = row_iota(tokens)
        t0 = t & (-BLK)
        piece = jnp.zeros((tokens, LANE), jnp.int32)
        opened = jnp.zeros((tokens, LANE), jnp.bool_)
        for s in starts:
            piece = piece + jnp.where((s > t0) & (s <= t), 1, 0)
            opened = opened | ((s >= t0) & (s <= t))
        part_s[...] = piece.astype(F32)
        first_s[...] = jnp.where(opened, 0.0, 1.0)

    pieces = jnp.int32(1)
    for b in range(count):
        inside = jnp.int32(1)
        for s in starts:
            inside = inside + ((s > b * BLK) & (s < (b + 1) * BLK)).astype(jnp.int32)
        pieces = jnp.maximum(pieces, inside)

    @pl.loop(0, width // LANE)
    def _(tile):
        lanes = lane_tile(tile)
        p_re = [rows_of(pole_ref, h, lanes) for h in range(halves)]
        p_im = [rows_of(pole_ref, halves + h, lanes) for h in range(halves)]
        q_re = [rows_of(coef_ref, h, lanes) for h in range(halves)]
        q_im = [rows_of(coef_ref, halves + h, lanes) for h in range(halves)]
        filt_s[pl.ds(0, BLK), :] = jnp.zeros((BLK, LANE), F32)
        for group in range(BLK // SUB):
            parts = []
            for k in range(SUB):
                parts.append(sum(q_re[1:], q_re[0]))
                for h in range(halves):
                    q_re[h], q_im[h] = cmul(q_re[h], q_im[h], p_re[h], p_im[h])
            filt_s[pl.ds(BLK + group * SUB, SUB), :] = column_sums(parts).astype(BF16).astype(F32)
        acc_s[...] = skip_ref[:, lanes] * z_ref[:, lanes].astype(F32)

        def one_piece(q, carry):
            mask = jnp.where(part_s[...] == q.astype(F32), 1.0, 0.0)
            z_s[...] = z_ref[:, lanes].astype(F32) * mask
            sums = [[None] * 2 for _ in range(count)]
            for s in range(BLK):
                for r in range(BLK // SUB):
                    if s >= (r + 1) * SUB:
                        continue
                    column = filt_s[pl.ds(BLK - s + r * SUB, SUB), :]
                    for b in range(count):
                        term = column * z_s[pl.ds(b * BLK + s, SUB, stride=0), :]
                        sums[b][r] = term if s == 0 else sums[b][r] + term
            for b in range(count):
                for r in range(BLK // SUB):
                    rows = pl.ds(b * BLK + r * SUB, SUB)
                    here = jnp.where(part_s[rows, :] == q.astype(F32), sums[b][r], 0.0)
                    acc_s[rows, :] = acc_s[rows, :] + here
            return carry

        lax.fori_loop(0, pieces, one_piece, 0)
        conv1 = short_filter(f1_ref[0, :, lanes], halo_ref[1, :, lanes], taps_ref[1, :, lanes], one_s[...], two_s[...])
        base_ref[:, lanes] = conv1 * acc_s[...]
        gain_ref[:, lanes] = conv1 * first_s[...]


def split(ref, lanes, *lead):
    modes = ref.shape[-2] // 2
    packed = ref[(*lead, slice(None), lanes)].astype(F32)
    return packed[:modes], packed[modes:]


def store(ref, lanes, pair):
    modes = ref.shape[-2] // 2
    ref[0:modes, lanes] = pair[0].astype(ref.dtype)
    ref[modes : 2 * modes, lanes] = pair[1].astype(ref.dtype)


def advance(gate, flag, state, addend):
    re, im = cmul(*gate, *state)
    return addend[0] + flag * re, addend[1] + flag * im


def choose(flag, a, b):
    return tuple(jnp.where(flag, x, y) for x, y in zip(a, b))


def first_kernel(lengths_ref, place_ref, kept_ref, came_ref, gate_ref, total_ref, send_ref, *, tokens):
    starts = starts_of(lengths_ref, 0)
    place = place_ref[0]
    odd = (place & 1) == 1
    second = place | 1
    flag = none_in(starts, second * tokens, (second + 1) * tokens)

    @pl.loop(0, kept_ref.shape[1] // LANE)
    def _(tile):
        lanes = lane_tile(tile)
        kept, came = split(kept_ref, lanes), split(came_ref, lanes)
        total = advance(split(gate_ref, lanes, 0), flag, choose(odd, came, kept), choose(odd, kept, came))
        store(total_ref, lanes, total)
        store(send_ref, lanes, total)


def round_kernel(lengths_ref, place_ref, total_ref, met_ref, prefix_ref, gate_ref, before_ref, *refs,
                 tokens, k, last):
    starts = starts_of(lengths_ref, 0)
    place = place_ref[0]
    distance = 1 << k
    upper = (place & distance) != 0
    group = (place >> k) << k
    even = (place >> 1) << 1
    later = group | distance
    enter = none_in(starts, group * tokens, even * tokens)
    enter = jnp.where(upper, enter, 0.0)
    whole = none_in(starts, later * tokens, (later + distance) * tokens)

    @pl.loop(0, met_ref.shape[1] // LANE)
    def _(tile):
        lanes = lane_tile(tile)
        met, total = split(met_ref, lanes), split(total_ref, lanes)
        prefix = split(prefix_ref, lanes) if k > 1 else (jnp.zeros_like(met[0]),) * 2
        prefix = advance(split(before_ref, lanes, k), enter, met, prefix)
        if not last:
            total_out, send_ref, prefix_out = refs
            total = advance(split(gate_ref, lanes, k), whole, choose(upper, met, total), choose(upper, total, met))
            store(total_out, lanes, total)
            store(send_ref, lanes, total)
            store(prefix_out, lanes, prefix)
        else:
            kept_ref, came_ref, own_ref, send_ref = refs
            odd = (place & 1) == 1
            kept, came = split(kept_ref, lanes), split(came_ref, lanes)
            flag = none_in(starts, even * tokens, (even + 1) * tokens)
            beyond = advance(split(gate_ref, lanes, 0), flag, prefix, choose(odd, came, kept))
            store(own_ref, lanes, choose(odd, beyond, prefix))
            store(send_ref, lanes, choose(odd, prefix, beyond))


def back_kernel(lengths_ref, place_ref, entry_ref, e_ref, pole_ref, coef_ref, base_ref, gain_ref, *refs):
    out_ref, y_s = refs[-2:]
    tokens, width = out_ref.shape
    count = tokens // BLK
    modes = pole_ref.shape[0] // 2
    halves = modes // SUB
    flags = block_flags(starts_of(lengths_ref, place_ref[0] * tokens), count)

    @pl.loop(0, width // LANE)
    def _(tile):
        lanes = lane_tile(tile)
        entry = [rows_of(entry_ref, h, lanes) for h in range(2 * halves)] if entry_ref.dtype == F32 else None
        if entry is None:
            packed = entry_ref[:, lanes].astype(F32)
            entry = [packed[h * SUB : (h + 1) * SUB] for h in range(2 * halves)]
        p_re = [rows_of(pole_ref, h, lanes) for h in range(halves)]
        p_im = [rows_of(pole_ref, halves + h, lanes) for h in range(halves)]
        q_re = [rows_of(coef_ref, h, lanes) for h in range(halves)]
        q_im = [rows_of(coef_ref, halves + h, lanes) for h in range(halves)]
        s_re, s_im = [entry[:halves]], [entry[halves:]]
        gate = [(p_re[h], p_im[h]) for h in range(halves)]
        for _ in range(BLK.bit_length() - 1):
            gate = [cmul(*g, *g) for g in gate]
        for b in range(count - 1):
            new_re, new_im = [], []
            for h in range(halves):
                move_re, move_im = cmul(*gate[h], s_re[b][h], s_im[b][h])
                new_re.append(flags[b] * move_re + e_ref[b, pl.ds(h * SUB, SUB), lanes])
                new_im.append(flags[b] * move_im + e_ref[b, pl.ds(modes + h * SUB, SUB), lanes])
            s_re.append(new_re)
            s_im.append(new_im)
        for k in range(BLK):
            for h in range(halves):
                q_re[h], q_im[h] = cmul(q_re[h], q_im[h], p_re[h], p_im[h])
            parts = []
            for b in range(count):
                part = q_re[0] * s_re[b][0] - q_im[0] * s_im[b][0]
                for h in range(1, halves):
                    part = part + q_re[h] * s_re[b][h] - q_im[h] * s_im[b][h]
                parts.append(part)
            y_s[pl.ds(k, SUB, stride=BLK), :] = column_sums(parts)
        out_ref[:, lanes] = (base_ref[:, lanes] + gain_ref[:, lanes] * y_s[...]).astype(BF16)


def per_device(features, kernel, skip, residues, decay, freq, lengths):
    tokens = features.shape[1]
    modes, width = decay.shape
    half = width // 2
    count = tokens // BLK
    n = lax.axis_size("seq")
    place = lax.axis_index("seq")
    core = place % 2
    tiles = half // TILE
    rounds = n.bit_length() - 1
    where = place.astype(jnp.int32)[None]

    rim = features[:, tokens - 2 :, :]
    inner = exchange(rim, 1)
    link = [(i, i + 1) for i in range(1, n - 1, 2)]
    outer = lax.ppermute(rim, "seq", link + [(b, a) for a, b in link])
    halo = jnp.where(core == 1, inner, outer)

    params = pltpu.CompilerParams(vmem_limit_bytes=12 * 1024 * 1024)
    plane = pltpu.VMEM((tokens, LANE), F32)
    whole = pl.BlockSpec(memory_space=pltpu.VMEM)

    def simple(body, prefetch, args, outs, name, aliases={}):
        return pl.pallas_call(
            body,
            grid_spec=pltpu.PrefetchScalarGridSpec(
                num_scalar_prefetch=len(prefetch), grid=(),
                in_specs=[whole] * len(args), out_specs=[whole] * len(outs),
            ),
            out_shape=[jax.ShapeDtypeStruct(*o) for o in outs],
            compiler_params=params, name=name,
        )(*prefetch, *args)

    packed = 2 * modes
    state, sent = ((packed, half), F32), ((packed, half), BF16)
    pole, coef, gates, befores = simple(
        functools.partial(tables_kernel, tokens=tokens), (where,), (decay, freq, residues),
        (((packed, width), F32), ((packed, width), F32), ((rounds, packed, half), F32), ((rounds, packed, half), F32)),
        "tables",
    )

    def half_of(mine, place_ref):
        core = place_ref[0] & 1
        return core if mine else 1 - core

    def call(body, mine, name, args, specs, outs, scratch, cost, aliases={}):
        return pl.pallas_call(
            body,
            grid_spec=pltpu.PrefetchScalarGridSpec(
                num_scalar_prefetch=2, grid=(tiles,), in_specs=specs,
                out_specs=[o[2] for o in outs], scratch_shapes=scratch,
            ),
            out_shape=[jax.ShapeDtypeStruct(o[0], o[1]) for o in outs],
            input_output_aliases=aliases,
            compiler_params=params, name=name,
            cost_estimate=pl.CostEstimate(flops=cost, bytes_accessed=1 << 20, transcendentals=0),
        )(lengths, where, *args)

    def columns(mine, *lead):
        zeros = (0,) * len(lead)
        return pl.BlockSpec((*lead, TILE), lambda i, n_ref, w_ref: (*zeros, half_of(mine, w_ref) * tiles + i))

    def stream(mine, r):
        return pl.BlockSpec((1, tokens, TILE), lambda i, n_ref, w_ref: (r, 0, half_of(mine, w_ref) * tiles + i))

    def local(*lead):
        zeros = (0,) * len(lead)
        return pl.BlockSpec((*lead, TILE), lambda i, *_: (*zeros, i))

    def front(mine):
        return call(
            front_kernel, mine, "front", (features, features, halo, kernel, pole),
            [stream(mine, 0), stream(mine, 2), columns(mine, 3, 2), columns(mine, 3, 3), columns(mine, packed)],
            [((tokens, half), BF16, local(tokens)), ((count, packed, half), F32, local(count, packed)),
             ((packed, half), BF16, local(packed))],
            [plane] * 4, 5_000_000,
        )

    def middle(mine, z):
        return call(
            middle_kernel, mine, "middle", (features, halo, kernel, z, skip[None], pole, coef),
            [stream(mine, 1), columns(mine, 3, 2), columns(mine, 3, 3), local(tokens), columns(mine, 1),
             columns(mine, packed), columns(mine, packed)],
            [((tokens, half), F32, local(tokens))] * 2,
            [plane] * 5 + [pltpu.VMEM((2 * BLK, LANE), F32), plane], 5_000_000,
        )

    def back(mine, entry, e, base, gain, out):
        args = (entry, e, pole, coef, base, gain)
        specs = [local(packed), local(count, packed), columns(mine, packed), columns(mine, packed),
                 local(tokens), local(tokens)]
        if out is not None:
            args, specs = args + (out,), specs + [pl.BlockSpec(memory_space=pl.ANY)]
        return call(
            back_kernel, mine, "back", args, specs, [((tokens, width), BF16, columns(mine, tokens))],
            [plane], 5_000_000, {} if out is None else {len(args) + 1: 0},
        )[0]

    z_other, e_other, end_other = front(False)
    came_start = exchange(end_other, 1)
    z_own, e_own, end_own = front(True)
    came = came_start
    total, send = simple(
        functools.partial(first_kernel, tokens=tokens), (lengths, where), (end_own, came, gates), (state, sent), "first"
    )
    prefix = total
    fillers = {1: lambda: middle(True, z_own), 2: lambda: middle(False, z_other)}
    filled = {}
    for k in range(1, rounds):
        met = exchange(send, 1 << k)
        if k in fillers:
            filled[k] = fillers[k]()
            met, filled[k] = lax.optimization_barrier((met, filled[k]))
        last = k == rounds - 1
        body = functools.partial(round_kernel, tokens=tokens, k=k, last=last)
        args = (total, met, prefix, gates, befores)
        if last:
            own, send = simple(body, (lengths, where), args + (end_own, came), (state, sent), "round")
        else:
            total, send, prefix = simple(body, (lengths, where), args, (state, sent, state), "round")
    other = exchange(send, 1)
    out = back(True, own, e_own, *filled[1], None)
    return back(False, other, e_other, *filled[2], out)


def solution(mesh):
    return jax.shard_map(
        per_device,
        mesh=mesh,
        in_specs=(P(None, ("groups", "seq"), None), P(), P(), P(), P(), P(), P("groups")),
        out_specs=P(("groups", "seq"), None),
        check_vma=False,
    )
```

```python
import functools

import jax
import jax.numpy as jnp
from jax import lax
from jax.experimental import pallas as pl
from jax.experimental.pallas import tpu as pltpu
from jax.sharding import PartitionSpec as P

BLK = 16
LANE = 128
SUB = 8
TILE = 512
PITCH = 40
ROOM = 49
F32 = jnp.float32
BF16 = jnp.bfloat16


def exchange(block, distance):
    devices = range(lax.axis_size("seq"))
    return lax.ppermute(block, "seq", [(i, i ^ distance) for i in devices])


def row_iota(rows):
    return lax.broadcasted_iota(jnp.int32, (rows, LANE), 0)


def starts_of(lengths_ref, origin):
    starts, at = [], -origin
    for i in range(lengths_ref.shape[0]):
        starts.append(at)
        at = at + lengths_ref[i]
    return starts


def none_in(starts, first, beyond):
    hit = jnp.int32(0)
    for s in starts:
        hit = hit | ((s >= first) & (s < beyond)).astype(jnp.int32)
    return (1 - hit).astype(F32)


def block_flags(starts, count):
    return [none_in(starts, b * BLK, (b + 1) * BLK) for b in range(count)]


def shift_matrix(starts, tokens):
    t = lax.broadcasted_iota(jnp.int32, (tokens, tokens), 0)
    u = lax.broadcasted_iota(jnp.int32, (tokens, tokens), 1)
    here = jnp.zeros((tokens, tokens), jnp.bool_)
    before = jnp.zeros((tokens, tokens), jnp.bool_)
    for s in starts:
        here = here | (t == s)
        before = before | (t - 1 == s)
    one = jnp.where((u == t - 1) & ~here, 1.0, 0.0)
    two = jnp.where((u == t - 2) & ~(here | before), 1.0, 0.0)
    return jnp.concatenate([one, two], axis=0).astype(BF16)


def edge_flags(starts):
    return none_in(starts, 0, 1), none_in(starts, -1, 1), none_in(starts, 0, 2)


def short_filter(rows, halo, taps, shift_ref, edges):
    tokens, width = rows.shape
    moved = jnp.dot(shift_ref[...], rows, preferred_element_type=F32)
    behind, further = moved[:tokens], moved[tokens:]
    edge = halo.astype(F32)
    far, near = edge[0:1, :], edge[1:2, :]
    row = lax.broadcasted_iota(jnp.int32, (SUB, width), 0)
    top = behind[:SUB] + jnp.where(row == 0, near * edges[0], 0.0)
    behind = jnp.concatenate([top, behind[SUB:]], axis=0)
    top = further[:SUB] + jnp.where(row == 0, far * edges[1], jnp.where(row == 1, near * edges[2], 0.0))
    further = jnp.concatenate([top, further[SUB:]], axis=0)
    return taps[0:1, :] * rows.astype(F32) + taps[1:2, :] * behind + taps[2:3, :] * further


def lane_tile(tile):
    return pl.ds(pl.multiple_of(tile * LANE, LANE), LANE)


def cmul(a_re, a_im, b_re, b_im):
    return a_re * b_re - a_im * b_im, a_re * b_im + a_im * b_re


def column_sums(parts):
    row = lax.broadcasted_iota(jnp.int32, (SUB, LANE), 0)
    low = row < 4
    level = []
    for b in range(4):
        keep = jnp.where(low, parts[b], parts[b + 4])
        move = jnp.where(low, parts[b + 4], parts[b])
        level.append(keep + pltpu.roll(move, 4, 0))
    for step in (2, 1):
        clear = (row & step) == 0
        level = [
            jnp.where(
                clear,
                level[b] + pltpu.roll(level[b], SUB - step, 0),
                level[b + step] + pltpu.roll(level[b + step], step, 0),
            )
            for b in range(step)
        ]
    return level[0]


def rows_of(ref, h, lanes):
    return ref[pl.ds(h * SUB, SUB), lanes]


def half_lanes(place_ref, mine, half, offset, size):
    core = place_ref[0] & 1
    core = core if mine else 1 - core
    return pl.ds(pl.multiple_of(core * half + offset, LANE), size)


def front_kernel(lengths_ref, place_ref, f0_ref, f2_ref, halo_ref, taps_ref, pole_ref,
                 z_ref, e_ref, end_ref, last_s, shift_s, z_s):
    tokens = z_ref.shape[0]
    width = f0_ref.shape[2]
    count = tokens // BLK
    modes = pole_ref.shape[0] // 2
    halves = modes // SUB
    origin = pl.program_id(0) * width
    wide = z_s.shape[0] * LANE
    starts = starts_of(lengths_ref, place_ref[0] * tokens)
    edges = edge_flags(starts)

    @pl.when(pl.program_id(0) == 0)
    def _():
        t = row_iota(tokens)
        last = jnp.full((tokens, LANE), -1, jnp.int32)
        for s in starts:
            last = jnp.maximum(last, jnp.where(s <= (t | (BLK - 1)), s, -1))
        last_s[...] = jnp.where(t >= last, 1.0, 0.0)
        shift_s[...] = shift_matrix(starts, tokens)

    @pl.loop(0, width // wide)
    def _(part):
        lanes = pl.ds(pl.multiple_of(part * wide, LANE), wide)
        conv0, conv2 = (
            short_filter(ref[0, :, lanes], halo_ref[r, :, lanes], taps_ref[r, :, lanes], shift_s, edges)
            for r, ref in ((0, f0_ref), (2, f2_ref))
        )
        z = (conv0 * conv2).astype(BF16)
        z_ref[:, pl.ds(pl.multiple_of(origin + part * wide, LANE), wide)] = z
        for i in range(wide // LANE):
            z_s[i] = z[:, i * LANE : (i + 1) * LANE].astype(F32) * last_s[...]
        for i in range(wide // LANE):
            z_i = z_s.at[i]
            from_lane = pl.ds(pl.multiple_of(part * wide + i * LANE, LANE), LANE)
            to_lane = pl.ds(pl.multiple_of(origin + part * wide + i * LANE, LANE), LANE)
            p_re = [rows_of(pole_ref, h, from_lane) for h in range(halves)]
            p_im = [rows_of(pole_ref, halves + h, from_lane) for h in range(halves)]
            pow_re, pow_im = list(p_re), list(p_im)
            e_re, e_im = [], []
            for b in range(count):
                now = z_i[pl.ds(b * BLK + BLK - 1, SUB, stride=0), :]
                prev = z_i[pl.ds(b * BLK + BLK - 2, SUB, stride=0), :]
                e_re.append([now + p_re[h] * prev for h in range(halves)])
                e_im.append([p_im[h] * prev for h in range(halves)])
            for k in range(2, BLK):
                for h in range(halves):
                    pow_re[h], pow_im[h] = cmul(pow_re[h], pow_im[h], p_re[h], p_im[h])
                for b in range(count):
                    now = z_i[pl.ds(b * BLK + BLK - 1 - k, SUB, stride=0), :]
                    for h in range(halves):
                        e_re[b][h] = e_re[b][h] + pow_re[h] * now
                        e_im[b][h] = e_im[b][h] + pow_im[h] * now
            for h in range(halves):
                rows, rows_im = pl.ds(h * SUB, SUB), pl.ds(modes + h * SUB, SUB)
                for b in range(count):
                    e_ref[b, rows, to_lane] = e_re[b][h]
                    e_ref[b, rows_im, to_lane] = e_im[b][h]
                gate = cmul(pow_re[h], pow_im[h], p_re[h], p_im[h])
                level = [(e_re[b][h], e_im[b][h]) for b in range(count)]
                span = BLK
                while len(level) > 1:
                    joined = []
                    for i in range(0, len(level), 2):
                        flag = none_in(starts, (i + 1) * span, (i + 2) * span)
                        joined.append(advance(gate, flag, level[i], level[i + 1]))
                    level = joined
                    gate = cmul(*gate, *gate)
                    span *= 2
                end_ref[rows, to_lane] = level[0][0].astype(BF16)
                end_ref[rows_im, to_lane] = level[0][1].astype(BF16)


def middle_kernel(lengths_ref, place_ref, features_ref, halo_ref, taps_ref, z_ref, skip_ref, pole_ref,
                  coef_ref, base_ref, gain_ref, first_s, part_s, z_s, filt_s, acc_s, shift_s, piece_s, *, mine):
    tokens, half = z_ref.shape
    count = tokens // BLK
    modes = pole_ref.shape[0] // 2
    halves = modes // SUB
    starts = starts_of(lengths_ref, place_ref[0] * tokens)
    edges = edge_flags(starts)
    t = row_iota(tokens)
    t0 = t & (-BLK)
    piece = jnp.zeros((tokens, LANE), jnp.int32)
    opened = jnp.zeros((tokens, LANE), jnp.bool_)
    for s in starts:
        piece = piece + jnp.where((s > t0) & (s <= t), 1, 0)
        opened = opened | ((s >= t0) & (s <= t))
    part_s[...] = piece.astype(F32)
    first_s[...] = jnp.where(opened, 0.0, 1.0)
    shift_s[...] = shift_matrix(starts, tokens)

    pieces = []
    for b in range(count):
        inside = jnp.int32(1)
        for s in starts:
            inside = inside + ((s > b * BLK) & (s < (b + 1) * BLK)).astype(jnp.int32)
        pieces.append(inside)
    wide = TILE

    @pl.loop(0, half // wide)
    def _(part):
        here = pl.ds(pl.multiple_of(part * wide, LANE), wide)
        lanes = half_lanes(place_ref, mine, half, part * wide, wide)
        conv1 = short_filter(features_ref[1, :, lanes], halo_ref[1, :, lanes], taps_ref[1, :, lanes], shift_s, edges)
        base_ref[:, here] = conv1
        for i in range(wide // LANE):
            inner = pl.ds(pl.multiple_of(part * wide + i * LANE, LANE), LANE)
            gain_ref[:, inner] = conv1[:, i * LANE : (i + 1) * LANE] * first_s[...]

    @pl.loop(0, half // LANE)
    def _(tile):
        here = lane_tile(tile)
        lanes = half_lanes(place_ref, mine, half, tile * LANE, LANE)
        p_re = [rows_of(pole_ref, h, lanes) for h in range(halves)]
        p_im = [rows_of(pole_ref, halves + h, lanes) for h in range(halves)]
        q_re = [rows_of(coef_ref, h, lanes) for h in range(halves)]
        q_im = [rows_of(coef_ref, halves + h, lanes) for h in range(halves)]
        filt_s[pl.ds(0, BLK), :] = jnp.zeros((BLK, LANE), F32)
        for group in range(BLK // SUB):
            parts = []
            for k in range(SUB):
                parts.append(sum(q_re[1:], q_re[0]))
                for h in range(halves):
                    q_re[h], q_im[h] = cmul(q_re[h], q_im[h], p_re[h], p_im[h])
            filt_s[pl.ds(BLK + group * SUB, SUB), :] = column_sums(parts).astype(BF16).astype(F32)
        z = z_ref[:, here].astype(F32)
        z_s[...] = z
        acc = skip_ref[:, lanes] * z
        sums = [[acc[b * BLK + r * SUB : b * BLK + (r + 1) * SUB] for r in range(BLK // SUB)] for b in range(count)]
        for s in range(BLK):
            firsts = range(s // SUB, BLK // SUB)
            columns = {r: filt_s[pl.ds(BLK - s + r * SUB, SUB), :] for r in firsts}
            for b in range(count):
                value = z_s[pl.ds(b * BLK + s, SUB, stride=0), :]
                for r in firsts:
                    sums[b][r] = sums[b][r] + columns[r] * value
        for b in range(count):
            for r in range(BLK // SUB):
                acc_s[pl.ds(b * BLK + r * SUB, SUB), :] = sums[b][r]

        for b in range(count):
            @pl.when(pieces[b] > 1)
            def _(b=b):
                rows = pl.ds(b * BLK, BLK)
                acc_s[rows, :] = skip_ref[:, lanes] * z_s[rows, :]

                def one_piece(q, carry):
                    member = part_s[rows, :] == q.astype(F32)
                    piece_s[...] = jnp.where(member, z_s[rows, :], 0.0)
                    total = jnp.zeros((BLK, LANE), F32)
                    for s in range(BLK):
                        total = total + filt_s[pl.ds(BLK - s, BLK), :] * piece_s[pl.ds(s, 1), :]
                    acc_s[rows, :] = acc_s[rows, :] + jnp.where(member, total, 0.0)
                    return carry

                lax.fori_loop(0, pieces[b], one_piece, 0)

        base_ref[:, here] = base_ref[:, here] * acc_s[...]


def prepare_kernel(lengths_ref, place_ref, e_ref, pole_ref, coef_ref, table_ref, local_ref, reach_ref, turn_s, *, mine):
    count, packed, half = e_ref.shape
    modes = packed // 2
    halves = modes // SUB
    starts = starts_of(lengths_ref, place_ref[0] * count * BLK)
    flags = block_flags(starts, count)
    pitch = turn_s.shape[0] // BLK

    @pl.loop(0, half // LANE)
    def _(tile):
        here = lane_tile(tile)
        lanes = half_lanes(place_ref, mine, half, tile * LANE, LANE)
        for h in range(halves):
            rows, rows_im = pl.ds(h * SUB, SUB), pl.ds(modes + h * SUB, SUB)
            p = pole_ref[rows, lanes], pole_ref[rows_im, lanes]
            q = coef_ref[rows, lanes], coef_ref[rows_im, lanes]
            for k in range(BLK):
                q = cmul(*q, *p)
                turn_s[pl.ds(k * pitch + h * SUB, SUB), :] = q[0]
                turn_s[pl.ds(k * pitch + modes + h * SUB, SUB), :] = -q[1]
            gate = p
            for _ in range(BLK.bit_length() - 1):
                gate = cmul(*gate, *gate)
            zero = jnp.zeros((SUB, LANE), F32)
            state, reach = (zero, zero), (zero + 1.0, zero)
            for b in range(count):
                local_ref[b, rows, here], local_ref[b, rows_im, here] = state
                reach_ref[b, rows, here], reach_ref[b, rows_im, here] = reach
                if b < count - 1:
                    state = advance(gate, flags[b], state, (e_ref[b, rows, here], e_ref[b, rows_im, here]))
                    reach = tuple(flags[b] * x for x in cmul(*gate, *reach))
        for m in range(packed):
            for r in range(BLK // SUB):
                table_ref[m, pl.ds(r * SUB, SUB), here] = turn_s[pl.ds(r * SUB * pitch + m, SUB, stride=pitch), :]


def split(ref, lanes, *lead):
    modes = ref.shape[-2] // 2
    packed = ref[(*lead, slice(None), lanes)].astype(F32)
    return packed[:modes], packed[modes:]


def store(ref, lanes, pair):
    modes = ref.shape[-2] // 2
    ref[0:modes, lanes] = pair[0].astype(ref.dtype)
    ref[modes : 2 * modes, lanes] = pair[1].astype(ref.dtype)


def advance(gate, flag, state, addend):
    re, im = cmul(*gate, *state)
    return addend[0] + flag * re, addend[1] + flag * im


def choose(flag, a, b):
    return tuple(jnp.where(flag, x, y) for x, y in zip(a, b))


def first_kernel(lengths_ref, place_ref, kept_ref, came_ref, pole_ref, total_ref, send_ref, gate_ref, *, tokens):
    starts = starts_of(lengths_ref, 0)
    place = place_ref[0]
    odd = (place & 1) == 1
    second = place | 1
    flag = none_in(starts, second * tokens, (second + 1) * tokens)
    half = kept_ref.shape[1]

    @pl.loop(0, half // LANE)
    def _(tile):
        lanes = lane_tile(tile)
        kept, came = split(kept_ref, lanes), split(came_ref, lanes)
        gate = split(pole_ref, half_lanes(place_ref, True, half, tile * LANE, LANE))
        reach = 1
        while reach < tokens:
            gate = cmul(*gate, *gate)
            reach *= 2
        total = advance(gate, flag, choose(odd, came, kept), choose(odd, kept, came))
        store(total_ref, lanes, total)
        store(send_ref, lanes, total)
        store(gate_ref, lanes, gate)


def round_kernel(lengths_ref, place_ref, total_ref, met_ref, *refs, tokens, k, last):
    starts = starts_of(lengths_ref, 0)
    place = place_ref[0]
    distance = 1 << k
    upper = (place & distance) != 0
    group = (place >> k) << k
    even = (place >> 1) << 1
    later = group | distance
    enter = none_in(starts, group * tokens, even * tokens)
    enter = jnp.where(upper, enter, 0.0)
    whole = none_in(starts, later * tokens, (later + distance) * tokens)
    flag = none_in(starts, even * tokens, (even + 1) * tokens)

    @pl.loop(0, met_ref.shape[1] // LANE)
    def _(tile):
        lanes = lane_tile(tile)
        rest = list(refs)
        met, total = split(met_ref, lanes), split(total_ref, lanes)
        power = split(rest.pop(0), lanes)
        if k == 1:
            prefix = tuple(enter * x for x in met)
        else:
            before, prefix = split(rest.pop(0), lanes), split(rest.pop(0), lanes)
            prefix = advance(before, enter, met, prefix)
        if not last:
            total_out, send_ref, power_out, before_out, prefix_out = rest
            power = cmul(*power, *power)
            total = advance(power, whole, choose(upper, met, total), choose(upper, total, met))
            store(total_out, lanes, total)
            store(send_ref, lanes, total)
            store(prefix_out, lanes, prefix)
            store(power_out, lanes, power)
            if k == 1:
                before = choose(upper, power, (jnp.ones_like(met[0]), jnp.zeros_like(met[0])))
            else:
                before = choose(upper, cmul(*before, *power), before)
            store(before_out, lanes, before)
        else:
            gate_ref, kept_ref, came_ref, own_ref, send_ref = rest
            odd = (place & 1) == 1
            kept, came = split(kept_ref, lanes), split(came_ref, lanes)
            beyond = advance(split(gate_ref, lanes), flag, prefix, choose(odd, came, kept))
            store(own_ref, lanes, choose(odd, beyond, prefix))
            store(send_ref, lanes, choose(odd, prefix, beyond))


def back_kernel(place_ref, entry_ref, table_ref, local_ref, reach_ref, base_ref, gain_ref, *refs):
    out_ref, state_s = refs[-2:]
    tokens, width = out_ref.shape
    count, packed, _ = local_ref.shape
    modes = packed // 2
    halves = modes // SUB
    origin = pl.program_id(0) * width

    @pl.loop(0, width // LANE)
    def _(tile):
        lanes = lane_tile(tile)
        here = pl.ds(pl.multiple_of(origin + tile * LANE, LANE), LANE)
        entry = entry_ref[:, here].astype(F32)
        for h in range(halves):
            rows, rows_im = pl.ds(h * SUB, SUB), pl.ds(modes + h * SUB, SUB)
            first = entry[h * SUB : (h + 1) * SUB], entry[modes + h * SUB : modes + (h + 1) * SUB]
            for b in range(count):
                state = first
                if b:
                    state = cmul(reach_ref[b, rows, here], reach_ref[b, rows_im, here], *first)
                    state = state[0] + local_ref[b, rows, here], state[1] + local_ref[b, rows_im, here]
                state_s[pl.ds(b * packed + h * SUB, SUB), :] = state[0]
                state_s[pl.ds(b * packed + modes + h * SUB, SUB), :] = state[1]
        sums = [[None] * (BLK // SUB) for _ in range(count)]
        for m in range(packed):
            turn = [table_ref[m, pl.ds(r * SUB, SUB), here] for r in range(BLK // SUB)]
            for b in range(count):
                state = state_s[pl.ds(b * packed + m, SUB, stride=0), :]
                for r in range(BLK // SUB):
                    term = turn[r] * state
                    sums[b][r] = term if m == 0 else sums[b][r] + term
        for b in range(count):
            rows = pl.ds(b * BLK, BLK)
            carried = jnp.concatenate(sums[b], axis=0)
            out_ref[rows, lanes] = (base_ref[rows, here] + gain_ref[rows, here] * carried).astype(BF16)


def per_device(features, kernel, skip, residues, decay, freq, lengths):
    tokens = features.shape[1]
    modes, width = decay.shape
    half = width // 2
    count = tokens // BLK
    n = lax.axis_size("seq")
    place = lax.axis_index("seq")
    core = place % 2
    rounds = n.bit_length() - 1
    where = place.astype(jnp.int32)[None]

    rim = features[:, tokens - 2 :, :]
    inner = exchange(rim, 1)
    link = [(i, i + 1) for i in range(1, n - 1, 2)]
    outer = lax.ppermute(rim, "seq", link + [(b, a) for a, b in link])
    halo = jnp.where(core == 1, inner, outer)

    fade = jnp.exp(-decay)
    q = freq * freq
    sine = freq * (1 + q * (-1 / 6 + q * (1 / 120 + q * (-1 / 5040 + q * (1 / 362880)))))
    cosine = 1 + q * (-1 / 2 + q * (1 / 24 + q * (-1 / 720 + q * (1 / 40320 - q * (1 / 3628800)))))
    d = 2 * decay
    scale = jnp.sqrt(d * (1 - d * (1 / 2 - d * (1 / 6 - d * (1 / 24 - d * (1 / 120 - d * (1 / 720)))))))
    pole = jnp.stack([fade * cosine, fade * sine]).reshape(2 * modes, width)
    coef = (residues * scale[None]).reshape(2 * modes, width)

    params = pltpu.CompilerParams(vmem_limit_bytes=16 * 1024 * 1024)
    roomy = pltpu.CompilerParams(vmem_limit_bytes=ROOM * 1024 * 1024)
    plane = pltpu.VMEM((tokens, LANE), F32)
    shifts = pltpu.VMEM((2 * tokens, tokens), BF16)
    whole = pl.BlockSpec(memory_space=pltpu.VMEM)

    def call(body, args, outs, name, scratch=(), cost=0.8e9):
        return pl.pallas_call(
            body,
            grid_spec=pltpu.PrefetchScalarGridSpec(
                num_scalar_prefetch=2, grid=(), in_specs=[whole] * len(args), out_specs=[whole] * len(outs),
                scratch_shapes=scratch,
            ),
            out_shape=[jax.ShapeDtypeStruct(*o) for o in outs],
            compiler_params=params, name=name,
            cost_estimate=pl.CostEstimate(flops=int(cost), bytes_accessed=1 << 20, transcendentals=0),
        )(lengths, where, *args)

    packed = 2 * modes
    tiles = half // TILE
    state, sent = ((packed, half), F32), ((packed, half), BF16)
    blocks, plain = ((count, packed, half), F32), ((tokens, half), F32)

    def tile_of(mine, i, w_ref):
        core = w_ref[0] & 1
        return (core if mine else 1 - core) * tiles + i

    def front(mine):
        def columns(*lead):
            return pl.BlockSpec((*lead, TILE), lambda i, n_ref, w_ref: (*(0,) * len(lead), tile_of(mine, i, w_ref)))

        def stream(r):
            return pl.BlockSpec((1, tokens, TILE), lambda i, n_ref, w_ref: (r, 0, tile_of(mine, i, w_ref)))

        return pl.pallas_call(
            front_kernel,
            grid_spec=pltpu.PrefetchScalarGridSpec(
                num_scalar_prefetch=2, grid=(tiles,),
                in_specs=[stream(0), stream(2), columns(3, 2), columns(3, 3), columns(packed)],
                out_specs=[whole] * 3,
                scratch_shapes=[plane, shifts, pltpu.VMEM((TILE // LANE, tokens, LANE), F32)],
            ),
            out_shape=[jax.ShapeDtypeStruct((tokens, half), BF16), jax.ShapeDtypeStruct(*blocks),
                       jax.ShapeDtypeStruct(*sent)],
            compiler_params=roomy, name="front",
            cost_estimate=pl.CostEstimate(flops=5_000_000_000, bytes_accessed=4 << 20, transcendentals=0),
        )(lengths, where, features, features, halo, kernel, pole)

    def middle(mine, z):
        return call(
            functools.partial(middle_kernel, mine=mine), (features, halo, kernel, z, skip[None], pole, coef),
            (plain, plain), "middle", [plane, plane, plane, pltpu.VMEM((2 * BLK, LANE), F32), plane, shifts, pltpu.VMEM((BLK, LANE), F32)], cost=5e9,
        )

    def prepare(mine, e):
        return call(
            functools.partial(prepare_kernel, mine=mine), (e, pole, coef),
            (((packed, BLK, half), F32), blocks, blocks), "prepare", [pltpu.VMEM((BLK * PITCH, LANE), F32)], cost=4e9,
        )

    def back(mine, args, out):
        specs = [whole] * len(args)
        if out is not None:
            args, specs = args + (out,), specs + [pl.BlockSpec(memory_space=pl.ANY)]

        return pl.pallas_call(
            back_kernel,
            grid_spec=pltpu.PrefetchScalarGridSpec(
                num_scalar_prefetch=1, grid=(tiles,), in_specs=specs,
                out_specs=pl.BlockSpec((tokens, TILE), lambda i, w_ref: (0, tile_of(mine, i, w_ref))),
                scratch_shapes=[pltpu.VMEM((count * packed, LANE), F32)],
            ),
            out_shape=jax.ShapeDtypeStruct((tokens, width), BF16),
            input_output_aliases={} if out is None else {len(args): 0},
            compiler_params=params, name="back",
            cost_estimate=pl.CostEstimate(flops=3_500_000_000, bytes_accessed=1 << 20, transcendentals=0),
        )(where, *args)

    z_other, e_other, end_other = front(False)
    came = exchange(end_other, 1)
    z_own, e_own, end_own = front(True)
    total, send, gate = call(
        functools.partial(first_kernel, tokens=tokens), (end_own, came, pole), (state, sent, state), "first"
    )
    power, carry = gate, ()
    jobs = [lambda z: middle(True, z), lambda z: middle(False, z), lambda es: (*prepare(True, es[0]), *prepare(False, es[1]))]
    inputs = [z_own, z_other, (e_own, e_other)]
    ready = []
    for k in range(1, rounds):
        last = k == rounds - 1
        met = exchange(send, 1 << k)
        for job, operand in [(jobs.pop(0), inputs.pop(0)) for _ in range(len(jobs) if last else min(1, len(jobs)))]:
            operand, send = lax.optimization_barrier((operand, send))
            met, done = lax.optimization_barrier((met, job(operand)))
            ready.append(done)
        body = functools.partial(round_kernel, tokens=tokens, k=k, last=last)
        args = (total, met, power, *carry)
        if last:
            own, send = call(body, args + (gate, end_own, came), (state, sent), "round")
        else:
            total, send, power, *carry = call(body, args, (state, sent, state, state, state), "round")
    other = exchange(send, 1)
    out = back(True, (own, *ready[2][:3], *ready[0]), None)
    return back(False, (other, *ready[2][3:], *ready[1]), out)


def solution(mesh):
    return jax.shard_map(
        per_device,
        mesh=mesh,
        in_specs=(P(None, ("groups", "seq"), None), P(), P(), P(), P(), P(), P("groups")),
        out_specs=P(("groups", "seq"), None),
        check_vma=False,
    )
```

```python
import functools

import jax
import jax.numpy as jnp
from jax import lax
from jax.experimental import pallas as pl
from jax.experimental.pallas import tpu as pltpu
from jax.sharding import PartitionSpec as P

BLK = 16
LANE = 128
SUB = 8
TILE = 512
PITCH = 40
ROOM = 48
PIECE = 256
CHUNK = 512
UNROLL = 2
F32 = jnp.float32
BF16 = jnp.bfloat16


def exchange(block, distance):
    devices = range(lax.axis_size("seq"))
    return lax.ppermute(block, "seq", [(i, i ^ distance) for i in devices])


def row_iota(rows):
    return lax.broadcasted_iota(jnp.int32, (rows, LANE), 0)


def starts_of(lengths_ref, origin):
    starts, at = [], -origin
    for i in range(lengths_ref.shape[0]):
        starts.append(at)
        at = at + lengths_ref[i]
    return starts


def none_in(starts, first, beyond):
    hit = jnp.int32(0)
    for s in starts:
        hit = hit | ((s >= first) & (s < beyond)).astype(jnp.int32)
    return (1 - hit).astype(F32)


def block_flags(starts, count):
    return [none_in(starts, b * BLK, (b + 1) * BLK) for b in range(count)]


def shift_matrix(starts, tokens):
    t = lax.broadcasted_iota(jnp.int32, (tokens, tokens), 0)
    u = lax.broadcasted_iota(jnp.int32, (tokens, tokens), 1)
    here = jnp.zeros((tokens, tokens), jnp.bool_)
    before = jnp.zeros((tokens, tokens), jnp.bool_)
    for s in starts:
        here = here | (t == s)
        before = before | (t - 1 == s)
    one = jnp.where((u == t - 1) & ~here, 1.0, 0.0)
    two = jnp.where((u == t - 2) & ~(here | before), 1.0, 0.0)
    return jnp.concatenate([one, two], axis=0).astype(BF16)


def edge_flags(starts):
    return none_in(starts, 0, 1), none_in(starts, -1, 1), none_in(starts, 0, 2)


def short_filter(rows, halo, taps, shift_ref, edges):
    tokens, width = rows.shape
    moved = jnp.dot(shift_ref[...], rows, preferred_element_type=F32)
    behind, further = moved[:tokens], moved[tokens:]
    edge = halo.astype(F32)
    far, near = edge[0:1, :], edge[1:2, :]
    row = lax.broadcasted_iota(jnp.int32, (SUB, width), 0)
    top = behind[:SUB] + jnp.where(row == 0, near * edges[0], 0.0)
    behind = jnp.concatenate([top, behind[SUB:]], axis=0)
    top = further[:SUB] + jnp.where(row == 0, far * edges[1], jnp.where(row == 1, near * edges[2], 0.0))
    further = jnp.concatenate([top, further[SUB:]], axis=0)
    return taps[0:1, :] * rows.astype(F32) + taps[1:2, :] * behind + taps[2:3, :] * further


def lane_tile(tile):
    return pl.ds(pl.multiple_of(tile * LANE, LANE), LANE)


def cmul(a_re, a_im, b_re, b_im):
    return a_re * b_re - a_im * b_im, a_re * b_im + a_im * b_re


def column_sums(parts):
    row = lax.broadcasted_iota(jnp.int32, (SUB, LANE), 0)
    low = row < 4
    level = []
    for b in range(4):
        keep = jnp.where(low, parts[b], parts[b + 4])
        move = jnp.where(low, parts[b + 4], parts[b])
        level.append(keep + pltpu.roll(move, 4, 0))
    for step in (2, 1):
        clear = (row & step) == 0
        level = [
            jnp.where(
                clear,
                level[b] + pltpu.roll(level[b], SUB - step, 0),
                level[b + step] + pltpu.roll(level[b + step], step, 0),
            )
            for b in range(step)
        ]
    return level[0]


def rows_of(ref, h, lanes):
    return ref[pl.ds(h * SUB, SUB), lanes]


def half_lanes(place_ref, mine, half, offset, size):
    core = place_ref[0] & 1
    core = core if mine else 1 - core
    return pl.ds(pl.multiple_of(core * half + offset, LANE), size)


def front_kernel(lengths_ref, place_ref, features_ref, halo_ref, taps_ref, pole_ref, z_ref, e_ref, end_ref, *refs, mine):
    last_s, shift_s, z_s = refs[-3:]
    tokens, half = z_ref.shape
    count = tokens // BLK
    modes = pole_ref.shape[0] // 2
    halves = modes // SUB
    wide = TILE
    tiles = half // wide
    if mine:
        streams_ref = features_ref
    else:
        next_ref, streams_ref, sems, next_sems = refs[:4]
        for j in range(tiles):
            for u, r in enumerate((0, 2)):
                lanes = half_lanes(place_ref, mine, half, j * wide, wide)
                here = pl.ds(j * wide, wide)
                pltpu.make_async_copy(features_ref.at[r, :, lanes], streams_ref.at[u, :, here], sems.at[u, j]).start()
        lanes = half_lanes(place_ref, True, half, 0, half)
        ahead = [pltpu.make_async_copy(features_ref.at[r, :, lanes], next_ref.at[u], next_sems.at[u])
                 for u, r in enumerate((0, 2))]
        for copy in ahead:
            copy.start()
    starts = starts_of(lengths_ref, place_ref[0] * tokens)
    edges = edge_flags(starts)
    t = row_iota(tokens)
    last = jnp.full((tokens, LANE), -1, jnp.int32)
    for s in starts:
        last = jnp.maximum(last, jnp.where(s <= (t | (BLK - 1)), s, -1))
    last_s[...] = jnp.where(t >= last, 1.0, 0.0)
    shift_s[...] = shift_matrix(starts, tokens)
    flags = {}
    span = BLK
    while span < tokens:
        for first in range(span, tokens, 2 * span):
            flags[first, span] = none_in(starts, first, first + span)
        span *= 2

    @pl.loop(0, tiles)
    def _(j):
        if not mine:
            here = pl.ds(pl.multiple_of(j * wide, LANE), wide)
            lanes = half_lanes(place_ref, mine, half, j * wide, wide)
            for u, r in enumerate((0, 2)):
                pltpu.make_async_copy(features_ref.at[r, :, lanes], streams_ref.at[u, :, here], sems.at[u, j]).wait()

        def gated(i, size):
            at = pl.ds(pl.multiple_of(j * wide + i * LANE, LANE), size)
            lanes = half_lanes(place_ref, mine, half, j * wide + i * LANE, size)
            conv0, conv2 = (
                short_filter(streams_ref[u, :, at], halo_ref[r, :, lanes], taps_ref[r, :, lanes], shift_s, edges)
                for u, r in enumerate((0, 2))
            )
            z = (conv0 * conv2).astype(BF16)
            z_ref[:, at] = z
            for v in range(size // LANE):
                z_s[i + v] = z[:, v * LANE : (v + 1) * LANE].astype(F32) * last_s[...]

        def states(i):
            at = pl.ds(pl.multiple_of(j * wide + i * LANE, LANE), LANE)
            lanes = half_lanes(place_ref, mine, half, j * wide + i * LANE, LANE)
            z_i = z_s.at[i]
            p_re = [rows_of(pole_ref, h, lanes) for h in range(halves)]
            p_im = [rows_of(pole_ref, halves + h, lanes) for h in range(halves)]
            pow_re, pow_im = list(p_re), list(p_im)
            e_re, e_im = [], []
            for b in range(count):
                now = z_i[pl.ds(b * BLK + BLK - 1, SUB, stride=0), :]
                prev = z_i[pl.ds(b * BLK + BLK - 2, SUB, stride=0), :]
                e_re.append([now + p_re[h] * prev for h in range(halves)])
                e_im.append([p_im[h] * prev for h in range(halves)])
            for k in range(2, BLK):
                for h in range(halves):
                    pow_re[h], pow_im[h] = cmul(pow_re[h], pow_im[h], p_re[h], p_im[h])
                for b in range(count):
                    now = z_i[pl.ds(b * BLK + BLK - 1 - k, SUB, stride=0), :]
                    for h in range(halves):
                        e_re[b][h] = e_re[b][h] + pow_re[h] * now
                        e_im[b][h] = e_im[b][h] + pow_im[h] * now
            for h in range(halves):
                rows, rows_im = pl.ds(h * SUB, SUB), pl.ds(modes + h * SUB, SUB)
                for b in range(count):
                    e_ref[b, rows, at] = e_re[b][h]
                    e_ref[b, rows_im, at] = e_im[b][h]
                gate = cmul(pow_re[h], pow_im[h], p_re[h], p_im[h])
                level = [(e_re[b][h], e_im[b][h]) for b in range(count)]
                span = BLK
                while len(level) > 1:
                    level = [
                        advance(gate, flags[(i + 1) * span, span], level[i], level[i + 1])
                        for i in range(0, len(level), 2)
                    ]
                    gate = cmul(*gate, *gate)
                    span *= 2
                end_ref[rows, at] = level[0][0].astype(BF16)
                end_ref[rows_im, at] = level[0][1].astype(BF16)

        lane_tiles = wide // LANE
        gated(0, PIECE)
        for i in range(lane_tiles):
            following = (i // (PIECE // LANE) + 1) * (PIECE // LANE)
            if i % (PIECE // LANE) == 0 and following < lane_tiles:
                gated(following, PIECE)
            states(i)

    if not mine:
        for copy in ahead:
            copy.wait()


def middle_kernel(lengths_ref, place_ref, features_ref, halo_ref, taps_ref, z_ref, skip_ref, pole_ref,
                  coef_ref, base_ref, gain_ref, first_s, part_s, z_s, filt_s, acc_s, shift_s, piece_s, *, mine):
    tokens, half = z_ref.shape
    count = tokens // BLK
    modes = pole_ref.shape[0] // 2
    halves = modes // SUB
    starts = starts_of(lengths_ref, place_ref[0] * tokens)
    edges = edge_flags(starts)
    t = row_iota(tokens)
    t0 = t & (-BLK)
    piece = jnp.zeros((tokens, LANE), jnp.int32)
    opened = jnp.zeros((tokens, LANE), jnp.bool_)
    for s in starts:
        piece = piece + jnp.where((s > t0) & (s <= t), 1, 0)
        opened = opened | ((s >= t0) & (s <= t))
    part_s[...] = piece.astype(F32)
    first_s[...] = jnp.where(opened, 0.0, 1.0)
    shift_s[...] = shift_matrix(starts, tokens)

    pieces = []
    for b in range(count):
        inside = jnp.int32(1)
        for s in starts:
            inside = inside + ((s > b * BLK) & (s < (b + 1) * BLK)).astype(jnp.int32)
        pieces.append(inside)
    wide = TILE

    @pl.loop(0, half // wide)
    def _(part):
        here = pl.ds(pl.multiple_of(part * wide, LANE), wide)
        lanes = half_lanes(place_ref, mine, half, part * wide, wide)
        conv1 = short_filter(features_ref[1, :, lanes], halo_ref[1, :, lanes], taps_ref[1, :, lanes], shift_s, edges)
        base_ref[:, here] = conv1
        for i in range(wide // LANE):
            inner = pl.ds(pl.multiple_of(part * wide + i * LANE, LANE), LANE)
            gain_ref[:, inner] = conv1[:, i * LANE : (i + 1) * LANE] * first_s[...]

    @pl.loop(0, half // LANE)
    def _(tile):
        here = lane_tile(tile)
        lanes = half_lanes(place_ref, mine, half, tile * LANE, LANE)
        p_re = [rows_of(pole_ref, h, lanes) for h in range(halves)]
        p_im = [rows_of(pole_ref, halves + h, lanes) for h in range(halves)]
        q_re = [rows_of(coef_ref, h, lanes) for h in range(halves)]
        q_im = [rows_of(coef_ref, halves + h, lanes) for h in range(halves)]
        filt_s[pl.ds(0, BLK), :] = jnp.zeros((BLK, LANE), F32)
        for group in range(BLK // SUB):
            parts = []
            for k in range(SUB):
                parts.append(sum(q_re[1:], q_re[0]))
                for h in range(halves):
                    q_re[h], q_im[h] = cmul(q_re[h], q_im[h], p_re[h], p_im[h])
            filt_s[pl.ds(BLK + group * SUB, SUB), :] = column_sums(parts).astype(BF16).astype(F32)
        z = z_ref[:, here].astype(F32)
        z_s[...] = z
        acc = skip_ref[:, lanes] * z
        sums = [[acc[b * BLK + r * SUB : b * BLK + (r + 1) * SUB] for r in range(BLK // SUB)] for b in range(count)]
        for s in range(BLK):
            firsts = range(s // SUB, BLK // SUB)
            columns = {r: filt_s[pl.ds(BLK - s + r * SUB, SUB), :] for r in firsts}
            for b in range(count):
                value = z_s[pl.ds(b * BLK + s, SUB, stride=0), :]
                for r in firsts:
                    sums[b][r] = sums[b][r] + columns[r] * value
        for b in range(count):
            for r in range(BLK // SUB):
                acc_s[pl.ds(b * BLK + r * SUB, SUB), :] = sums[b][r]

        for b in range(count):
            @pl.when(pieces[b] > 1)
            def _(b=b):
                rows = pl.ds(b * BLK, BLK)
                acc_s[rows, :] = skip_ref[:, lanes] * z_s[rows, :]

                def one_piece(q, carry):
                    member = part_s[rows, :] == q.astype(F32)
                    piece_s[...] = jnp.where(member, z_s[rows, :], 0.0)
                    total = jnp.zeros((BLK, LANE), F32)
                    for s in range(BLK):
                        total = total + filt_s[pl.ds(BLK - s, BLK), :] * piece_s[pl.ds(s, 1), :]
                    acc_s[rows, :] = acc_s[rows, :] + jnp.where(member, total, 0.0)
                    return carry

                lax.fori_loop(0, pieces[b], one_piece, 0)

        base_ref[:, here] = base_ref[:, here] * acc_s[...]


def prepare_kernel(lengths_ref, place_ref, e_ref, pole_ref, coef_ref, table_ref, local_ref, reach_ref, turn_s, *, mine):
    count, packed, half = e_ref.shape
    modes = packed // 2
    halves = modes // SUB
    starts = starts_of(lengths_ref, place_ref[0] * count * BLK)
    flags = block_flags(starts, count)
    pitch = turn_s.shape[0] // BLK

    @pl.loop(0, half // LANE)
    def _(tile):
        here = lane_tile(tile)
        lanes = half_lanes(place_ref, mine, half, tile * LANE, LANE)
        for h in range(halves):
            rows, rows_im = pl.ds(h * SUB, SUB), pl.ds(modes + h * SUB, SUB)
            p = pole_ref[rows, lanes], pole_ref[rows_im, lanes]
            q = coef_ref[rows, lanes], coef_ref[rows_im, lanes]
            for k in range(BLK):
                q = cmul(*q, *p)
                turn_s[pl.ds(k * pitch + h * SUB, SUB), :] = q[0]
                turn_s[pl.ds(k * pitch + modes + h * SUB, SUB), :] = -q[1]
            gate = p
            for _ in range(BLK.bit_length() - 1):
                gate = cmul(*gate, *gate)
            zero = jnp.zeros((SUB, LANE), F32)
            state, reach = (zero, zero), (zero + 1.0, zero)
            for b in range(count):
                local_ref[b, rows, here], local_ref[b, rows_im, here] = state
                reach_ref[b, rows, here], reach_ref[b, rows_im, here] = reach
                if b < count - 1:
                    state = advance(gate, flags[b], state, (e_ref[b, rows, here], e_ref[b, rows_im, here]))
                    reach = tuple(flags[b] * x for x in cmul(*gate, *reach))
        for m in range(packed):
            for r in range(BLK // SUB):
                table_ref[m, pl.ds(r * SUB, SUB), here] = turn_s[pl.ds(r * SUB * pitch + m, SUB, stride=pitch), :]


def split(ref, lanes, *lead):
    modes = ref.shape[-2] // 2
    packed = ref[(*lead, slice(None), lanes)].astype(F32)
    return packed[:modes], packed[modes:]


def store(ref, lanes, pair):
    modes = ref.shape[-2] // 2
    ref[0:modes, lanes] = pair[0].astype(ref.dtype)
    ref[modes : 2 * modes, lanes] = pair[1].astype(ref.dtype)


def advance(gate, flag, state, addend):
    re, im = cmul(*gate, *state)
    return addend[0] + flag * re, addend[1] + flag * im


def choose(flag, a, b):
    return tuple(jnp.where(flag, x, y) for x, y in zip(a, b))


def first_kernel(lengths_ref, place_ref, kept_ref, came_ref, pole_ref, total_ref, send_ref, gate_ref, *, tokens):
    starts = starts_of(lengths_ref, 0)
    place = place_ref[0]
    odd = (place & 1) == 1
    second = place | 1
    flag = none_in(starts, second * tokens, (second + 1) * tokens)
    half = kept_ref.shape[1]

    @pl.loop(0, half // CHUNK)
    def _(part):
        lanes = pl.ds(pl.multiple_of(part * CHUNK, LANE), CHUNK)
        kept, came = split(kept_ref, lanes), split(came_ref, lanes)
        gate = split(pole_ref, half_lanes(place_ref, True, half, part * CHUNK, CHUNK))
        reach = 1
        while reach < tokens:
            gate = cmul(*gate, *gate)
            reach *= 2
        total = advance(gate, flag, choose(odd, came, kept), choose(odd, kept, came))
        store(total_ref, lanes, total)
        store(send_ref, lanes, total)
        store(gate_ref, lanes, gate)


def round_kernel(lengths_ref, place_ref, total_ref, met_ref, *refs, tokens, k, last):
    starts = starts_of(lengths_ref, 0)
    place = place_ref[0]
    distance = 1 << k
    upper = (place & distance) != 0
    group = (place >> k) << k
    even = (place >> 1) << 1
    later = group | distance
    enter = none_in(starts, group * tokens, even * tokens)
    enter = jnp.where(upper, enter, 0.0)
    whole = none_in(starts, later * tokens, (later + distance) * tokens)
    flag = none_in(starts, even * tokens, (even + 1) * tokens)

    @pl.loop(0, met_ref.shape[1] // CHUNK)
    def _(part):
        lanes = pl.ds(pl.multiple_of(part * CHUNK, LANE), CHUNK)
        rest = list(refs)
        met, total = split(met_ref, lanes), split(total_ref, lanes)
        power = split(rest.pop(0), lanes)
        if k == 1:
            prefix = tuple(enter * x for x in met)
        else:
            before, prefix = split(rest.pop(0), lanes), split(rest.pop(0), lanes)
            prefix = advance(before, enter, met, prefix)
        if not last:
            total_out, send_ref, power_out, before_out, prefix_out = rest
            power = cmul(*power, *power)
            total = advance(power, whole, choose(upper, met, total), choose(upper, total, met))
            store(total_out, lanes, total)
            store(send_ref, lanes, total)
            store(prefix_out, lanes, prefix)
            store(power_out, lanes, power)
            if k == 1:
                before = choose(upper, power, (jnp.ones_like(met[0]), jnp.zeros_like(met[0])))
            else:
                before = choose(upper, cmul(*before, *power), before)
            store(before_out, lanes, before)
        else:
            gate_ref, kept_ref, came_ref, own_ref, send_ref = rest
            odd = (place & 1) == 1
            kept, came = split(kept_ref, lanes), split(came_ref, lanes)
            beyond = advance(split(gate_ref, lanes), flag, prefix, choose(odd, came, kept))
            store(own_ref, lanes, choose(odd, beyond, prefix))
            store(send_ref, lanes, choose(odd, prefix, beyond))


def back_kernel(place_ref, entry_ref, table_ref, local_ref, reach_ref, base_ref, gain_ref, *refs):
    out_ref, state_s = refs[-2:]
    tokens, width = out_ref.shape
    count, packed, _ = local_ref.shape
    modes = packed // 2
    halves = modes // SUB
    origin = pl.program_id(0) * width

    def one_tile(tile, state_s):
        lanes = lane_tile(tile)
        here = pl.ds(pl.multiple_of(origin + tile * LANE, LANE), LANE)
        entry = entry_ref[:, here].astype(F32)
        for h in range(halves):
            rows, rows_im = pl.ds(h * SUB, SUB), pl.ds(modes + h * SUB, SUB)
            first = entry[h * SUB : (h + 1) * SUB], entry[modes + h * SUB : modes + (h + 1) * SUB]
            for b in range(count):
                state = first
                if b:
                    state = cmul(reach_ref[b, rows, here], reach_ref[b, rows_im, here], *first)
                    state = state[0] + local_ref[b, rows, here], state[1] + local_ref[b, rows_im, here]
                state_s[pl.ds(b * packed + h * SUB, SUB), :] = state[0]
                state_s[pl.ds(b * packed + modes + h * SUB, SUB), :] = state[1]
        sums = [[None] * (BLK // SUB) for _ in range(count)]
        for m in range(packed):
            turn = [table_ref[m, pl.ds(r * SUB, SUB), here] for r in range(BLK // SUB)]
            for b in range(count):
                state = state_s[pl.ds(b * packed + m, SUB, stride=0), :]
                for r in range(BLK // SUB):
                    term = turn[r] * state
                    sums[b][r] = term if m == 0 else sums[b][r] + term
        for b in range(count):
            rows = pl.ds(b * BLK, BLK)
            carried = jnp.concatenate(sums[b], axis=0)
            out_ref[rows, lanes] = (base_ref[rows, here] + gain_ref[rows, here] * carried).astype(BF16)

    @pl.loop(0, width // LANE // state_s.shape[0])
    def _(step):
        for v in range(state_s.shape[0]):
            one_tile(step * state_s.shape[0] + v, state_s.at[v])


def per_device(features, kernel, skip, residues, decay, freq, lengths):
    tokens = features.shape[1]
    modes, width = decay.shape
    half = width // 2
    count = tokens // BLK
    n = lax.axis_size("seq")
    place = lax.axis_index("seq")
    core = place % 2
    rounds = n.bit_length() - 1
    where = place.astype(jnp.int32)[None]

    rim = features[:, tokens - 2 :, :]
    halo = lax.ppermute(rim, "seq", [(i, (i + 1) % n) for i in range(n)])

    fade = jnp.exp(-decay)
    q = freq * freq
    sine = freq * (1 + q * (-1 / 6 + q * (1 / 120 + q * (-1 / 5040 + q * (1 / 362880)))))
    cosine = 1 + q * (-1 / 2 + q * (1 / 24 + q * (-1 / 720 + q * (1 / 40320 - q * (1 / 3628800)))))
    d = 2 * decay
    scale = jnp.sqrt(d * (1 - d * (1 / 2 - d * (1 / 6 - d * (1 / 24 - d * (1 / 120 - d * (1 / 720)))))))
    pole = jnp.stack([fade * cosine, fade * sine]).reshape(2 * modes, width)
    coef = (residues * scale[None]).reshape(2 * modes, width)

    params = pltpu.CompilerParams(vmem_limit_bytes=16 * 1024 * 1024)
    roomy = pltpu.CompilerParams(vmem_limit_bytes=ROOM * 1024 * 1024)
    plane = pltpu.VMEM((tokens, LANE), F32)
    shifts = pltpu.VMEM((2 * tokens, tokens), BF16)
    whole = pl.BlockSpec(memory_space=pltpu.VMEM)

    def call(body, args, outs, name, scratch=(), cost=0.8e9):
        return pl.pallas_call(
            body,
            grid_spec=pltpu.PrefetchScalarGridSpec(
                num_scalar_prefetch=2, grid=(), in_specs=[whole] * len(args), out_specs=[whole] * len(outs),
                scratch_shapes=scratch,
            ),
            out_shape=[jax.ShapeDtypeStruct(*o) for o in outs],
            compiler_params=params, name=name,
            cost_estimate=pl.CostEstimate(flops=int(cost), bytes_accessed=1 << 20, transcendentals=0),
        )(lengths, where, *args)

    packed = 2 * modes
    tiles = half // TILE
    state, sent = ((packed, half), F32), ((packed, half), BF16)
    blocks, plain = ((count, packed, half), F32), ((tokens, half), F32)

    def tile_of(mine, i, w_ref):
        core = w_ref[0] & 1
        return (core if mine else 1 - core) * tiles + i

    def front(mine, streams):
        outs = [((tokens, half), BF16), blocks, sent]
        scratch = [plane, shifts, pltpu.VMEM((TILE // LANE, tokens, LANE), F32)]
        if not mine:
            pair = (2, tokens, half)
            outs = outs + [(pair, BF16)]
            scratch = [pltpu.VMEM(pair, BF16), pltpu.SemaphoreType.DMA((2, half // TILE)),
                       pltpu.SemaphoreType.DMA((2,))] + scratch
        return pl.pallas_call(
            functools.partial(front_kernel, mine=mine),
            grid_spec=pltpu.PrefetchScalarGridSpec(
                num_scalar_prefetch=2, grid=(),
                in_specs=[whole if mine else pl.BlockSpec(memory_space=pl.ANY)] + [whole] * 3,
                out_specs=[whole] * len(outs), scratch_shapes=scratch,
            ),
            out_shape=[jax.ShapeDtypeStruct(*o) for o in outs],
            compiler_params=params if mine else roomy, name="front",
            cost_estimate=pl.CostEstimate(flops=5_000_000_000, bytes_accessed=4 << 20, transcendentals=0),
        )(lengths, where, streams, halo, kernel, pole)

    def middle(mine, z):
        return call(
            functools.partial(middle_kernel, mine=mine), (features, halo, kernel, z, skip[None], pole, coef),
            (plain, plain), "middle", [plane, plane, plane, pltpu.VMEM((2 * BLK, LANE), F32), plane, shifts, pltpu.VMEM((BLK, LANE), F32)], cost=5e9,
        )

    def prepare(mine, e):
        return call(
            functools.partial(prepare_kernel, mine=mine), (e, pole, coef),
            (((packed, BLK, half), F32), blocks, blocks), "prepare", [pltpu.VMEM((BLK * PITCH, LANE), F32)], cost=4e9,
        )

    def back(mine, args, out):
        specs = [whole] * len(args)
        if out is not None:
            args, specs = args + (out,), specs + [pl.BlockSpec(memory_space=pl.ANY)]

        return pl.pallas_call(
            back_kernel,
            grid_spec=pltpu.PrefetchScalarGridSpec(
                num_scalar_prefetch=1, grid=(tiles,), in_specs=specs,
                out_specs=pl.BlockSpec((tokens, TILE), lambda i, w_ref: (0, tile_of(mine, i, w_ref))),
                scratch_shapes=[pltpu.VMEM((UNROLL, count * packed, LANE), F32)],
            ),
            out_shape=jax.ShapeDtypeStruct((tokens, width), BF16),
            input_output_aliases={} if out is None else {len(args): 0},
            compiler_params=params, name="back",
            cost_estimate=pl.CostEstimate(flops=3_500_000_000, bytes_accessed=1 << 20, transcendentals=0),
        )(where, *args)

    z_other, e_other, end_other, streams = front(False, features)
    came = exchange(end_other, 1)
    z_own, e_own, end_own = front(True, streams)
    total, send, gate = call(
        functools.partial(first_kernel, tokens=tokens), (end_own, came, pole), (state, sent, state), "first"
    )
    power, carry = gate, ()
    jobs = [lambda z: middle(True, z), lambda z: middle(False, z), lambda es: (*prepare(True, es[0]), *prepare(False, es[1]))]
    inputs = [z_own, z_other, (e_own, e_other)]
    ready = []
    for k in range(1, rounds):
        last = k == rounds - 1
        met = exchange(send, 1 << k)
        for job, operand in [(jobs.pop(0), inputs.pop(0)) for _ in range(len(jobs) if last else min(1, len(jobs)))]:
            operand, send = lax.optimization_barrier((operand, send))
            met, done = lax.optimization_barrier((met, job(operand)))
            ready.append(done)
        body = functools.partial(round_kernel, tokens=tokens, k=k, last=last)
        args = (total, met, power, *carry)
        if last:
            own, send = call(body, args + (gate, end_own, came), (state, sent), "round")
        else:
            total, send, power, *carry = call(body, args, (state, sent, state, state, state), "round")
    other = exchange(send, 1)
    out = back(True, (own, *ready[2][:3], *ready[0]), None)
    return back(False, (other, *ready[2][3:], *ready[1]), out)


def solution(mesh):
    return jax.shard_map(
        per_device,
        mesh=mesh,
        in_specs=(P(None, ("groups", "seq"), None), P(), P(), P(), P(), P(), P("groups")),
        out_specs=P(("groups", "seq"), None),
        check_vma=False,
    )
```

```python
import functools

import jax
import jax.numpy as jnp
from jax import lax
from jax.experimental import pallas as pl
from jax.experimental.pallas import tpu as pltpu
from jax.sharding import PartitionSpec as P

BLK = 16
LANE = 128
SUB = 8
TILE = 512
PITCH = 40
ROOM = 50
PIECE = 256
CHUNK = 512
UNROLL = 2
F32 = jnp.float32
BF16 = jnp.bfloat16


def exchange(block, distance):
    devices = range(lax.axis_size("seq"))
    return lax.ppermute(block, "seq", [(i, i ^ distance) for i in devices])


def row_iota(rows):
    return lax.broadcasted_iota(jnp.int32, (rows, LANE), 0)


def starts_of(lengths_ref, origin):
    starts, at = [], -origin
    for i in range(lengths_ref.shape[0]):
        starts.append(at)
        at = at + lengths_ref[i]
    return starts


def none_in(starts, first, beyond):
    hit = jnp.int32(0)
    for s in starts:
        hit = hit | ((s >= first) & (s < beyond)).astype(jnp.int32)
    return (1 - hit).astype(F32)


def block_flags(starts, count):
    return [none_in(starts, b * BLK, (b + 1) * BLK) for b in range(count)]


def shift_matrix(starts, tokens):
    t = lax.broadcasted_iota(jnp.int32, (tokens, tokens), 0)
    u = lax.broadcasted_iota(jnp.int32, (tokens, tokens), 1)
    here = jnp.zeros((tokens, tokens), jnp.bool_)
    before = jnp.zeros((tokens, tokens), jnp.bool_)
    for s in starts:
        here = here | (t == s)
        before = before | (t - 1 == s)
    one = jnp.where((u == t - 1) & ~here, 1.0, 0.0)
    two = jnp.where((u == t - 2) & ~(here | before), 1.0, 0.0)
    return jnp.concatenate([one, two], axis=0).astype(BF16)


def edge_flags(starts):
    return none_in(starts, 0, 1), none_in(starts, -1, 1), none_in(starts, 0, 2)


def short_filter(rows, halo, taps, shift_ref, edges):
    tokens, width = rows.shape
    moved = jnp.dot(shift_ref[...], rows, preferred_element_type=F32)
    behind, further = moved[:tokens], moved[tokens:]
    edge = halo.astype(F32)
    far, near = edge[0:1, :], edge[1:2, :]
    row = lax.broadcasted_iota(jnp.int32, (SUB, width), 0)
    top = behind[:SUB] + jnp.where(row == 0, near * edges[0], 0.0)
    behind = jnp.concatenate([top, behind[SUB:]], axis=0)
    top = further[:SUB] + jnp.where(row == 0, far * edges[1], jnp.where(row == 1, near * edges[2], 0.0))
    further = jnp.concatenate([top, further[SUB:]], axis=0)
    return taps[0:1, :] * rows.astype(F32) + taps[1:2, :] * behind + taps[2:3, :] * further


def lane_tile(tile):
    return pl.ds(pl.multiple_of(tile * LANE, LANE), LANE)


def cmul(a_re, a_im, b_re, b_im):
    return a_re * b_re - a_im * b_im, a_re * b_im + a_im * b_re


def column_sums(parts):
    row = lax.broadcasted_iota(jnp.int32, (SUB, LANE), 0)
    low = row < 4
    level = []
    for b in range(4):
        keep = jnp.where(low, parts[b], parts[b + 4])
        move = jnp.where(low, parts[b + 4], parts[b])
        level.append(keep + pltpu.roll(move, 4, 0))
    for step in (2, 1):
        clear = (row & step) == 0
        level = [
            jnp.where(
                clear,
                level[b] + pltpu.roll(level[b], SUB - step, 0),
                level[b + step] + pltpu.roll(level[b + step], step, 0),
            )
            for b in range(step)
        ]
    return level[0]


def rows_of(ref, h, lanes):
    return ref[pl.ds(h * SUB, SUB), lanes]


def half_lanes(mine, half, offset, size):
    core = lax.axis_index("seq") & 1
    core = core if mine else 1 - core
    return pl.ds(pl.multiple_of(core * half + offset, LANE), size)


def flag_rows(rounds):
    names = ["odd", "second", "even", "edge0", "edge1", "edge2"] + [("tree", i) for i in range(16)]
    names += [(kind, k) for k in range(1, rounds) for kind in ("upper", "enter", "whole")]
    return {name: i for i, name in enumerate(names)}


def prelude_kernel(lengths_ref, features_ref, streams_ref, shift_ref, last_ref, flags_ref, sems, *, rounds):
    copies = [pltpu.make_async_copy(features_ref.at[r], streams_ref.at[u], sems.at[u]) for u, r in enumerate((0, 2))]
    for copy in copies:
        copy.start()
    tokens = streams_ref.shape[1]
    place = lax.axis_index("seq")
    starts = starts_of(lengths_ref, place * tokens)
    t = row_iota(tokens)
    last = jnp.full((tokens, LANE), -1, jnp.int32)
    for s in starts:
        last = jnp.maximum(last, jnp.where(s <= (t | (BLK - 1)), s, -1))
    last_ref[...] = jnp.where(t >= last, 1.0, 0.0)
    shift_ref[...] = shift_matrix(starts, tokens)
    values = dict(zip(("edge0", "edge1", "edge2"), edge_flags(starts)))
    span, i = BLK, 0
    while span < tokens:
        for first in range(span, tokens, 2 * span):
            values["tree", i] = none_in(starts, first, first + span)
            i += 1
        span *= 2
    starts = starts_of(lengths_ref, 0)
    even, second = place & -2, place | 1
    values["odd"] = (place & 1).astype(F32)
    values["even"] = none_in(starts, even * tokens, (even + 1) * tokens)
    values["second"] = none_in(starts, second * tokens, (second + 1) * tokens)
    for k in range(1, rounds):
        distance = 1 << k
        upper = ((place >> k) & 1).astype(F32)
        group = (place >> k) << k
        later = group | distance
        values["upper", k] = upper
        values["enter", k] = upper * none_in(starts, group * tokens, even * tokens)
        values["whole", k] = none_in(starts, later * tokens, (later + distance) * tokens)
    for name, row in flag_rows(rounds).items():
        if name in values:
            flags_ref[row : row + 1, :] = jnp.full((1, CHUNK), values[name], F32)
    for copy in copies:
        copy.wait()


def front_kernel(streams_ref, halo_ref, taps_ref, pole_ref, shift_s, last_s, flags_ref, z_ref, e_ref, end_ref, z_s, *, mine):
    tokens, half = z_ref.shape
    count = tokens // BLK
    modes = pole_ref.shape[0] // 2
    halves = modes // SUB
    wide = TILE
    rows_at = flag_rows(1)

    def flag(name, size):
        return flags_ref[rows_at[name] : rows_at[name] + 1, 0:size]

    edges = [flag(name, PIECE) for name in ("edge0", "edge1", "edge2")]

    @pl.loop(0, half // wide)
    def _(j):
        def gated(i, size):
            at = pl.ds(pl.multiple_of(j * wide + i * LANE, LANE), size)
            lanes = half_lanes(mine, half, j * wide + i * LANE, size)
            conv0, conv2 = (
                short_filter(streams_ref[u, :, lanes], halo_ref[r, :, lanes], taps_ref[r, :, lanes], shift_s, edges)
                for u, r in enumerate((0, 2))
            )
            z = (conv0 * conv2).astype(BF16)
            z_ref[:, at] = z
            for v in range(size // LANE):
                z_s[i + v] = z[:, v * LANE : (v + 1) * LANE].astype(F32) * last_s[...]

        def states(i):
            at = pl.ds(pl.multiple_of(j * wide + i * LANE, LANE), LANE)
            lanes = half_lanes(mine, half, j * wide + i * LANE, LANE)
            z_i = z_s.at[i]
            p_re = [rows_of(pole_ref, h, lanes) for h in range(halves)]
            p_im = [rows_of(pole_ref, halves + h, lanes) for h in range(halves)]
            pow_re, pow_im = list(p_re), list(p_im)
            e_re, e_im = [], []
            for b in range(count):
                now = z_i[pl.ds(b * BLK + BLK - 1, SUB, stride=0), :]
                prev = z_i[pl.ds(b * BLK + BLK - 2, SUB, stride=0), :]
                e_re.append([now + p_re[h] * prev for h in range(halves)])
                e_im.append([p_im[h] * prev for h in range(halves)])
            for k in range(2, BLK):
                for h in range(halves):
                    pow_re[h], pow_im[h] = cmul(pow_re[h], pow_im[h], p_re[h], p_im[h])
                for b in range(count):
                    now = z_i[pl.ds(b * BLK + BLK - 1 - k, SUB, stride=0), :]
                    for h in range(halves):
                        e_re[b][h] = e_re[b][h] + pow_re[h] * now
                        e_im[b][h] = e_im[b][h] + pow_im[h] * now
            for h in range(halves):
                rows, rows_im = pl.ds(h * SUB, SUB), pl.ds(modes + h * SUB, SUB)
                for b in range(count):
                    e_ref[b, rows, at] = e_re[b][h]
                    e_ref[b, rows_im, at] = e_im[b][h]
                gate = cmul(pow_re[h], pow_im[h], p_re[h], p_im[h])
                level = [(e_re[b][h], e_im[b][h]) for b in range(count)]
                step = 0
                while len(level) > 1:
                    pairs = range(0, len(level), 2)
                    level = [
                        advance(gate, flag(("tree", step + i // 2), LANE), level[i], level[i + 1]) for i in pairs
                    ]
                    step += len(pairs)
                    gate = cmul(*gate, *gate)
                end_ref[rows, at] = level[0][0].astype(BF16)
                end_ref[rows_im, at] = level[0][1].astype(BF16)

        lane_tiles = wide // LANE
        gated(0, PIECE)
        for i in range(lane_tiles):
            following = (i // (PIECE // LANE) + 1) * (PIECE // LANE)
            if i % (PIECE // LANE) == 0 and following < lane_tiles:
                gated(following, PIECE)
            states(i)


def middle_kernel(lengths_ref, features_ref, halo_ref, taps_ref, z_ref, skip_ref, pole_ref,
                  coef_ref, base_ref, gain_ref, first_s, part_s, z_s, filt_s, acc_s, shift_s, piece_s, *, mine):
    tokens, half = z_ref.shape
    count = tokens // BLK
    modes = pole_ref.shape[0] // 2
    halves = modes // SUB
    starts = starts_of(lengths_ref, lax.axis_index("seq") * tokens)
    edges = edge_flags(starts)
    t = row_iota(tokens)
    t0 = t & (-BLK)
    piece = jnp.zeros((tokens, LANE), jnp.int32)
    opened = jnp.zeros((tokens, LANE), jnp.bool_)
    for s in starts:
        piece = piece + jnp.where((s > t0) & (s <= t), 1, 0)
        opened = opened | ((s >= t0) & (s <= t))
    part_s[...] = piece.astype(F32)
    first_s[...] = jnp.where(opened, 0.0, 1.0)
    shift_s[...] = shift_matrix(starts, tokens)

    pieces = []
    for b in range(count):
        inside = jnp.int32(1)
        for s in starts:
            inside = inside + ((s > b * BLK) & (s < (b + 1) * BLK)).astype(jnp.int32)
        pieces.append(inside)
    wide = TILE

    @pl.loop(0, half // wide)
    def _(part):
        here = pl.ds(pl.multiple_of(part * wide, LANE), wide)
        lanes = half_lanes(mine, half, part * wide, wide)
        conv1 = short_filter(features_ref[1, :, lanes], halo_ref[1, :, lanes], taps_ref[1, :, lanes], shift_s, edges)
        base_ref[:, here] = conv1
        for i in range(wide // LANE):
            inner = pl.ds(pl.multiple_of(part * wide + i * LANE, LANE), LANE)
            gain_ref[:, inner] = conv1[:, i * LANE : (i + 1) * LANE] * first_s[...]

    @pl.loop(0, half // LANE)
    def _(tile):
        here = lane_tile(tile)
        lanes = half_lanes(mine, half, tile * LANE, LANE)
        p_re = [rows_of(pole_ref, h, lanes) for h in range(halves)]
        p_im = [rows_of(pole_ref, halves + h, lanes) for h in range(halves)]
        q_re = [rows_of(coef_ref, h, lanes) for h in range(halves)]
        q_im = [rows_of(coef_ref, halves + h, lanes) for h in range(halves)]
        filt_s[pl.ds(0, BLK), :] = jnp.zeros((BLK, LANE), F32)
        for group in range(BLK // SUB):
            parts = []
            for k in range(SUB):
                parts.append(sum(q_re[1:], q_re[0]))
                for h in range(halves):
                    q_re[h], q_im[h] = cmul(q_re[h], q_im[h], p_re[h], p_im[h])
            filt_s[pl.ds(BLK + group * SUB, SUB), :] = column_sums(parts).astype(BF16).astype(F32)
        z = z_ref[:, here].astype(F32)
        z_s[...] = z
        acc = skip_ref[:, lanes] * z
        sums = [[acc[b * BLK + r * SUB : b * BLK + (r + 1) * SUB] for r in range(BLK // SUB)] for b in range(count)]
        for s in range(BLK):
            firsts = range(s // SUB, BLK // SUB)
            columns = {r: filt_s[pl.ds(BLK - s + r * SUB, SUB), :] for r in firsts}
            for b in range(count):
                value = z_s[pl.ds(b * BLK + s, SUB, stride=0), :]
                for r in firsts:
                    sums[b][r] = sums[b][r] + columns[r] * value
        for b in range(count):
            for r in range(BLK // SUB):
                acc_s[pl.ds(b * BLK + r * SUB, SUB), :] = sums[b][r]

        for b in range(count):
            @pl.when(pieces[b] > 1)
            def _(b=b):
                rows = pl.ds(b * BLK, BLK)
                acc_s[rows, :] = skip_ref[:, lanes] * z_s[rows, :]

                def one_piece(q, carry):
                    member = part_s[rows, :] == q.astype(F32)
                    piece_s[...] = jnp.where(member, z_s[rows, :], 0.0)
                    total = jnp.zeros((BLK, LANE), F32)
                    for s in range(BLK):
                        total = total + filt_s[pl.ds(BLK - s, BLK), :] * piece_s[pl.ds(s, 1), :]
                    acc_s[rows, :] = acc_s[rows, :] + jnp.where(member, total, 0.0)
                    return carry

                lax.fori_loop(0, pieces[b], one_piece, 0)

        base_ref[:, here] = base_ref[:, here] * acc_s[...]


def prepare_kernel(lengths_ref, e_ref, pole_ref, coef_ref, table_ref, local_ref, reach_ref, turn_s, *, mine):
    count, packed, half = e_ref.shape
    modes = packed // 2
    halves = modes // SUB
    starts = starts_of(lengths_ref, lax.axis_index("seq") * count * BLK)
    flags = block_flags(starts, count)
    pitch = turn_s.shape[0] // BLK

    @pl.loop(0, half // LANE)
    def _(tile):
        here = lane_tile(tile)
        lanes = half_lanes(mine, half, tile * LANE, LANE)
        for h in range(halves):
            rows, rows_im = pl.ds(h * SUB, SUB), pl.ds(modes + h * SUB, SUB)
            p = pole_ref[rows, lanes], pole_ref[rows_im, lanes]
            q = coef_ref[rows, lanes], coef_ref[rows_im, lanes]
            for k in range(BLK):
                q = cmul(*q, *p)
                turn_s[pl.ds(k * pitch + h * SUB, SUB), :] = q[0]
                turn_s[pl.ds(k * pitch + modes + h * SUB, SUB), :] = -q[1]
            gate = p
            for _ in range(BLK.bit_length() - 1):
                gate = cmul(*gate, *gate)
            zero = jnp.zeros((SUB, LANE), F32)
            state, reach = (zero, zero), (zero + 1.0, zero)
            for b in range(count):
                local_ref[b, rows, here], local_ref[b, rows_im, here] = state
                reach_ref[b, rows, here], reach_ref[b, rows_im, here] = reach
                if b < count - 1:
                    state = advance(gate, flags[b], state, (e_ref[b, rows, here], e_ref[b, rows_im, here]))
                    reach = tuple(flags[b] * x for x in cmul(*gate, *reach))
        for m in range(packed):
            for r in range(BLK // SUB):
                table_ref[m, pl.ds(r * SUB, SUB), here] = turn_s[pl.ds(r * SUB * pitch + m, SUB, stride=pitch), :]


def split(ref, lanes, *lead):
    modes = ref.shape[-2] // 2
    packed = ref[(*lead, slice(None), lanes)].astype(F32)
    return packed[:modes], packed[modes:]


def store(ref, lanes, pair):
    modes = ref.shape[-2] // 2
    ref[0:modes, lanes] = pair[0].astype(ref.dtype)
    ref[modes : 2 * modes, lanes] = pair[1].astype(ref.dtype)


def advance(gate, flag, state, addend):
    re, im = cmul(*gate, *state)
    return addend[0] + flag * re, addend[1] + flag * im


def choose(flag, a, b):
    return tuple(jnp.where(flag, x, y) for x, y in zip(a, b))


def first_kernel(kept_ref, came_ref, pole_ref, flags_ref, total_ref, send_ref, gate_ref, *, tokens):
    half = kept_ref.shape[1]
    rows_at = flag_rows(1)
    shape = kept_ref.shape[0] // 2, CHUNK

    @pl.loop(0, half // CHUNK)
    def _(part):
        def flag(name):
            return jnp.broadcast_to(flags_ref[rows_at[name] : rows_at[name] + 1, :], shape)

        lanes = pl.ds(pl.multiple_of(part * CHUNK, LANE), CHUNK)
        kept, came = split(kept_ref, lanes), split(came_ref, lanes)
        gate = split(pole_ref, half_lanes(True, half, part * CHUNK, CHUNK))
        odd = flag("odd") > 0.5
        reach = 1
        while reach < tokens:
            gate = cmul(*gate, *gate)
            reach *= 2
        total = advance(gate, flag("second"), choose(odd, came, kept), choose(odd, kept, came))
        store(total_ref, lanes, total)
        store(send_ref, lanes, total)
        store(gate_ref, lanes, gate)


def round_kernel(total_ref, met_ref, flags_ref, *refs, k, rounds):
    rows_at = flag_rows(rounds)
    shape = met_ref.shape[0] // 2, CHUNK

    @pl.loop(0, met_ref.shape[1] // CHUNK)
    def _(part):
        def flag(name):
            return jnp.broadcast_to(flags_ref[rows_at[name] : rows_at[name] + 1, :], shape)

        lanes = pl.ds(pl.multiple_of(part * CHUNK, LANE), CHUNK)
        rest = list(refs)
        met, total = split(met_ref, lanes), split(total_ref, lanes)
        power = split(rest.pop(0), lanes)
        enter = flag(("enter", k))
        if k == 1:
            prefix = tuple(enter * x for x in met)
        else:
            before, prefix = split(rest.pop(0), lanes), split(rest.pop(0), lanes)
            prefix = advance(before, enter, met, prefix)
        if k < rounds - 1:
            total_out, send_ref, power_out, before_out, prefix_out = rest
            upper = flag(("upper", k)) > 0.5
            power = cmul(*power, *power)
            total = advance(power, flag(("whole", k)), choose(upper, met, total), choose(upper, total, met))
            store(total_out, lanes, total)
            store(send_ref, lanes, total)
            store(prefix_out, lanes, prefix)
            store(power_out, lanes, power)
            if k == 1:
                before = choose(upper, power, (jnp.ones_like(met[0]), jnp.zeros_like(met[0])))
            else:
                before = choose(upper, cmul(*before, *power), before)
            store(before_out, lanes, before)
        else:
            gate_ref, kept_ref, came_ref, own_ref, send_ref = rest
            odd = flag("odd") > 0.5
            kept, came = split(kept_ref, lanes), split(came_ref, lanes)
            beyond = advance(split(gate_ref, lanes), flag("even"), prefix, choose(odd, came, kept))
            store(own_ref, lanes, choose(odd, beyond, prefix))
            store(send_ref, lanes, choose(odd, prefix, beyond))


def back_kernel(entry_ref, table_ref, local_ref, reach_ref, base_ref, gain_ref, *refs, mine):
    out_hbm, out_ref, state_s, sems = refs[-4:]
    tokens, half = out_ref.shape
    width = TILE
    count, packed, _ = local_ref.shape
    modes = packed // 2
    halves = modes // SUB
    def one_tile(tile, state_s):
        lanes = here = lane_tile(tile)
        entry = entry_ref[:, here].astype(F32)
        for h in range(halves):
            rows, rows_im = pl.ds(h * SUB, SUB), pl.ds(modes + h * SUB, SUB)
            first = entry[h * SUB : (h + 1) * SUB], entry[modes + h * SUB : modes + (h + 1) * SUB]
            for b in range(count):
                state = first
                if b:
                    state = cmul(reach_ref[b, rows, here], reach_ref[b, rows_im, here], *first)
                    state = state[0] + local_ref[b, rows, here], state[1] + local_ref[b, rows_im, here]
                state_s[pl.ds(b * packed + h * SUB, SUB), :] = state[0]
                state_s[pl.ds(b * packed + modes + h * SUB, SUB), :] = state[1]
        sums = [[None] * (BLK // SUB) for _ in range(count)]
        for m in range(packed):
            turn = [table_ref[m, pl.ds(r * SUB, SUB), here] for r in range(BLK // SUB)]
            for b in range(count):
                state = state_s[pl.ds(b * packed + m, SUB, stride=0), :]
                for r in range(BLK // SUB):
                    term = turn[r] * state
                    sums[b][r] = term if m == 0 else sums[b][r] + term
        for b in range(count):
            rows = pl.ds(b * BLK, BLK)
            carried = jnp.concatenate(sums[b], axis=0)
            out_ref[rows, lanes] = (base_ref[rows, here] + gain_ref[rows, here] * carried).astype(BF16)

    def leaving(j):
        lanes = half_lanes(mine, half, j * width, width)
        here = pl.ds(pl.multiple_of(j * width, LANE), width)
        return pltpu.make_async_copy(out_ref.at[:, here], out_hbm.at[:, lanes], sems.at[j])

    @pl.loop(0, half // width)
    def _(j):
        @pl.loop(0, width // LANE // state_s.shape[0])
        def _(step):
            for v in range(state_s.shape[0]):
                one_tile(j * (width // LANE) + step * state_s.shape[0] + v, state_s.at[v])

        leaving(j).start()

    for j in range(half // width):
        leaving(j).wait()


def per_device(features, kernel, skip, residues, decay, freq, lengths):
    tokens = features.shape[1]
    modes, width = decay.shape
    half = width // 2
    count = tokens // BLK
    n = lax.axis_size("seq")
    place = lax.axis_index("seq")
    core = place % 2
    rounds = n.bit_length() - 1

    rim = features[:, tokens - 2 :, :]
    halo = lax.ppermute(rim, "seq", [(i, (i + 1) % n) for i in range(n)])

    fade = jnp.exp(-decay)
    q = freq * freq
    sine = freq * (1 + q * (-1 / 6 + q * (1 / 120 + q * (-1 / 5040 + q * (1 / 362880)))))
    cosine = 1 + q * (-1 / 2 + q * (1 / 24 + q * (-1 / 720 + q * (1 / 40320 - q * (1 / 3628800)))))
    d = 2 * decay
    scale = jnp.sqrt(d * (1 - d * (1 / 2 - d * (1 / 6 - d * (1 / 24 - d * (1 / 120 - d * (1 / 720)))))))
    part = lax.broadcasted_iota(jnp.int32, (2, modes, width), 0)
    pole = (fade * jnp.where(part == 0, cosine, sine)).reshape(2 * modes, width)
    coef = (residues * scale[None]).reshape(2 * modes, width)

    params = pltpu.CompilerParams(vmem_limit_bytes=16 * 1024 * 1024)
    roomy = pltpu.CompilerParams(vmem_limit_bytes=ROOM * 1024 * 1024)
    plane = pltpu.VMEM((tokens, LANE), F32)
    shifts = pltpu.VMEM((2 * tokens, tokens), BF16)
    whole = pl.BlockSpec(memory_space=pltpu.VMEM)

    def call(body, args, outs, name, scratch=(), cost=0.8e9, ragged=False, spec=whole, limit=params):
        return pl.pallas_call(
            body,
            grid_spec=pltpu.PrefetchScalarGridSpec(
                num_scalar_prefetch=int(ragged), grid=(), in_specs=[spec] * len(args), out_specs=[whole] * len(outs),
                scratch_shapes=scratch,
            ),
            out_shape=[jax.ShapeDtypeStruct(*o) for o in outs],
            compiler_params=limit, name=name,
            cost_estimate=pl.CostEstimate(flops=int(cost), bytes_accessed=1 << 20, transcendentals=0),
        )(*((lengths,) if ragged else ()), *args)

    packed = 2 * modes
    state, sent = ((packed, half), F32), ((packed, half), BF16)
    blocks, plain = ((count, packed, half), F32), ((tokens, half), F32)

    flag_count = -(-len(flag_rows(rounds)) // SUB) * SUB
    streams, shift, last_mask, flags = call(
        functools.partial(prelude_kernel, rounds=rounds), (features,),
        (((2, tokens, width), BF16), ((2 * tokens, tokens), BF16), ((tokens, LANE), F32), ((flag_count, CHUNK), F32)),
        "prelude", [pltpu.SemaphoreType.DMA((2,))], ragged=True, spec=pl.BlockSpec(memory_space=pl.ANY), limit=roomy,
        cost=1.2e9,
    )

    def front(mine):
        return call(
            functools.partial(front_kernel, mine=mine), (streams, halo, kernel, pole, shift, last_mask, flags),
            (((tokens, half), BF16), blocks, sent), "front", [pltpu.VMEM((TILE // LANE, tokens, LANE), F32)], cost=5e9,
        )

    def middle(mine, z):
        return call(
            functools.partial(middle_kernel, mine=mine), (features, halo, kernel, z, skip[None], pole, coef),
            (plain, plain), "middle", [plane, plane, plane, pltpu.VMEM((2 * BLK, LANE), F32), plane, shifts, pltpu.VMEM((BLK, LANE), F32)], cost=5e9, ragged=True,
        )

    def prepare(mine, e):
        return call(
            functools.partial(prepare_kernel, mine=mine), (e, pole, coef),
            (((packed, BLK, half), F32), blocks, blocks), "prepare", [pltpu.VMEM((BLK * PITCH, LANE), F32)], cost=2.5e9, ragged=True,
        )

    def back(mine, args, out):
        specs = [whole] * len(args)
        if out is not None:
            args, specs = args + (out,), specs + [pl.BlockSpec(memory_space=pl.ANY)]

        return pl.pallas_call(
            functools.partial(back_kernel, mine=mine),
            in_specs=specs, out_specs=pl.BlockSpec(memory_space=pl.ANY),
            out_shape=jax.ShapeDtypeStruct((tokens, width), BF16),
            scratch_shapes=[pltpu.VMEM((tokens, half), BF16), pltpu.VMEM((UNROLL, count * packed, LANE), F32),
                            pltpu.SemaphoreType.DMA((half // TILE,))],
            input_output_aliases={} if out is None else {len(args) - 1: 0},
            compiler_params=params, name="back",
            cost_estimate=pl.CostEstimate(flops=3_500_000_000, bytes_accessed=1 << 20, transcendentals=0),
        )(*args)

    z_other, e_other, end_other = front(False)
    came = exchange(end_other, 1)
    z_own, e_own, end_own = front(True)
    total, send, gate = call(
        functools.partial(first_kernel, tokens=tokens), (end_own, came, pole, flags), (state, sent, state), "first"
    )
    power, carry = gate, ()
    jobs = [lambda z: middle(True, z), lambda z: middle(False, z), lambda es: (*prepare(True, es[0]), *prepare(False, es[1]))]
    inputs = [z_own, z_other, (e_own, e_other)]
    ready = []
    for k in range(1, rounds):
        last = k == rounds - 1
        met = exchange(send, 1 << k)
        for job, operand in [(jobs.pop(0), inputs.pop(0)) for _ in range(len(jobs) if last else min(1, len(jobs)))]:
            operand, send = lax.optimization_barrier((operand, send))
            met, done = lax.optimization_barrier((met, job(operand)))
            ready.append(done)
        body = functools.partial(round_kernel, k=k, rounds=rounds)
        args = (total, met, flags, power, *carry)
        if last:
            own, send = call(body, args + (gate, end_own, came), (state, sent), "round")
        else:
            total, send, power, *carry = call(body, args, (state, sent, state, state, state), "round")
    other = exchange(send, 1)
    out = back(True, (own, *ready[2][:3], *ready[0]), None)
    return back(False, (other, *ready[2][3:], *ready[1]), out)


def solution(mesh):
    return jax.shard_map(
        per_device,
        mesh=mesh,
        in_specs=(P(None, ("groups", "seq"), None), P(), P(), P(), P(), P(), P("groups")),
        out_specs=P(("groups", "seq"), None),
        check_vma=False,
    )
```

```python
import functools

import jax
import jax.numpy as jnp
from jax import lax
from jax.experimental import pallas as pl
from jax.experimental.pallas import tpu as pltpu
from jax.sharding import PartitionSpec as P

BLK = 16
LANE = 128
SUB = 8
TILE = 512
PITCH = 40
ROOM = 50
PIECE = 256
CHUNK = 512
UNROLL = 2
F32 = jnp.float32
BF16 = jnp.bfloat16


def exchange(block, distance):
    devices = range(lax.axis_size("seq"))
    return lax.ppermute(block, "seq", [(i, i ^ distance) for i in devices])


def row_iota(rows):
    return lax.broadcasted_iota(jnp.int32, (rows, LANE), 0)


def starts_of(lengths_ref, origin):
    starts, at = [], -origin
    for i in range(lengths_ref.shape[0]):
        starts.append(at)
        at = at + lengths_ref[i]
    return starts


def none_in(starts, first, beyond):
    hit = jnp.int32(0)
    for s in starts:
        hit = hit | ((s >= first) & (s < beyond)).astype(jnp.int32)
    return (1 - hit).astype(F32)


def block_flags(starts, count):
    return [none_in(starts, b * BLK, (b + 1) * BLK) for b in range(count)]


def shift_matrix(starts, tokens):
    t = lax.broadcasted_iota(jnp.int32, (tokens, tokens), 0)
    u = lax.broadcasted_iota(jnp.int32, (tokens, tokens), 1)
    here = jnp.zeros((tokens, tokens), jnp.bool_)
    before = jnp.zeros((tokens, tokens), jnp.bool_)
    for s in starts:
        here = here | (t == s)
        before = before | (t - 1 == s)
    one = jnp.where((u == t - 1) & ~here, 1.0, 0.0)
    two = jnp.where((u == t - 2) & ~(here | before), 1.0, 0.0)
    return jnp.concatenate([one, two], axis=0).astype(BF16)


def edge_flags(starts):
    return none_in(starts, 0, 1), none_in(starts, -1, 1), none_in(starts, 0, 2)


def short_filter(rows, halo, taps, shift_ref, edges):
    tokens, width = rows.shape
    moved = jnp.dot(shift_ref[...], rows, preferred_element_type=F32)
    behind, further = moved[:tokens], moved[tokens:]
    edge = halo.astype(F32)
    far, near = edge[0:1, :], edge[1:2, :]
    row = lax.broadcasted_iota(jnp.int32, (SUB, width), 0)
    top = behind[:SUB] + jnp.where(row == 0, near * edges[0], 0.0)
    behind = jnp.concatenate([top, behind[SUB:]], axis=0)
    top = further[:SUB] + jnp.where(row == 0, far * edges[1], jnp.where(row == 1, near * edges[2], 0.0))
    further = jnp.concatenate([top, further[SUB:]], axis=0)
    return taps[0:1, :] * rows.astype(F32) + taps[1:2, :] * behind + taps[2:3, :] * further


def lane_tile(tile):
    return pl.ds(pl.multiple_of(tile * LANE, LANE), LANE)


def cmul(a_re, a_im, b_re, b_im):
    return a_re * b_re - a_im * b_im, a_re * b_im + a_im * b_re


def column_sums(parts):
    row = lax.broadcasted_iota(jnp.int32, (SUB, LANE), 0)
    low = row < 4
    level = []
    for b in range(4):
        keep = jnp.where(low, parts[b], parts[b + 4])
        move = jnp.where(low, parts[b + 4], parts[b])
        level.append(keep + pltpu.roll(move, 4, 0))
    for step in (2, 1):
        clear = (row & step) == 0
        level = [
            jnp.where(
                clear,
                level[b] + pltpu.roll(level[b], SUB - step, 0),
                level[b + step] + pltpu.roll(level[b + step], step, 0),
            )
            for b in range(step)
        ]
    return level[0]


def rows_of(ref, h, lanes):
    return ref[pl.ds(h * SUB, SUB), lanes]


def half_lanes(mine, half, offset, size):
    core = lax.axis_index("seq") & 1
    core = core if mine else 1 - core
    return pl.ds(pl.multiple_of(core * half + offset, LANE), size)


def flag_rows(rounds):
    names = ["odd", "second", "even", "edge0", "edge1", "edge2"] + [("tree", i) for i in range(16)]
    names += [(kind, k) for k in range(1, rounds) for kind in ("upper", "enter", "whole")]
    return {name: i for i, name in enumerate(names)}


def prelude_kernel(lengths_ref, features_ref, streams_ref, shift_ref, last_ref, flags_ref, sems, *, rounds):
    copies = [pltpu.make_async_copy(features_ref.at[r], streams_ref.at[u], sems.at[u]) for u, r in enumerate((0, 2))]
    for copy in copies:
        copy.start()
    tokens = streams_ref.shape[1]
    place = lax.axis_index("seq")
    starts = starts_of(lengths_ref, place * tokens)
    t = row_iota(tokens)
    last = jnp.full((tokens, LANE), -1, jnp.int32)
    for s in starts:
        last = jnp.maximum(last, jnp.where(s <= (t | (BLK - 1)), s, -1))
    last_ref[...] = jnp.where(t >= last, 1.0, 0.0)
    shift_ref[...] = shift_matrix(starts, tokens)
    values = dict(zip(("edge0", "edge1", "edge2"), edge_flags(starts)))
    span, i = BLK, 0
    while span < tokens:
        for first in range(span, tokens, 2 * span):
            values["tree", i] = none_in(starts, first, first + span)
            i += 1
        span *= 2
    starts = starts_of(lengths_ref, 0)
    even, second = place & -2, place | 1
    values["odd"] = (place & 1).astype(F32)
    values["even"] = none_in(starts, even * tokens, (even + 1) * tokens)
    values["second"] = none_in(starts, second * tokens, (second + 1) * tokens)
    for k in range(1, rounds):
        distance = 1 << k
        upper = ((place >> k) & 1).astype(F32)
        group = (place >> k) << k
        later = group | distance
        values["upper", k] = upper
        values["enter", k] = upper * none_in(starts, group * tokens, even * tokens)
        values["whole", k] = none_in(starts, later * tokens, (later + distance) * tokens)
    for name, row in flag_rows(rounds).items():
        if name in values:
            flags_ref[row : row + 1, :] = jnp.full((1, CHUNK), values[name], F32)
    for copy in copies:
        copy.wait()


def tables_kernel(decay_ref, freq_ref, residues_ref, pole_ref, coef_ref):
    modes, width = decay_ref.shape

    @pl.loop(0, width // CHUNK)
    def _(part):
        lanes = pl.ds(pl.multiple_of(part * CHUNK, LANE), CHUNK)
        decay, x = decay_ref[:, lanes], freq_ref[:, lanes]
        fade = jnp.exp(-decay)
        q = x * x
        sine = x * (1 + q * (-1 / 6 + q * (1 / 120 + q * (-1 / 5040 + q * (1 / 362880)))))
        cosine = 1 + q * (-1 / 2 + q * (1 / 24 + q * (-1 / 720 + q * (1 / 40320 - q * (1 / 3628800)))))
        store(pole_ref, lanes, (fade * cosine, fade * sine))
        d = 2 * decay
        scale = jnp.sqrt(d * (1 - d * (1 / 2 - d * (1 / 6 - d * (1 / 24 - d * (1 / 120 - d * (1 / 720)))))))
        store(coef_ref, lanes, (residues_ref[0, :, lanes] * scale, residues_ref[1, :, lanes] * scale))


def front_kernel(streams_ref, halo_ref, taps_ref, pole_ref, shift_s, last_s, flags_ref, z_ref, e_ref, end_ref, z_s, *, mine):
    tokens, half = z_ref.shape
    count = tokens // BLK
    modes = pole_ref.shape[0] // 2
    halves = modes // SUB
    wide = TILE
    rows_at = flag_rows(1)

    def flag(name, size):
        return flags_ref[rows_at[name] : rows_at[name] + 1, 0:size]

    edges = [flag(name, PIECE) for name in ("edge0", "edge1", "edge2")]

    @pl.loop(0, half // wide)
    def _(j):
        def gated(i, size):
            at = pl.ds(pl.multiple_of(j * wide + i * LANE, LANE), size)
            lanes = half_lanes(mine, half, j * wide + i * LANE, size)
            conv0, conv2 = (
                short_filter(streams_ref[u, :, lanes], halo_ref[r, :, lanes], taps_ref[r, :, lanes], shift_s, edges)
                for u, r in enumerate((0, 2))
            )
            z = (conv0 * conv2).astype(BF16)
            z_ref[:, at] = z
            for v in range(size // LANE):
                z_s[i + v] = z[:, v * LANE : (v + 1) * LANE].astype(F32) * last_s[...]

        def states(i):
            at = pl.ds(pl.multiple_of(j * wide + i * LANE, LANE), LANE)
            lanes = half_lanes(mine, half, j * wide + i * LANE, LANE)
            z_i = z_s.at[i]
            p_re = [rows_of(pole_ref, h, lanes) for h in range(halves)]
            p_im = [rows_of(pole_ref, halves + h, lanes) for h in range(halves)]
            pow_re, pow_im = list(p_re), list(p_im)
            e_re, e_im = [], []
            for b in range(count):
                now = z_i[pl.ds(b * BLK + BLK - 1, SUB, stride=0), :]
                prev = z_i[pl.ds(b * BLK + BLK - 2, SUB, stride=0), :]
                e_re.append([now + p_re[h] * prev for h in range(halves)])
                e_im.append([p_im[h] * prev for h in range(halves)])
            for k in range(2, BLK):
                for h in range(halves):
                    pow_re[h], pow_im[h] = cmul(pow_re[h], pow_im[h], p_re[h], p_im[h])
                for b in range(count):
                    now = z_i[pl.ds(b * BLK + BLK - 1 - k, SUB, stride=0), :]
                    for h in range(halves):
                        e_re[b][h] = e_re[b][h] + pow_re[h] * now
                        e_im[b][h] = e_im[b][h] + pow_im[h] * now
            for h in range(halves):
                rows, rows_im = pl.ds(h * SUB, SUB), pl.ds(modes + h * SUB, SUB)
                for b in range(count):
                    e_ref[b, rows, at] = e_re[b][h]
                    e_ref[b, rows_im, at] = e_im[b][h]
                gate = cmul(pow_re[h], pow_im[h], p_re[h], p_im[h])
                level = [(e_re[b][h], e_im[b][h]) for b in range(count)]
                step = 0
                while len(level) > 1:
                    pairs = range(0, len(level), 2)
                    level = [
                        advance(gate, flag(("tree", step + i // 2), LANE), level[i], level[i + 1]) for i in pairs
                    ]
                    step += len(pairs)
                    gate = cmul(*gate, *gate)
                end_ref[rows, at] = level[0][0].astype(BF16)
                end_ref[rows_im, at] = level[0][1].astype(BF16)

        lane_tiles = wide // LANE
        gated(0, PIECE)
        for i in range(lane_tiles):
            following = (i // (PIECE // LANE) + 1) * (PIECE // LANE)
            if i % (PIECE // LANE) == 0 and following < lane_tiles:
                gated(following, PIECE)
            states(i)


def middle_kernel(lengths_ref, features_ref, halo_ref, taps_ref, z_ref, skip_ref, pole_ref,
                  coef_ref, base_ref, gain_ref, first_s, part_s, z_s, filt_s, acc_s, shift_s, piece_s, *, mine):
    tokens, half = z_ref.shape
    count = tokens // BLK
    modes = pole_ref.shape[0] // 2
    halves = modes // SUB
    starts = starts_of(lengths_ref, lax.axis_index("seq") * tokens)
    edges = edge_flags(starts)
    t = row_iota(tokens)
    t0 = t & (-BLK)
    piece = jnp.zeros((tokens, LANE), jnp.int32)
    opened = jnp.zeros((tokens, LANE), jnp.bool_)
    for s in starts:
        piece = piece + jnp.where((s > t0) & (s <= t), 1, 0)
        opened = opened | ((s >= t0) & (s <= t))
    part_s[...] = piece.astype(F32)
    first_s[...] = jnp.where(opened, 0.0, 1.0)
    shift_s[...] = shift_matrix(starts, tokens)

    pieces = []
    for b in range(count):
        inside = jnp.int32(1)
        for s in starts:
            inside = inside + ((s > b * BLK) & (s < (b + 1) * BLK)).astype(jnp.int32)
        pieces.append(inside)
    wide = TILE

    @pl.loop(0, half // wide)
    def _(part):
        here = pl.ds(pl.multiple_of(part * wide, LANE), wide)
        lanes = half_lanes(mine, half, part * wide, wide)
        conv1 = short_filter(features_ref[1, :, lanes], halo_ref[1, :, lanes], taps_ref[1, :, lanes], shift_s, edges)
        base_ref[:, here] = conv1
        for i in range(wide // LANE):
            inner = pl.ds(pl.multiple_of(part * wide + i * LANE, LANE), LANE)
            gain_ref[:, inner] = conv1[:, i * LANE : (i + 1) * LANE] * first_s[...]

    @pl.loop(0, half // LANE)
    def _(tile):
        here = lane_tile(tile)
        lanes = half_lanes(mine, half, tile * LANE, LANE)
        p_re = [rows_of(pole_ref, h, lanes) for h in range(halves)]
        p_im = [rows_of(pole_ref, halves + h, lanes) for h in range(halves)]
        q_re = [rows_of(coef_ref, h, lanes) for h in range(halves)]
        q_im = [rows_of(coef_ref, halves + h, lanes) for h in range(halves)]
        filt_s[pl.ds(0, BLK), :] = jnp.zeros((BLK, LANE), F32)
        for group in range(BLK // SUB):
            parts = []
            for k in range(SUB):
                parts.append(sum(q_re[1:], q_re[0]))
                for h in range(halves):
                    q_re[h], q_im[h] = cmul(q_re[h], q_im[h], p_re[h], p_im[h])
            filt_s[pl.ds(BLK + group * SUB, SUB), :] = column_sums(parts).astype(BF16).astype(F32)
        z = z_ref[:, here].astype(F32)
        z_s[...] = z
        acc = skip_ref[:, lanes] * z
        sums = [[acc[b * BLK + r * SUB : b * BLK + (r + 1) * SUB] for r in range(BLK // SUB)] for b in range(count)]
        for s in range(BLK):
            firsts = range(s // SUB, BLK // SUB)
            columns = {r: filt_s[pl.ds(BLK - s + r * SUB, SUB), :] for r in firsts}
            for b in range(count):
                value = z_s[pl.ds(b * BLK + s, SUB, stride=0), :]
                for r in firsts:
                    sums[b][r] = sums[b][r] + columns[r] * value
        for b in range(count):
            for r in range(BLK // SUB):
                acc_s[pl.ds(b * BLK + r * SUB, SUB), :] = sums[b][r]

        for b in range(count):
            @pl.when(pieces[b] > 1)
            def _(b=b):
                rows = pl.ds(b * BLK, BLK)
                acc_s[rows, :] = skip_ref[:, lanes] * z_s[rows, :]

                def one_piece(q, carry):
                    member = part_s[rows, :] == q.astype(F32)
                    piece_s[...] = jnp.where(member, z_s[rows, :], 0.0)
                    total = jnp.zeros((BLK, LANE), F32)
                    for s in range(BLK):
                        total = total + filt_s[pl.ds(BLK - s, BLK), :] * piece_s[pl.ds(s, 1), :]
                    acc_s[rows, :] = acc_s[rows, :] + jnp.where(member, total, 0.0)
                    return carry

                lax.fori_loop(0, pieces[b], one_piece, 0)

        base_ref[:, here] = base_ref[:, here] * acc_s[...]


def prepare_kernel(lengths_ref, e_ref, pole_ref, coef_ref, table_ref, local_ref, reach_ref, turn_s, *, mine):
    count, packed, half = e_ref.shape
    modes = packed // 2
    halves = modes // SUB
    starts = starts_of(lengths_ref, lax.axis_index("seq") * count * BLK)
    flags = block_flags(starts, count)
    pitch = turn_s.shape[0] // BLK

    @pl.loop(0, half // LANE)
    def _(tile):
        here = lane_tile(tile)
        lanes = half_lanes(mine, half, tile * LANE, LANE)
        for h in range(halves):
            rows, rows_im = pl.ds(h * SUB, SUB), pl.ds(modes + h * SUB, SUB)
            p = pole_ref[rows, lanes], pole_ref[rows_im, lanes]
            q = coef_ref[rows, lanes], coef_ref[rows_im, lanes]
            for k in range(BLK):
                q = cmul(*q, *p)
                turn_s[pl.ds(k * pitch + h * SUB, SUB), :] = q[0]
                turn_s[pl.ds(k * pitch + modes + h * SUB, SUB), :] = -q[1]
            gate = p
            for _ in range(BLK.bit_length() - 1):
                gate = cmul(*gate, *gate)
            zero = jnp.zeros((SUB, LANE), F32)
            state, reach = (zero, zero), (zero + 1.0, zero)
            for b in range(count):
                local_ref[b, rows, here], local_ref[b, rows_im, here] = state
                reach_ref[b, rows, here], reach_ref[b, rows_im, here] = reach
                if b < count - 1:
                    state = advance(gate, flags[b], state, (e_ref[b, rows, here], e_ref[b, rows_im, here]))
                    reach = tuple(flags[b] * x for x in cmul(*gate, *reach))
        for m in range(packed):
            for r in range(BLK // SUB):
                table_ref[m, pl.ds(r * SUB, SUB), here] = turn_s[pl.ds(r * SUB * pitch + m, SUB, stride=pitch), :]


def split(ref, lanes, *lead):
    modes = ref.shape[-2] // 2
    packed = ref[(*lead, slice(None), lanes)].astype(F32)
    return packed[:modes], packed[modes:]


def store(ref, lanes, pair):
    modes = ref.shape[-2] // 2
    ref[0:modes, lanes] = pair[0].astype(ref.dtype)
    ref[modes : 2 * modes, lanes] = pair[1].astype(ref.dtype)


def advance(gate, flag, state, addend):
    re, im = cmul(*gate, *state)
    return addend[0] + flag * re, addend[1] + flag * im


def choose(flag, a, b):
    return tuple(jnp.where(flag, x, y) for x, y in zip(a, b))


def first_kernel(kept_ref, came_ref, pole_ref, flags_ref, total_ref, send_ref, gate_ref, *, tokens):
    half = kept_ref.shape[1]
    rows_at = flag_rows(1)
    shape = kept_ref.shape[0] // 2, CHUNK

    @pl.loop(0, half // CHUNK)
    def _(part):
        def flag(name):
            return jnp.broadcast_to(flags_ref[rows_at[name] : rows_at[name] + 1, :], shape)

        lanes = pl.ds(pl.multiple_of(part * CHUNK, LANE), CHUNK)
        kept, came = split(kept_ref, lanes), split(came_ref, lanes)
        gate = split(pole_ref, half_lanes(True, half, part * CHUNK, CHUNK))
        odd = flag("odd") > 0.5
        reach = 1
        while reach < tokens:
            gate = cmul(*gate, *gate)
            reach *= 2
        total = advance(gate, flag("second"), choose(odd, came, kept), choose(odd, kept, came))
        store(total_ref, lanes, total)
        store(send_ref, lanes, total)
        store(gate_ref, lanes, gate)


def round_kernel(total_ref, met_ref, flags_ref, *refs, k, rounds):
    rows_at = flag_rows(rounds)
    shape = met_ref.shape[0] // 2, CHUNK

    @pl.loop(0, met_ref.shape[1] // CHUNK)
    def _(part):
        def flag(name):
            return jnp.broadcast_to(flags_ref[rows_at[name] : rows_at[name] + 1, :], shape)

        lanes = pl.ds(pl.multiple_of(part * CHUNK, LANE), CHUNK)
        rest = list(refs)
        met, total = split(met_ref, lanes), split(total_ref, lanes)
        power = split(rest.pop(0), lanes)
        enter = flag(("enter", k))
        if k == 1:
            prefix = tuple(enter * x for x in met)
        else:
            before, prefix = split(rest.pop(0), lanes), split(rest.pop(0), lanes)
            prefix = advance(before, enter, met, prefix)
        if k < rounds - 1:
            total_out, send_ref, power_out, before_out, prefix_out = rest
            upper = flag(("upper", k)) > 0.5
            power = cmul(*power, *power)
            total = advance(power, flag(("whole", k)), choose(upper, met, total), choose(upper, total, met))
            store(total_out, lanes, total)
            store(send_ref, lanes, total)
            store(prefix_out, lanes, prefix)
            store(power_out, lanes, power)
            if k == 1:
                before = choose(upper, power, (jnp.ones_like(met[0]), jnp.zeros_like(met[0])))
            else:
                before = choose(upper, cmul(*before, *power), before)
            store(before_out, lanes, before)
        else:
            gate_ref, kept_ref, came_ref, own_ref, send_ref = rest
            odd = flag("odd") > 0.5
            kept, came = split(kept_ref, lanes), split(came_ref, lanes)
            beyond = advance(split(gate_ref, lanes), flag("even"), prefix, choose(odd, came, kept))
            store(own_ref, lanes, choose(odd, beyond, prefix))
            store(send_ref, lanes, choose(odd, prefix, beyond))


def back_kernel(entry_ref, table_ref, local_ref, reach_ref, base_ref, gain_ref, *refs, mine):
    out_hbm, out_ref, state_s, sems = refs[-4:]
    tokens, half = out_ref.shape
    width = TILE
    count, packed, _ = local_ref.shape
    modes = packed // 2
    halves = modes // SUB
    def one_tile(tile, state_s):
        lanes = here = lane_tile(tile)
        entry = entry_ref[:, here].astype(F32)
        for h in range(halves):
            rows, rows_im = pl.ds(h * SUB, SUB), pl.ds(modes + h * SUB, SUB)
            first = entry[h * SUB : (h + 1) * SUB], entry[modes + h * SUB : modes + (h + 1) * SUB]
            for b in range(count):
                state = first
                if b:
                    state = cmul(reach_ref[b, rows, here], reach_ref[b, rows_im, here], *first)
                    state = state[0] + local_ref[b, rows, here], state[1] + local_ref[b, rows_im, here]
                state_s[pl.ds(b * packed + h * SUB, SUB), :] = state[0]
                state_s[pl.ds(b * packed + modes + h * SUB, SUB), :] = state[1]
        sums = [[None] * (BLK // SUB) for _ in range(count)]
        for m in range(packed):
            turn = [table_ref[m, pl.ds(r * SUB, SUB), here] for r in range(BLK // SUB)]
            for b in range(count):
                state = state_s[pl.ds(b * packed + m, SUB, stride=0), :]
                for r in range(BLK // SUB):
                    term = turn[r] * state
                    sums[b][r] = term if m == 0 else sums[b][r] + term
        for b in range(count):
            rows = pl.ds(b * BLK, BLK)
            carried = jnp.concatenate(sums[b], axis=0)
            out_ref[rows, lanes] = (base_ref[rows, here] + gain_ref[rows, here] * carried).astype(BF16)

    def leaving(j):
        lanes = half_lanes(mine, half, j * width, width)
        here = pl.ds(pl.multiple_of(j * width, LANE), width)
        return pltpu.make_async_copy(out_ref.at[:, here], out_hbm.at[:, lanes], sems.at[j])

    @pl.loop(0, half // width)
    def _(j):
        @pl.loop(0, width // LANE // state_s.shape[0])
        def _(step):
            for v in range(state_s.shape[0]):
                one_tile(j * (width // LANE) + step * state_s.shape[0] + v, state_s.at[v])

        leaving(j).start()

    for j in range(half // width):
        leaving(j).wait()


def per_device(features, kernel, skip, residues, decay, freq, lengths):
    tokens = features.shape[1]
    modes, width = decay.shape
    half = width // 2
    count = tokens // BLK
    n = lax.axis_size("seq")
    place = lax.axis_index("seq")
    core = place % 2
    rounds = n.bit_length() - 1

    rim = features[:, tokens - 2 :, :]
    halo = lax.ppermute(rim, "seq", [(i, (i + 1) % n) for i in range(n)])

    params = pltpu.CompilerParams(vmem_limit_bytes=16 * 1024 * 1024)
    roomy = pltpu.CompilerParams(vmem_limit_bytes=ROOM * 1024 * 1024)
    plane = pltpu.VMEM((tokens, LANE), F32)
    shifts = pltpu.VMEM((2 * tokens, tokens), BF16)
    whole = pl.BlockSpec(memory_space=pltpu.VMEM)

    def call(body, args, outs, name, scratch=(), cost=0.8e9, ragged=False, spec=whole, limit=params):
        return pl.pallas_call(
            body,
            grid_spec=pltpu.PrefetchScalarGridSpec(
                num_scalar_prefetch=int(ragged), grid=(), in_specs=[spec] * len(args), out_specs=[whole] * len(outs),
                scratch_shapes=scratch,
            ),
            out_shape=[jax.ShapeDtypeStruct(*o) for o in outs],
            compiler_params=limit, name=name,
            cost_estimate=pl.CostEstimate(flops=int(cost), bytes_accessed=1 << 20, transcendentals=0),
        )(*((lengths,) if ragged else ()), *args)

    packed = 2 * modes
    state, sent = ((packed, half), F32), ((packed, half), BF16)
    blocks, plain = ((count, packed, half), F32), ((tokens, half), F32)

    flag_count = -(-len(flag_rows(rounds)) // SUB) * SUB
    streams, shift, last_mask, flags = call(
        functools.partial(prelude_kernel, rounds=rounds), (features,),
        (((2, tokens, width), BF16), ((2 * tokens, tokens), BF16), ((tokens, LANE), F32), ((flag_count, CHUNK), F32)),
        "prelude", [pltpu.SemaphoreType.DMA((2,))], ragged=True, spec=pl.BlockSpec(memory_space=pl.ANY), limit=roomy,
        cost=1.2e9,
    )

    table = ((packed, width), F32)
    pole, coef = call(tables_kernel, (decay, freq, residues), (table, table), "tables", cost=0.5e9)

    def front(mine):
        return call(
            functools.partial(front_kernel, mine=mine), (streams, halo, kernel, pole, shift, last_mask, flags),
            (((tokens, half), BF16), blocks, sent), "front", [pltpu.VMEM((TILE // LANE, tokens, LANE), F32)], cost=5e9,
        )

    def middle(mine, z):
        return call(
            functools.partial(middle_kernel, mine=mine), (features, halo, kernel, z, skip[None], pole, coef),
            (plain, plain), "middle", [plane, plane, plane, pltpu.VMEM((2 * BLK, LANE), F32), plane, shifts, pltpu.VMEM((BLK, LANE), F32)], cost=5e9, ragged=True,
        )

    def prepare(mine, e):
        return call(
            functools.partial(prepare_kernel, mine=mine), (e, pole, coef),
            (((packed, BLK, half), F32), blocks, blocks), "prepare", [pltpu.VMEM((BLK * PITCH, LANE), F32)], cost=2.5e9, ragged=True,
        )

    def back(mine, args, out):
        specs = [whole] * len(args)
        if out is not None:
            args, specs = args + (out,), specs + [pl.BlockSpec(memory_space=pl.ANY)]

        return pl.pallas_call(
            functools.partial(back_kernel, mine=mine),
            in_specs=specs, out_specs=pl.BlockSpec(memory_space=pl.ANY),
            out_shape=jax.ShapeDtypeStruct((tokens, width), BF16),
            scratch_shapes=[pltpu.VMEM((tokens, half), BF16), pltpu.VMEM((UNROLL, count * packed, LANE), F32),
                            pltpu.SemaphoreType.DMA((half // TILE,))],
            input_output_aliases={} if out is None else {len(args) - 1: 0},
            compiler_params=params, name="back",
            cost_estimate=pl.CostEstimate(flops=3_500_000_000, bytes_accessed=1 << 20, transcendentals=0),
        )(*args)

    z_other, e_other, end_other = front(False)
    came = exchange(end_other, 1)
    z_own, e_own, end_own = front(True)
    total, send, gate = call(
        functools.partial(first_kernel, tokens=tokens), (end_own, came, pole, flags), (state, sent, state), "first"
    )
    power, carry = gate, ()
    jobs = [lambda z: middle(True, z), lambda z: middle(False, z), lambda es: (*prepare(True, es[0]), *prepare(False, es[1]))]
    inputs = [z_own, z_other, (e_own, e_other)]
    ready = []
    for k in range(1, rounds):
        last = k == rounds - 1
        met = exchange(send, 1 << k)
        for job, operand in [(jobs.pop(0), inputs.pop(0)) for _ in range(len(jobs) if last else min(1, len(jobs)))]:
            operand, send = lax.optimization_barrier((operand, send))
            met, done = lax.optimization_barrier((met, job(operand)))
            ready.append(done)
        body = functools.partial(round_kernel, k=k, rounds=rounds)
        args = (total, met, flags, power, *carry)
        if last:
            own, send = call(body, args + (gate, end_own, came), (state, sent), "round")
        else:
            total, send, power, *carry = call(body, args, (state, sent, state, state, state), "round")
    other = exchange(send, 1)
    out = back(True, (own, *ready[2][:3], *ready[0]), None)
    return back(False, (other, *ready[2][3:], *ready[1]), out)


def solution(mesh):
    return jax.shard_map(
        per_device,
        mesh=mesh,
        in_specs=(P(None, ("groups", "seq"), None), P(), P(), P(), P(), P(), P("groups")),
        out_specs=P(("groups", "seq"), None),
        check_vma=False,
    )
```

```python
import functools

import jax
import jax.numpy as jnp
from jax import lax
from jax.experimental import pallas as pl
from jax.experimental.pallas import tpu as pltpu
from jax.sharding import PartitionSpec as P

BLK = 16
LANE = 128
SUB = 8
TILE = 512
PITCH = 40
ROOM = 50
PIECE = 256
CHUNK = 512
UNROLL = 2
F32 = jnp.float32
BF16 = jnp.bfloat16


def exchange(block, distance):
    devices = range(lax.axis_size("seq"))
    return lax.ppermute(block, "seq", [(i, i ^ distance) for i in devices])


def row_iota(rows):
    return lax.broadcasted_iota(jnp.int32, (rows, LANE), 0)


def starts_of(lengths_ref, origin):
    starts, at = [], -origin
    for i in range(lengths_ref.shape[0]):
        starts.append(at)
        at = at + lengths_ref[i]
    return starts


def none_in(starts, first, beyond):
    hit = jnp.int32(0)
    for s in starts:
        hit = hit | ((s >= first) & (s < beyond)).astype(jnp.int32)
    return (1 - hit).astype(F32)


def block_flags(starts, count):
    return [none_in(starts, b * BLK, (b + 1) * BLK) for b in range(count)]


def shift_matrix(starts, tokens):
    t = lax.broadcasted_iota(jnp.int32, (tokens, tokens), 0)
    u = lax.broadcasted_iota(jnp.int32, (tokens, tokens), 1)
    here = jnp.zeros((tokens, tokens), jnp.bool_)
    before = jnp.zeros((tokens, tokens), jnp.bool_)
    for s in starts:
        here = here | (t == s)
        before = before | (t - 1 == s)
    one = jnp.where((u == t - 1) & ~here, 1.0, 0.0)
    two = jnp.where((u == t - 2) & ~(here | before), 1.0, 0.0)
    return jnp.concatenate([one, two], axis=0).astype(BF16)


def edge_flags(starts):
    return none_in(starts, 0, 1), none_in(starts, -1, 1), none_in(starts, 0, 2)


def short_filter(rows, halo, taps, shift_ref, edges):
    tokens, width = rows.shape
    moved = jnp.dot(shift_ref[...], rows, preferred_element_type=F32)
    behind, further = moved[:tokens], moved[tokens:]
    edge = halo.astype(F32)
    far, near = edge[0:1, :], edge[1:2, :]
    row = lax.broadcasted_iota(jnp.int32, (SUB, width), 0)
    top = behind[:SUB] + jnp.where(row == 0, near * edges[0], 0.0)
    behind = jnp.concatenate([top, behind[SUB:]], axis=0)
    top = further[:SUB] + jnp.where(row == 0, far * edges[1], jnp.where(row == 1, near * edges[2], 0.0))
    further = jnp.concatenate([top, further[SUB:]], axis=0)
    return taps[0:1, :] * rows.astype(F32) + taps[1:2, :] * behind + taps[2:3, :] * further


def lane_tile(tile):
    return pl.ds(pl.multiple_of(tile * LANE, LANE), LANE)


def cmul(a_re, a_im, b_re, b_im):
    return a_re * b_re - a_im * b_im, a_re * b_im + a_im * b_re


def column_sums(parts):
    row = lax.broadcasted_iota(jnp.int32, (SUB, LANE), 0)
    low = row < 4
    level = []
    for b in range(4):
        keep = jnp.where(low, parts[b], parts[b + 4])
        move = jnp.where(low, parts[b + 4], parts[b])
        level.append(keep + pltpu.roll(move, 4, 0))
    for step in (2, 1):
        clear = (row & step) == 0
        level = [
            jnp.where(
                clear,
                level[b] + pltpu.roll(level[b], SUB - step, 0),
                level[b + step] + pltpu.roll(level[b + step], step, 0),
            )
            for b in range(step)
        ]
    return level[0]


def rows_of(ref, h, lanes):
    return ref[pl.ds(h * SUB, SUB), lanes]


def half_lanes(mine, half, offset, size):
    core = lax.axis_index("seq") & 1
    core = core if mine else 1 - core
    return pl.ds(pl.multiple_of(core * half + offset, LANE), size)


def flag_rows(rounds):
    names = ["odd", "second", "even", "edge0", "edge1", "edge2"] + [("tree", i) for i in range(16)]
    names += [(kind, k) for k in range(1, rounds) for kind in ("upper", "enter", "whole")]
    return {name: i for i, name in enumerate(names)}


def prelude_kernel(lengths_ref, features_ref, streams_ref, shift_ref, last_ref, flags_ref, sems, *, rounds):
    size = streams_ref.shape[1] // sems.shape[1]
    copies = [
        pltpu.make_async_copy(
            features_ref.at[r, pl.ds(j * size, size), :], streams_ref.at[u, pl.ds(j * size, size), :], sems.at[u, j]
        )
        for u, r in enumerate((0, 2))
        for j in range(sems.shape[1])
    ]
    for copy in copies:
        copy.start()
    tokens = streams_ref.shape[1]
    place = lax.axis_index("seq")
    starts = starts_of(lengths_ref, place * tokens)
    t = row_iota(tokens)
    last = jnp.full((tokens, LANE), -1, jnp.int32)
    for s in starts:
        last = jnp.maximum(last, jnp.where(s <= (t | (BLK - 1)), s, -1))
    last_ref[...] = jnp.where(t >= last, 1.0, 0.0)
    shift_ref[...] = shift_matrix(starts, tokens)
    values = dict(zip(("edge0", "edge1", "edge2"), edge_flags(starts)))
    span, i = BLK, 0
    while span < tokens:
        for first in range(span, tokens, 2 * span):
            values["tree", i] = none_in(starts, first, first + span)
            i += 1
        span *= 2
    starts = starts_of(lengths_ref, 0)
    even, second = place & -2, place | 1
    values["odd"] = (place & 1).astype(F32)
    values["even"] = none_in(starts, even * tokens, (even + 1) * tokens)
    values["second"] = none_in(starts, second * tokens, (second + 1) * tokens)
    for k in range(1, rounds):
        distance = 1 << k
        upper = ((place >> k) & 1).astype(F32)
        group = (place >> k) << k
        later = group | distance
        values["upper", k] = upper
        values["enter", k] = upper * none_in(starts, group * tokens, even * tokens)
        values["whole", k] = none_in(starts, later * tokens, (later + distance) * tokens)
    for name, row in flag_rows(rounds).items():
        if name in values:
            flags_ref[row : row + 1, :] = jnp.full((1, CHUNK), values[name], F32)
    for copy in copies:
        copy.wait()


def tables_kernel(decay_ref, freq_ref, residues_ref, pole_ref, coef_ref):
    modes, width = decay_ref.shape

    @pl.loop(0, width // CHUNK)
    def _(part):
        lanes = pl.ds(pl.multiple_of(part * CHUNK, LANE), CHUNK)
        decay, x = decay_ref[:, lanes], freq_ref[:, lanes]
        fade = jnp.exp(-decay)
        q = x * x
        sine = x * (1 + q * (-1 / 6 + q * (1 / 120 + q * (-1 / 5040 + q * (1 / 362880)))))
        cosine = 1 + q * (-1 / 2 + q * (1 / 24 + q * (-1 / 720 + q * (1 / 40320 - q * (1 / 3628800)))))
        store(pole_ref, lanes, (fade * cosine, fade * sine))
        d = 2 * decay
        scale = jnp.sqrt(d * (1 - d * (1 / 2 - d * (1 / 6 - d * (1 / 24 - d * (1 / 120 - d * (1 / 720)))))))
        store(coef_ref, lanes, (residues_ref[0, :, lanes] * scale, residues_ref[1, :, lanes] * scale))


def front_kernel(streams_ref, halo_ref, taps_ref, pole_ref, shift_s, last_s, flags_ref, z_ref, e_ref, end_ref, z_s, *, mine):
    tokens, half = z_ref.shape
    count = tokens // BLK
    modes = pole_ref.shape[0] // 2
    halves = modes // SUB
    wide = TILE
    rows_at = flag_rows(1)

    def flag(name, size):
        return flags_ref[rows_at[name] : rows_at[name] + 1, 0:size]

    edges = [flag(name, PIECE) for name in ("edge0", "edge1", "edge2")]

    @pl.loop(0, half // wide)
    def _(j):
        def gated(i, size):
            at = pl.ds(pl.multiple_of(j * wide + i * LANE, LANE), size)
            lanes = half_lanes(mine, half, j * wide + i * LANE, size)
            conv0, conv2 = (
                short_filter(streams_ref[u, :, lanes], halo_ref[r, :, lanes], taps_ref[r, :, lanes], shift_s, edges)
                for u, r in enumerate((0, 2))
            )
            z = (conv0 * conv2).astype(BF16)
            z_ref[:, at] = z
            for v in range(size // LANE):
                z_s[i + v, 0:tokens, :] = z[:, v * LANE : (v + 1) * LANE].astype(F32) * last_s[...]

        def states(i):
            at = pl.ds(pl.multiple_of(j * wide + i * LANE, LANE), LANE)
            lanes = half_lanes(mine, half, j * wide + i * LANE, LANE)
            z_i = z_s.at[i]
            p_re = [rows_of(pole_ref, h, lanes) for h in range(halves)]
            p_im = [rows_of(pole_ref, halves + h, lanes) for h in range(halves)]
            pow_re, pow_im = list(p_re), list(p_im)
            e_re, e_im = [], []
            for b in range(count):
                now = z_i[pl.ds(b * BLK + BLK - 1, SUB, stride=0), :]
                prev = z_i[pl.ds(b * BLK + BLK - 2, SUB, stride=0), :]
                e_re.append([now + p_re[h] * prev for h in range(halves)])
                e_im.append([p_im[h] * prev for h in range(halves)])
            for k in range(2, BLK):
                for h in range(halves):
                    pow_re[h], pow_im[h] = cmul(pow_re[h], pow_im[h], p_re[h], p_im[h])
                for b in range(count):
                    now = z_i[pl.ds(b * BLK + BLK - 1 - k, SUB, stride=0), :]
                    for h in range(halves):
                        e_re[b][h] = e_re[b][h] + pow_re[h] * now
                        e_im[b][h] = e_im[b][h] + pow_im[h] * now
            for h in range(halves):
                rows, rows_im = pl.ds(h * SUB, SUB), pl.ds(modes + h * SUB, SUB)
                for b in range(count):
                    e_ref[b, rows, at] = e_re[b][h]
                    e_ref[b, rows_im, at] = e_im[b][h]
                gate = cmul(pow_re[h], pow_im[h], p_re[h], p_im[h])
                level = [(e_re[b][h], e_im[b][h]) for b in range(count)]
                step = 0
                while len(level) > 1:
                    pairs = range(0, len(level), 2)
                    level = [
                        advance(gate, flag(("tree", step + i // 2), LANE), level[i], level[i + 1]) for i in pairs
                    ]
                    step += len(pairs)
                    gate = cmul(*gate, *gate)
                end_ref[rows, at] = level[0][0].astype(BF16)
                end_ref[rows_im, at] = level[0][1].astype(BF16)

        lane_tiles = wide // LANE
        gated(0, PIECE)
        for i in range(lane_tiles):
            following = (i // (PIECE // LANE) + 1) * (PIECE // LANE)
            if i % (PIECE // LANE) == 0 and following < lane_tiles:
                gated(following, PIECE)
            states(i)


def middle_kernel(lengths_ref, features_ref, halo_ref, taps_ref, z_ref, skip_ref, pole_ref,
                  coef_ref, base_ref, gain_ref, first_s, part_s, z_s, filt_s, acc_s, shift_s, piece_s, *, mine):
    tokens, half = z_ref.shape
    count = tokens // BLK
    modes = pole_ref.shape[0] // 2
    halves = modes // SUB
    starts = starts_of(lengths_ref, lax.axis_index("seq") * tokens)
    edges = edge_flags(starts)
    t = row_iota(tokens)
    t0 = t & (-BLK)
    piece = jnp.zeros((tokens, LANE), jnp.int32)
    opened = jnp.zeros((tokens, LANE), jnp.bool_)
    for s in starts:
        piece = piece + jnp.where((s > t0) & (s <= t), 1, 0)
        opened = opened | ((s >= t0) & (s <= t))
    part_s[...] = piece.astype(F32)
    first_s[...] = jnp.where(opened, 0.0, 1.0)
    shift_s[...] = shift_matrix(starts, tokens)

    pieces = []
    for b in range(count):
        inside = jnp.int32(1)
        for s in starts:
            inside = inside + ((s > b * BLK) & (s < (b + 1) * BLK)).astype(jnp.int32)
        pieces.append(inside)
    wide = TILE

    @pl.loop(0, half // wide)
    def _(part):
        here = pl.ds(pl.multiple_of(part * wide, LANE), wide)
        lanes = half_lanes(mine, half, part * wide, wide)
        conv1 = short_filter(features_ref[1, :, lanes], halo_ref[1, :, lanes], taps_ref[1, :, lanes], shift_s, edges)
        base_ref[:, here] = conv1
        for i in range(wide // LANE):
            inner = pl.ds(pl.multiple_of(part * wide + i * LANE, LANE), LANE)
            gain_ref[:, inner] = conv1[:, i * LANE : (i + 1) * LANE] * first_s[...]

    @pl.loop(0, half // LANE)
    def _(tile):
        here = lane_tile(tile)
        lanes = half_lanes(mine, half, tile * LANE, LANE)
        p_re = [rows_of(pole_ref, h, lanes) for h in range(halves)]
        p_im = [rows_of(pole_ref, halves + h, lanes) for h in range(halves)]
        q_re = [rows_of(coef_ref, h, lanes) for h in range(halves)]
        q_im = [rows_of(coef_ref, halves + h, lanes) for h in range(halves)]
        filt_s[pl.ds(0, BLK), :] = jnp.zeros((BLK, LANE), F32)
        for group in range(BLK // SUB):
            parts = []
            for k in range(SUB):
                parts.append(sum(q_re[1:], q_re[0]))
                for h in range(halves):
                    q_re[h], q_im[h] = cmul(q_re[h], q_im[h], p_re[h], p_im[h])
            filt_s[pl.ds(BLK + group * SUB, SUB), :] = column_sums(parts).astype(BF16).astype(F32)
        z = z_ref[:, here].astype(F32)
        z_s[0:tokens, :] = z
        acc = skip_ref[:, lanes] * z
        sums = [[acc[b * BLK + r * SUB : b * BLK + (r + 1) * SUB] for r in range(BLK // SUB)] for b in range(count)]
        for s in range(BLK):
            firsts = range(s // SUB, BLK // SUB)
            columns = {r: filt_s[pl.ds(BLK - s + r * SUB, SUB), :] for r in firsts}
            for b in range(count):
                value = z_s[pl.ds(b * BLK + s, SUB, stride=0), :]
                for r in firsts:
                    sums[b][r] = sums[b][r] + columns[r] * value
        for b in range(count):
            for r in range(BLK // SUB):
                acc_s[pl.ds(b * BLK + r * SUB, SUB), :] = sums[b][r]

        for b in range(count):
            @pl.when(pieces[b] > 1)
            def _(b=b):
                rows = pl.ds(b * BLK, BLK)
                acc_s[rows, :] = skip_ref[:, lanes] * z_s[rows, :]

                def one_piece(q, carry):
                    member = part_s[rows, :] == q.astype(F32)
                    piece_s[...] = jnp.where(member, z_s[rows, :], 0.0)
                    total = jnp.zeros((BLK, LANE), F32)
                    for s in range(BLK):
                        total = total + filt_s[pl.ds(BLK - s, BLK), :] * piece_s[pl.ds(s, 1), :]
                    acc_s[rows, :] = acc_s[rows, :] + jnp.where(member, total, 0.0)
                    return carry

                lax.fori_loop(0, pieces[b], one_piece, 0)

        base_ref[:, here] = base_ref[:, here] * acc_s[...]


def prepare_kernel(lengths_ref, e_ref, pole_ref, coef_ref, table_ref, local_ref, reach_ref, turn_s, *, mine):
    count, packed, half = e_ref.shape
    modes = packed // 2
    halves = modes // SUB
    starts = starts_of(lengths_ref, lax.axis_index("seq") * count * BLK)
    flags = block_flags(starts, count)
    pitch = turn_s.shape[0] // BLK

    @pl.loop(0, half // LANE)
    def _(tile):
        here = lane_tile(tile)
        lanes = half_lanes(mine, half, tile * LANE, LANE)
        for h in range(halves):
            rows, rows_im = pl.ds(h * SUB, SUB), pl.ds(modes + h * SUB, SUB)
            p = pole_ref[rows, lanes], pole_ref[rows_im, lanes]
            q = coef_ref[rows, lanes], coef_ref[rows_im, lanes]
            for k in range(BLK):
                q = cmul(*q, *p)
                turn_s[pl.ds(k * pitch + h * SUB, SUB), :] = q[0]
                turn_s[pl.ds(k * pitch + modes + h * SUB, SUB), :] = -q[1]
            gate = p
            for _ in range(BLK.bit_length() - 1):
                gate = cmul(*gate, *gate)
            zero = jnp.zeros((SUB, LANE), F32)
            state, reach = (zero, zero), (zero + 1.0, zero)
            for b in range(count):
                local_ref[b, rows, here], local_ref[b, rows_im, here] = state
                reach_ref[b, rows, here], reach_ref[b, rows_im, here] = reach
                if b < count - 1:
                    state = advance(gate, flags[b], state, (e_ref[b, rows, here], e_ref[b, rows_im, here]))
                    reach = tuple(flags[b] * x for x in cmul(*gate, *reach))
        for m in range(packed):
            for r in range(BLK // SUB):
                table_ref[m, pl.ds(r * SUB, SUB), here] = turn_s[pl.ds(r * SUB * pitch + m, SUB, stride=pitch), :]


def split(ref, lanes, *lead):
    modes = ref.shape[-2] // 2
    packed = ref[(*lead, slice(None), lanes)].astype(F32)
    return packed[:modes], packed[modes:]


def store(ref, lanes, pair):
    modes = ref.shape[-2] // 2
    ref[0:modes, lanes] = pair[0].astype(ref.dtype)
    ref[modes : 2 * modes, lanes] = pair[1].astype(ref.dtype)


def advance(gate, flag, state, addend):
    re, im = cmul(*gate, *state)
    return addend[0] + flag * re, addend[1] + flag * im


def choose(flag, a, b):
    return tuple(jnp.where(flag, x, y) for x, y in zip(a, b))


def first_kernel(kept_ref, came_ref, pole_ref, flags_ref, total_ref, send_ref, gate_ref, *, tokens):
    half = kept_ref.shape[1]
    rows_at = flag_rows(1)
    shape = kept_ref.shape[0] // 2, CHUNK

    @pl.loop(0, half // CHUNK)
    def _(part):
        def flag(name):
            return jnp.broadcast_to(flags_ref[rows_at[name] : rows_at[name] + 1, :], shape)

        lanes = pl.ds(pl.multiple_of(part * CHUNK, LANE), CHUNK)
        kept, came = split(kept_ref, lanes), split(came_ref, lanes)
        gate = split(pole_ref, half_lanes(True, half, part * CHUNK, CHUNK))
        odd = flag("odd") > 0.5
        reach = 1
        while reach < tokens:
            gate = cmul(*gate, *gate)
            reach *= 2
        total = advance(gate, flag("second"), choose(odd, came, kept), choose(odd, kept, came))
        store(total_ref, lanes, total)
        store(send_ref, lanes, total)
        store(gate_ref, lanes, gate)


def round_kernel(total_ref, met_ref, flags_ref, *refs, k, rounds):
    rows_at = flag_rows(rounds)
    shape = met_ref.shape[0] // 2, CHUNK

    @pl.loop(0, met_ref.shape[1] // CHUNK)
    def _(part):
        def flag(name):
            return jnp.broadcast_to(flags_ref[rows_at[name] : rows_at[name] + 1, :], shape)

        lanes = pl.ds(pl.multiple_of(part * CHUNK, LANE), CHUNK)
        rest = list(refs)
        met, total = split(met_ref, lanes), split(total_ref, lanes)
        power = split(rest.pop(0), lanes)
        enter = flag(("enter", k))
        if k == 1:
            prefix = tuple(enter * x for x in met)
        else:
            before, prefix = split(rest.pop(0), lanes), split(rest.pop(0), lanes)
            prefix = advance(before, enter, met, prefix)
        if k < rounds - 1:
            total_out, send_ref, power_out, before_out, prefix_out = rest
            upper = flag(("upper", k)) > 0.5
            power = cmul(*power, *power)
            total = advance(power, flag(("whole", k)), choose(upper, met, total), choose(upper, total, met))
            store(total_out, lanes, total)
            store(send_ref, lanes, total)
            store(prefix_out, lanes, prefix)
            store(power_out, lanes, power)
            if k == 1:
                before = choose(upper, power, (jnp.ones_like(met[0]), jnp.zeros_like(met[0])))
            else:
                before = choose(upper, cmul(*before, *power), before)
            store(before_out, lanes, before)
        else:
            gate_ref, kept_ref, came_ref, own_ref, send_ref = rest
            odd = flag("odd") > 0.5
            kept, came = split(kept_ref, lanes), split(came_ref, lanes)
            beyond = advance(split(gate_ref, lanes), flag("even"), prefix, choose(odd, came, kept))
            store(own_ref, lanes, choose(odd, beyond, prefix))
            store(send_ref, lanes, choose(odd, prefix, beyond))


def back_kernel(entry_ref, table_ref, local_ref, reach_ref, base_ref, gain_ref, *refs, mine):
    out_hbm, out_ref, state_s, sems = refs[-4:]
    tokens, half = out_ref.shape
    width = TILE
    count, packed, _ = local_ref.shape
    modes = packed // 2
    halves = modes // SUB
    def one_tile(tile, state_s):
        lanes = here = lane_tile(tile)
        entry = entry_ref[:, here].astype(F32)
        for h in range(halves):
            rows, rows_im = pl.ds(h * SUB, SUB), pl.ds(modes + h * SUB, SUB)
            first = entry[h * SUB : (h + 1) * SUB], entry[modes + h * SUB : modes + (h + 1) * SUB]
            for b in range(count):
                state = first
                if b:
                    state = cmul(reach_ref[b, rows, here], reach_ref[b, rows_im, here], *first)
                    state = state[0] + local_ref[b, rows, here], state[1] + local_ref[b, rows_im, here]
                state_s[pl.ds(b * packed + h * SUB, SUB), :] = state[0]
                state_s[pl.ds(b * packed + modes + h * SUB, SUB), :] = state[1]
        sums = [[None] * (BLK // SUB) for _ in range(count)]
        for m in range(packed):
            turn = [table_ref[m, pl.ds(r * SUB, SUB), here] for r in range(BLK // SUB)]
            for b in range(count):
                state = state_s[pl.ds(b * packed + m, SUB, stride=0), :]
                for r in range(BLK // SUB):
                    term = turn[r] * state
                    sums[b][r] = term if m == 0 else sums[b][r] + term
        for b in range(count):
            rows = pl.ds(b * BLK, BLK)
            carried = jnp.concatenate(sums[b], axis=0)
            out_ref[rows, lanes] = (base_ref[rows, here] + gain_ref[rows, here] * carried).astype(BF16)

    def leaving(j):
        lanes = half_lanes(mine, half, j * width, width)
        here = pl.ds(pl.multiple_of(j * width, LANE), width)
        return pltpu.make_async_copy(out_ref.at[:, here], out_hbm.at[:, lanes], sems.at[j])

    @pl.loop(0, half // width)
    def _(j):
        @pl.loop(0, width // LANE // state_s.shape[0])
        def _(step):
            for v in range(state_s.shape[0]):
                one_tile(j * (width // LANE) + step * state_s.shape[0] + v, state_s.at[v])

        leaving(j).start()

    for j in range(half // width):
        leaving(j).wait()


def per_device(features, kernel, skip, residues, decay, freq, lengths):
    tokens = features.shape[1]
    modes, width = decay.shape
    half = width // 2
    count = tokens // BLK
    n = lax.axis_size("seq")
    place = lax.axis_index("seq")
    core = place % 2
    rounds = n.bit_length() - 1

    rim = features[:, tokens - 2 :, :]
    halo = lax.ppermute(rim, "seq", [(i, (i + 1) % n) for i in range(n)])

    params = pltpu.CompilerParams(vmem_limit_bytes=16 * 1024 * 1024)
    roomy = pltpu.CompilerParams(vmem_limit_bytes=ROOM * 1024 * 1024)
    plane = pltpu.VMEM((tokens, LANE), F32)
    shifts = pltpu.VMEM((2 * tokens, tokens), BF16)
    whole = pl.BlockSpec(memory_space=pltpu.VMEM)

    def call(body, args, outs, name, scratch=(), cost=0.8e9, ragged=False, spec=whole, limit=params):
        return pl.pallas_call(
            body,
            grid_spec=pltpu.PrefetchScalarGridSpec(
                num_scalar_prefetch=int(ragged), grid=(), in_specs=[spec] * len(args), out_specs=[whole] * len(outs),
                scratch_shapes=scratch,
            ),
            out_shape=[jax.ShapeDtypeStruct(*o) for o in outs],
            compiler_params=limit, name=name,
            cost_estimate=pl.CostEstimate(flops=int(cost), bytes_accessed=1 << 20, transcendentals=0),
        )(*((lengths,) if ragged else ()), *args)

    packed = 2 * modes
    state, sent = ((packed, half), F32), ((packed, half), BF16)
    blocks, plain = ((count, packed, half), F32), ((tokens, half), F32)

    flag_count = -(-len(flag_rows(rounds)) // SUB) * SUB
    streams, shift, last_mask, flags = call(
        functools.partial(prelude_kernel, rounds=rounds), (features,),
        (((2, tokens, width), BF16), ((2 * tokens, tokens), BF16), ((tokens, LANE), F32), ((flag_count, CHUNK), F32)),
        "prelude", [pltpu.SemaphoreType.DMA((2, 4))], ragged=True, spec=pl.BlockSpec(memory_space=pl.ANY), limit=roomy,
        cost=1.2e9,
    )

    table = ((packed, width), F32)
    pole, coef = call(tables_kernel, (decay, freq, residues), (table, table), "tables", cost=0.5e9)

    def front(mine):
        return call(
            functools.partial(front_kernel, mine=mine), (streams, halo, kernel, pole, shift, last_mask, flags),
            (((tokens, half), BF16), blocks, sent), "front", [pltpu.VMEM((TILE // LANE, tokens + SUB, LANE), F32)], cost=5e9,
        )

    def middle(mine, z):
        return call(
            functools.partial(middle_kernel, mine=mine), (features, halo, kernel, z, skip[None], pole, coef),
            (plain, plain), "middle", [plane, plane, pltpu.VMEM((tokens + SUB, LANE), F32), pltpu.VMEM((2 * BLK, LANE), F32), plane, shifts, pltpu.VMEM((BLK, LANE), F32)], cost=5e9, ragged=True,
        )

    def prepare(mine, e):
        return call(
            functools.partial(prepare_kernel, mine=mine), (e, pole, coef),
            (((packed, BLK, half), F32), blocks, blocks), "prepare", [pltpu.VMEM((BLK * PITCH, LANE), F32)], cost=2.5e9, ragged=True,
        )

    def back(mine, args, out):
        specs = [whole] * len(args)
        if out is not None:
            args, specs = args + (out,), specs + [pl.BlockSpec(memory_space=pl.ANY)]

        return pl.pallas_call(
            functools.partial(back_kernel, mine=mine),
            in_specs=specs, out_specs=pl.BlockSpec(memory_space=pl.ANY),
            out_shape=jax.ShapeDtypeStruct((tokens, width), BF16),
            scratch_shapes=[pltpu.VMEM((tokens, half), BF16), pltpu.VMEM((UNROLL, count * packed + SUB, LANE), F32),
                            pltpu.SemaphoreType.DMA((half // TILE,))],
            input_output_aliases={} if out is None else {len(args) - 1: 0},
            compiler_params=params, name="back",
            cost_estimate=pl.CostEstimate(flops=3_500_000_000, bytes_accessed=1 << 20, transcendentals=0),
        )(*args)

    z_other, e_other, end_other = front(False)
    came = exchange(end_other, 1)
    z_own, e_own, end_own = front(True)
    total, send, gate = call(
        functools.partial(first_kernel, tokens=tokens), (end_own, came, pole, flags), (state, sent, state), "first"
    )
    power, carry = gate, ()
    jobs = [lambda z: middle(True, z), lambda z: middle(False, z), lambda es: (*prepare(True, es[0]), *prepare(False, es[1]))]
    inputs = [z_own, z_other, (e_own, e_other)]
    ready = []
    for k in range(1, rounds):
        last = k == rounds - 1
        met = exchange(send, 1 << k)
        for job, operand in [(jobs.pop(0), inputs.pop(0)) for _ in range(len(jobs) if last else min(1, len(jobs)))]:
            operand, send = lax.optimization_barrier((operand, send))
            met, done = lax.optimization_barrier((met, job(operand)))
            ready.append(done)
        body = functools.partial(round_kernel, k=k, rounds=rounds)
        args = (total, met, flags, power, *carry)
        if last:
            own, send = call(body, args + (gate, end_own, came), (state, sent), "round")
        else:
            total, send, power, *carry = call(body, args, (state, sent, state, state, state), "round")
    other = exchange(send, 1)
    out = back(True, (own, *ready[2][:3], *ready[0]), None)
    return back(False, (other, *ready[2][3:], *ready[1]), out)


def solution(mesh):
    return jax.shard_map(
        per_device,
        mesh=mesh,
        in_specs=(P(None, ("groups", "seq"), None), P(), P(), P(), P(), P(), P("groups")),
        out_specs=P(("groups", "seq"), None),
        check_vma=False,
    )
```

```python
import functools

import jax
import jax.numpy as jnp
from jax import lax
from jax.experimental import pallas as pl
from jax.experimental.pallas import tpu as pltpu
from jax.sharding import PartitionSpec as P

BLK = 16
LANE = 128
SUB = 8
TILE = 512
PITCH = 40
ROOM = 50
PIECE = 256
CHUNK = 512
UNROLL = 2
F32 = jnp.float32
BF16 = jnp.bfloat16


def exchange(block, distance):
    devices = range(lax.axis_size("seq"))
    return lax.ppermute(block, "seq", [(i, i ^ distance) for i in devices])


def row_iota(rows):
    return lax.broadcasted_iota(jnp.int32, (rows, LANE), 0)


def starts_of(lengths_ref, origin):
    starts, at = [], -origin
    for i in range(lengths_ref.shape[0]):
        starts.append(at)
        at = at + lengths_ref[i]
    return starts


def none_in(starts, first, beyond):
    hit = jnp.int32(0)
    for s in starts:
        hit = hit | ((s >= first) & (s < beyond)).astype(jnp.int32)
    return (1 - hit).astype(F32)


def block_flags(starts, count):
    return [none_in(starts, b * BLK, (b + 1) * BLK) for b in range(count)]


def shift_matrix(starts, tokens):
    t = lax.broadcasted_iota(jnp.int32, (tokens, tokens), 0)
    u = lax.broadcasted_iota(jnp.int32, (tokens, tokens), 1)
    last = jnp.full((tokens, tokens), -(1 << 30), jnp.int32)
    for s in starts:
        last = jnp.maximum(last, jnp.where(s <= t, s, -(1 << 30)))
    one = jnp.where((u == t - 1) & (u >= last), 1.0, 0.0)
    two = jnp.where((u == t - 2) & (u >= last), 1.0, 0.0)
    return jnp.concatenate([one, two], axis=0).astype(BF16)


def edge_flags(starts):
    return none_in(starts, 0, 1), none_in(starts, -1, 1), none_in(starts, 0, 2)


def short_filter(rows, halo, taps, shift_ref, edges):
    tokens, width = rows.shape
    moved = jnp.dot(shift_ref[...], rows, preferred_element_type=F32)
    behind, further = moved[:tokens], moved[tokens:]
    edge = halo.astype(F32)
    far, near = edge[0:1, :], edge[1:2, :]
    row = lax.broadcasted_iota(jnp.int32, (SUB, width), 0)
    top = behind[:SUB] + jnp.where(row == 0, near * edges[0], 0.0)
    behind = jnp.concatenate([top, behind[SUB:]], axis=0)
    top = further[:SUB] + jnp.where(row == 0, far * edges[1], jnp.where(row == 1, near * edges[2], 0.0))
    further = jnp.concatenate([top, further[SUB:]], axis=0)
    return taps[0:1, :] * rows.astype(F32) + taps[1:2, :] * behind + taps[2:3, :] * further


def lane_tile(tile):
    return pl.ds(pl.multiple_of(tile * LANE, LANE), LANE)


def cmul(a_re, a_im, b_re, b_im):
    return a_re * b_re - a_im * b_im, a_re * b_im + a_im * b_re


def column_sums(parts):
    row = lax.broadcasted_iota(jnp.int32, (SUB, LANE), 0)
    low = row < 4
    level = []
    for b in range(4):
        keep = jnp.where(low, parts[b], parts[b + 4])
        move = jnp.where(low, parts[b + 4], parts[b])
        level.append(keep + pltpu.roll(move, 4, 0))
    for step in (2, 1):
        clear = (row & step) == 0
        level = [
            jnp.where(
                clear,
                level[b] + pltpu.roll(level[b], SUB - step, 0),
                level[b + step] + pltpu.roll(level[b + step], step, 0),
            )
            for b in range(step)
        ]
    return level[0]


def rows_of(ref, h, lanes):
    return ref[pl.ds(h * SUB, SUB), lanes]


def half_lanes(mine, half, offset, size):
    core = lax.axis_index("seq") & 1
    core = core if mine else 1 - core
    return pl.ds(pl.multiple_of(core * half + offset, LANE), size)


def flag_rows(rounds):
    names = ["odd", "second", "even", "edge0", "edge1", "edge2"] + [("tree", i) for i in range(16)]
    names += [(kind, k) for k in range(1, rounds) for kind in ("upper", "enter", "whole")]
    return {name: i for i, name in enumerate(names)}


def prelude_kernel(lengths_ref, features_ref, streams_ref, shift_ref, last_ref, flags_ref, sems, *, rounds):
    size = streams_ref.shape[1] // sems.shape[1]
    copies = [
        pltpu.make_async_copy(
            features_ref.at[r, pl.ds(j * size, size), :], streams_ref.at[u, pl.ds(j * size, size), :], sems.at[u, j]
        )
        for u, r in enumerate((0, 2))
        for j in range(sems.shape[1])
    ]
    for copy in copies:
        copy.start()
    tokens = streams_ref.shape[1]
    place = lax.axis_index("seq")
    starts = starts_of(lengths_ref, place * tokens)
    t = row_iota(tokens)
    last = jnp.full((tokens, LANE), -1, jnp.int32)
    for s in starts:
        last = jnp.maximum(last, jnp.where(s <= (t | (BLK - 1)), s, -1))
    last_ref[...] = jnp.where(t >= last, 1.0, 0.0)
    shift_ref[...] = shift_matrix(starts, tokens)
    values = dict(zip(("edge0", "edge1", "edge2"), edge_flags(starts)))
    span, i = BLK, 0
    while span < tokens:
        for first in range(span, tokens, 2 * span):
            values["tree", i] = none_in(starts, first, first + span)
            i += 1
        span *= 2
    starts = starts_of(lengths_ref, 0)
    even, second = place & -2, place | 1
    values["odd"] = (place & 1).astype(F32)
    values["even"] = none_in(starts, even * tokens, (even + 1) * tokens)
    values["second"] = none_in(starts, second * tokens, (second + 1) * tokens)
    for k in range(1, rounds):
        distance = 1 << k
        upper = ((place >> k) & 1).astype(F32)
        group = (place >> k) << k
        later = group | distance
        values["upper", k] = upper
        values["enter", k] = upper * none_in(starts, group * tokens, even * tokens)
        values["whole", k] = none_in(starts, later * tokens, (later + distance) * tokens)
    for name, row in flag_rows(rounds).items():
        if name in values:
            flags_ref[row : row + 1, :] = jnp.full((1, CHUNK), values[name], F32)
    for copy in copies:
        copy.wait()


def tables_kernel(decay_ref, freq_ref, residues_ref, pole_ref, coef_ref):
    modes, width = decay_ref.shape

    @pl.loop(0, width // CHUNK)
    def _(part):
        lanes = pl.ds(pl.multiple_of(part * CHUNK, LANE), CHUNK)
        decay, x = decay_ref[:, lanes], freq_ref[:, lanes]
        fade = jnp.exp(-decay)
        q = x * x
        sine = x * (1 + q * (-1 / 6 + q * (1 / 120 + q * (-1 / 5040 + q * (1 / 362880)))))
        cosine = 1 + q * (-1 / 2 + q * (1 / 24 + q * (-1 / 720 + q * (1 / 40320 - q * (1 / 3628800)))))
        store(pole_ref, lanes, (fade * cosine, fade * sine))
        d = 2 * decay
        scale = jnp.sqrt(d * (1 - d * (1 / 2 - d * (1 / 6 - d * (1 / 24 - d * (1 / 120 - d * (1 / 720)))))))
        store(coef_ref, lanes, (residues_ref[0, :, lanes] * scale, residues_ref[1, :, lanes] * scale))


def front_kernel(streams_ref, halo_ref, taps_ref, pole_ref, shift_s, last_s, flags_ref, z_ref, e_ref, end_ref, z_s, *, mine):
    tokens, half = z_ref.shape
    count = tokens // BLK
    modes = pole_ref.shape[0] // 2
    halves = modes // SUB
    wide = TILE
    rows_at = flag_rows(1)

    def flag(name, size):
        return flags_ref[rows_at[name] : rows_at[name] + 1, 0:size]

    edges = [flag(name, PIECE) for name in ("edge0", "edge1", "edge2")]

    @pl.loop(0, half // wide)
    def _(j):
        def gated(i, size):
            at = pl.ds(pl.multiple_of(j * wide + i * LANE, LANE), size)
            lanes = half_lanes(mine, half, j * wide + i * LANE, size)
            conv0, conv2 = (
                short_filter(streams_ref[u, :, lanes], halo_ref[r, :, lanes], taps_ref[r, :, lanes], shift_s, edges)
                for u, r in enumerate((0, 2))
            )
            z = (conv0 * conv2).astype(BF16)
            z_ref[:, at] = z
            for v in range(size // LANE):
                z_s[i + v, 0:tokens, :] = z[:, v * LANE : (v + 1) * LANE].astype(F32) * last_s[...]

        def states(i):
            at = pl.ds(pl.multiple_of(j * wide + i * LANE, LANE), LANE)
            lanes = half_lanes(mine, half, j * wide + i * LANE, LANE)
            z_i = z_s.at[i]
            p_re = [rows_of(pole_ref, h, lanes) for h in range(halves)]
            p_im = [rows_of(pole_ref, halves + h, lanes) for h in range(halves)]
            pow_re, pow_im = list(p_re), list(p_im)
            e_re, e_im = [], []
            for b in range(count):
                now = z_i[pl.ds(b * BLK + BLK - 1, SUB, stride=0), :]
                prev = z_i[pl.ds(b * BLK + BLK - 2, SUB, stride=0), :]
                e_re.append([now + p_re[h] * prev for h in range(halves)])
                e_im.append([p_im[h] * prev for h in range(halves)])
            for k in range(2, BLK):
                for h in range(halves):
                    pow_re[h], pow_im[h] = cmul(pow_re[h], pow_im[h], p_re[h], p_im[h])
                for b in range(count):
                    now = z_i[pl.ds(b * BLK + BLK - 1 - k, SUB, stride=0), :]
                    for h in range(halves):
                        e_re[b][h] = e_re[b][h] + pow_re[h] * now
                        e_im[b][h] = e_im[b][h] + pow_im[h] * now
            for h in range(halves):
                rows, rows_im = pl.ds(h * SUB, SUB), pl.ds(modes + h * SUB, SUB)
                for b in range(count):
                    e_ref[b, rows, at] = e_re[b][h]
                    e_ref[b, rows_im, at] = e_im[b][h]
                gate = cmul(pow_re[h], pow_im[h], p_re[h], p_im[h])
                level = [(e_re[b][h], e_im[b][h]) for b in range(count)]
                step = 0
                while len(level) > 1:
                    pairs = range(0, len(level), 2)
                    level = [
                        advance(gate, flag(("tree", step + i // 2), LANE), level[i], level[i + 1]) for i in pairs
                    ]
                    step += len(pairs)
                    gate = cmul(*gate, *gate)
                end_ref[rows, at] = level[0][0].astype(BF16)
                end_ref[rows_im, at] = level[0][1].astype(BF16)

        lane_tiles = wide // LANE
        gated(0, PIECE)
        for i in range(lane_tiles):
            following = (i // (PIECE // LANE) + 1) * (PIECE // LANE)
            if i % (PIECE // LANE) == 0 and following < lane_tiles:
                gated(following, PIECE)
            states(i)


def middle_kernel(lengths_ref, features_ref, halo_ref, taps_ref, z_ref, skip_ref, pole_ref,
                  coef_ref, base_ref, gain_ref, first_s, part_s, z_s, filt_s, acc_s, shift_s, piece_s, *, mine):
    tokens, half = z_ref.shape
    count = tokens // BLK
    modes = pole_ref.shape[0] // 2
    halves = modes // SUB
    starts = starts_of(lengths_ref, lax.axis_index("seq") * tokens)
    edges = edge_flags(starts)
    t = row_iota(tokens)
    t0 = t & (-BLK)
    piece = jnp.zeros((tokens, LANE), jnp.int32)
    opened = jnp.zeros((tokens, LANE), jnp.bool_)
    for s in starts:
        piece = piece + jnp.where((s > t0) & (s <= t), 1, 0)
        opened = opened | ((s >= t0) & (s <= t))
    part_s[...] = piece.astype(F32)
    first_s[...] = jnp.where(opened, 0.0, 1.0)
    shift_s[...] = shift_matrix(starts, tokens)

    pieces = []
    for b in range(count):
        inside = jnp.int32(1)
        for s in starts:
            inside = inside + ((s > b * BLK) & (s < (b + 1) * BLK)).astype(jnp.int32)
        pieces.append(inside)
    wide = TILE

    @pl.loop(0, half // wide)
    def _(part):
        here = pl.ds(pl.multiple_of(part * wide, LANE), wide)
        lanes = half_lanes(mine, half, part * wide, wide)
        conv1 = short_filter(features_ref[1, :, lanes], halo_ref[1, :, lanes], taps_ref[1, :, lanes], shift_s, edges)
        base_ref[:, here] = conv1
        for i in range(wide // LANE):
            inner = pl.ds(pl.multiple_of(part * wide + i * LANE, LANE), LANE)
            gain_ref[:, inner] = conv1[:, i * LANE : (i + 1) * LANE] * first_s[...]

    @pl.loop(0, half // LANE)
    def _(tile):
        here = lane_tile(tile)
        lanes = half_lanes(mine, half, tile * LANE, LANE)
        p_re = [rows_of(pole_ref, h, lanes) for h in range(halves)]
        p_im = [rows_of(pole_ref, halves + h, lanes) for h in range(halves)]
        q_re = [rows_of(coef_ref, h, lanes) for h in range(halves)]
        q_im = [rows_of(coef_ref, halves + h, lanes) for h in range(halves)]
        filt_s[pl.ds(0, BLK), :] = jnp.zeros((BLK, LANE), F32)
        for group in range(BLK // SUB):
            parts = []
            for k in range(SUB):
                parts.append(sum(q_re[1:], q_re[0]))
                for h in range(halves):
                    q_re[h], q_im[h] = cmul(q_re[h], q_im[h], p_re[h], p_im[h])
            filt_s[pl.ds(BLK + group * SUB, SUB), :] = column_sums(parts).astype(BF16).astype(F32)
        z = z_ref[:, here].astype(F32)
        z_s[0:tokens, :] = z
        acc = skip_ref[:, lanes] * z
        sums = [[acc[b * BLK + r * SUB : b * BLK + (r + 1) * SUB] for r in range(BLK // SUB)] for b in range(count)]
        for s in range(BLK):
            firsts = range(s // SUB, BLK // SUB)
            columns = {r: filt_s[pl.ds(BLK - s + r * SUB, SUB), :] for r in firsts}
            for b in range(count):
                value = z_s[pl.ds(b * BLK + s, SUB, stride=0), :]
                for r in firsts:
                    sums[b][r] = sums[b][r] + columns[r] * value
        for b in range(count):
            for r in range(BLK // SUB):
                acc_s[pl.ds(b * BLK + r * SUB, SUB), :] = sums[b][r]

        for b in range(count):
            @pl.when(pieces[b] > 1)
            def _(b=b):
                rows = pl.ds(b * BLK, BLK)
                acc_s[rows, :] = skip_ref[:, lanes] * z_s[rows, :]

                def one_piece(q, carry):
                    member = part_s[rows, :] == q.astype(F32)
                    piece_s[...] = jnp.where(member, z_s[rows, :], 0.0)
                    total = jnp.zeros((BLK, LANE), F32)
                    for s in range(BLK):
                        total = total + filt_s[pl.ds(BLK - s, BLK), :] * piece_s[pl.ds(s, 1), :]
                    acc_s[rows, :] = acc_s[rows, :] + jnp.where(member, total, 0.0)
                    return carry

                lax.fori_loop(0, pieces[b], one_piece, 0)

        base_ref[:, here] = base_ref[:, here] * acc_s[...]


def prepare_kernel(lengths_ref, e_ref, pole_ref, coef_ref, table_ref, local_ref, reach_ref, turn_s, *, mine):
    count, packed, half = e_ref.shape
    modes = packed // 2
    halves = modes // SUB
    starts = starts_of(lengths_ref, lax.axis_index("seq") * count * BLK)
    flags = block_flags(starts, count)
    pitch = turn_s.shape[0] // BLK

    @pl.loop(0, half // LANE)
    def _(tile):
        here = lane_tile(tile)
        lanes = half_lanes(mine, half, tile * LANE, LANE)
        for h in range(halves):
            rows, rows_im = pl.ds(h * SUB, SUB), pl.ds(modes + h * SUB, SUB)
            p = pole_ref[rows, lanes], pole_ref[rows_im, lanes]
            q = coef_ref[rows, lanes], coef_ref[rows_im, lanes]
            for k in range(BLK):
                q = cmul(*q, *p)
                turn_s[pl.ds(k * pitch + h * SUB, SUB), :] = q[0]
                turn_s[pl.ds(k * pitch + modes + h * SUB, SUB), :] = -q[1]
            gate = p
            for _ in range(BLK.bit_length() - 1):
                gate = cmul(*gate, *gate)
            zero = jnp.zeros((SUB, LANE), F32)
            state, reach = (zero, zero), (zero + 1.0, zero)
            for b in range(count):
                local_ref[b, rows, here], local_ref[b, rows_im, here] = state
                reach_ref[b, rows, here], reach_ref[b, rows_im, here] = reach
                if b < count - 1:
                    state = advance(gate, flags[b], state, (e_ref[b, rows, here], e_ref[b, rows_im, here]))
                    reach = tuple(flags[b] * x for x in cmul(*gate, *reach))
        for m in range(packed):
            for r in range(BLK // SUB):
                table_ref[m, pl.ds(r * SUB, SUB), here] = turn_s[pl.ds(r * SUB * pitch + m, SUB, stride=pitch), :]


def split(ref, lanes, *lead):
    modes = ref.shape[-2] // 2
    packed = ref[(*lead, slice(None), lanes)].astype(F32)
    return packed[:modes], packed[modes:]


def store(ref, lanes, pair):
    modes = ref.shape[-2] // 2
    ref[0:modes, lanes] = pair[0].astype(ref.dtype)
    ref[modes : 2 * modes, lanes] = pair[1].astype(ref.dtype)


def advance(gate, flag, state, addend):
    re, im = cmul(*gate, *state)
    return addend[0] + flag * re, addend[1] + flag * im


def choose(flag, a, b):
    return tuple(jnp.where(flag, x, y) for x, y in zip(a, b))


def first_kernel(kept_ref, came_ref, pole_ref, flags_ref, total_ref, send_ref, gate_ref, *, tokens):
    half = kept_ref.shape[1]
    rows_at = flag_rows(1)
    shape = kept_ref.shape[0] // 2, CHUNK

    @pl.loop(0, half // CHUNK)
    def _(part):
        def flag(name):
            return jnp.broadcast_to(flags_ref[rows_at[name] : rows_at[name] + 1, :], shape)

        lanes = pl.ds(pl.multiple_of(part * CHUNK, LANE), CHUNK)
        kept, came = split(kept_ref, lanes), split(came_ref, lanes)
        gate = split(pole_ref, half_lanes(True, half, part * CHUNK, CHUNK))
        odd = flag("odd") > 0.5
        reach = 1
        while reach < tokens:
            gate = cmul(*gate, *gate)
            reach *= 2
        total = advance(gate, flag("second"), choose(odd, came, kept), choose(odd, kept, came))
        store(total_ref, lanes, total)
        store(send_ref, lanes, total)
        store(gate_ref, lanes, gate)


def round_kernel(total_ref, met_ref, flags_ref, *refs, k, rounds):
    rows_at = flag_rows(rounds)
    shape = met_ref.shape[0] // 2, CHUNK

    @pl.loop(0, met_ref.shape[1] // CHUNK)
    def _(part):
        def flag(name):
            return jnp.broadcast_to(flags_ref[rows_at[name] : rows_at[name] + 1, :], shape)

        lanes = pl.ds(pl.multiple_of(part * CHUNK, LANE), CHUNK)
        rest = list(refs)
        met, total = split(met_ref, lanes), split(total_ref, lanes)
        power = split(rest.pop(0), lanes)
        enter = flag(("enter", k))
        if k == 1:
            prefix = tuple(enter * x for x in met)
        else:
            before, prefix = split(rest.pop(0), lanes), split(rest.pop(0), lanes)
            prefix = advance(before, enter, met, prefix)
        if k < rounds - 1:
            total_out, send_ref, power_out, before_out, prefix_out = rest
            upper = flag(("upper", k)) > 0.5
            power = cmul(*power, *power)
            total = advance(power, flag(("whole", k)), choose(upper, met, total), choose(upper, total, met))
            store(total_out, lanes, total)
            store(send_ref, lanes, total)
            store(prefix_out, lanes, prefix)
            store(power_out, lanes, power)
            if k == 1:
                before = choose(upper, power, (jnp.ones_like(met[0]), jnp.zeros_like(met[0])))
            else:
                before = choose(upper, cmul(*before, *power), before)
            store(before_out, lanes, before)
        else:
            gate_ref, kept_ref, came_ref, own_ref, send_ref = rest
            odd = flag("odd") > 0.5
            kept, came = split(kept_ref, lanes), split(came_ref, lanes)
            beyond = advance(split(gate_ref, lanes), flag("even"), prefix, choose(odd, came, kept))
            store(own_ref, lanes, choose(odd, beyond, prefix))
            store(send_ref, lanes, choose(odd, prefix, beyond))


def back_kernel(entry_ref, table_ref, local_ref, reach_ref, base_ref, gain_ref, *refs, mine):
    out_hbm, out_ref, state_s, sems = refs[-4:]
    tokens, half = out_ref.shape
    width = TILE
    count, packed, _ = local_ref.shape
    modes = packed // 2
    halves = modes // SUB
    def one_tile(tile, state_s):
        lanes = here = lane_tile(tile)
        entry = entry_ref[:, here].astype(F32)
        for h in range(halves):
            rows, rows_im = pl.ds(h * SUB, SUB), pl.ds(modes + h * SUB, SUB)
            first = entry[h * SUB : (h + 1) * SUB], entry[modes + h * SUB : modes + (h + 1) * SUB]
            for b in range(count):
                state = first
                if b:
                    state = cmul(reach_ref[b, rows, here], reach_ref[b, rows_im, here], *first)
                    state = state[0] + local_ref[b, rows, here], state[1] + local_ref[b, rows_im, here]
                state_s[pl.ds(b * packed + h * SUB, SUB), :] = state[0]
                state_s[pl.ds(b * packed + modes + h * SUB, SUB), :] = state[1]
        sums = [[None] * (BLK // SUB) for _ in range(count)]
        for m in range(packed):
            turn = [table_ref[m, pl.ds(r * SUB, SUB), here] for r in range(BLK // SUB)]
            for b in range(count):
                state = state_s[pl.ds(b * packed + m, SUB, stride=0), :]
                for r in range(BLK // SUB):
                    term = turn[r] * state
                    sums[b][r] = term if m == 0 else sums[b][r] + term
        for b in range(count):
            rows = pl.ds(b * BLK, BLK)
            carried = jnp.concatenate(sums[b], axis=0)
            out_ref[rows, lanes] = (base_ref[rows, here] + gain_ref[rows, here] * carried).astype(BF16)

    def leaving(j):
        lanes = half_lanes(mine, half, j * width, width)
        here = pl.ds(pl.multiple_of(j * width, LANE), width)
        return pltpu.make_async_copy(out_ref.at[:, here], out_hbm.at[:, lanes], sems.at[j])

    @pl.loop(0, half // width)
    def _(j):
        @pl.loop(0, width // LANE // state_s.shape[0])
        def _(step):
            for v in range(state_s.shape[0]):
                one_tile(j * (width // LANE) + step * state_s.shape[0] + v, state_s.at[v])

        leaving(j).start()

    for j in range(half // width):
        leaving(j).wait()


def per_device(features, kernel, skip, residues, decay, freq, lengths):
    tokens = features.shape[1]
    modes, width = decay.shape
    half = width // 2
    count = tokens // BLK
    n = lax.axis_size("seq")
    place = lax.axis_index("seq")
    core = place % 2
    rounds = n.bit_length() - 1

    rim = features[:, tokens - 2 :, :]
    halo = lax.ppermute(rim, "seq", [(i, (i + 1) % n) for i in range(n)])

    params = pltpu.CompilerParams(vmem_limit_bytes=16 * 1024 * 1024)
    roomy = pltpu.CompilerParams(vmem_limit_bytes=ROOM * 1024 * 1024)
    plane = pltpu.VMEM((tokens, LANE), F32)
    shifts = pltpu.VMEM((2 * tokens, tokens), BF16)
    whole = pl.BlockSpec(memory_space=pltpu.VMEM)

    def call(body, args, outs, name, scratch=(), cost=0.8e9, ragged=False, spec=whole, limit=params):
        return pl.pallas_call(
            body,
            grid_spec=pltpu.PrefetchScalarGridSpec(
                num_scalar_prefetch=int(ragged), grid=(), in_specs=[spec] * len(args), out_specs=[whole] * len(outs),
                scratch_shapes=scratch,
            ),
            out_shape=[jax.ShapeDtypeStruct(*o) for o in outs],
            compiler_params=limit, name=name,
            cost_estimate=pl.CostEstimate(flops=int(cost), bytes_accessed=1 << 20, transcendentals=0),
        )(*((lengths,) if ragged else ()), *args)

    packed = 2 * modes
    state, sent = ((packed, half), F32), ((packed, half), BF16)
    blocks, plain = ((count, packed, half), F32), ((tokens, half), F32)

    flag_count = -(-len(flag_rows(rounds)) // SUB) * SUB
    streams, shift, last_mask, flags = call(
        functools.partial(prelude_kernel, rounds=rounds), (features,),
        (((2, tokens, width), BF16), ((2 * tokens, tokens), BF16), ((tokens, LANE), F32), ((flag_count, CHUNK), F32)),
        "prelude", [pltpu.SemaphoreType.DMA((2, 4))], ragged=True, spec=pl.BlockSpec(memory_space=pl.ANY), limit=roomy,
        cost=1.2e9,
    )

    table = ((packed, width), F32)
    pole, coef = call(tables_kernel, (decay, freq, residues), (table, table), "tables", cost=0.5e9)

    def front(mine):
        return call(
            functools.partial(front_kernel, mine=mine), (streams, halo, kernel, pole, shift, last_mask, flags),
            (((tokens, half), BF16), blocks, sent), "front", [pltpu.VMEM((TILE // LANE, tokens + SUB, LANE), F32)], cost=5e9,
        )

    def middle(mine, z):
        return call(
            functools.partial(middle_kernel, mine=mine), (features, halo, kernel, z, skip[None], pole, coef),
            (plain, plain), "middle", [plane, plane, pltpu.VMEM((tokens + SUB, LANE), F32), pltpu.VMEM((2 * BLK, LANE), F32), plane, shifts, pltpu.VMEM((BLK, LANE), F32)], cost=5e9, ragged=True,
        )

    def prepare(mine, e):
        return call(
            functools.partial(prepare_kernel, mine=mine), (e, pole, coef),
            (((packed, BLK, half), F32), blocks, blocks), "prepare", [pltpu.VMEM((BLK * PITCH, LANE), F32)], cost=2.5e9, ragged=True,
        )

    def back(mine, args, out):
        specs = [whole] * len(args)
        if out is not None:
            args, specs = args + (out,), specs + [pl.BlockSpec(memory_space=pl.ANY)]

        return pl.pallas_call(
            functools.partial(back_kernel, mine=mine),
            in_specs=specs, out_specs=pl.BlockSpec(memory_space=pl.ANY),
            out_shape=jax.ShapeDtypeStruct((tokens, width), BF16),
            scratch_shapes=[pltpu.VMEM((tokens, half), BF16), pltpu.VMEM((UNROLL, count * packed + SUB, LANE), F32),
                            pltpu.SemaphoreType.DMA((half // TILE,))],
            input_output_aliases={} if out is None else {len(args) - 1: 0},
            compiler_params=params, name="back",
            cost_estimate=pl.CostEstimate(flops=3_500_000_000, bytes_accessed=1 << 20, transcendentals=0),
        )(*args)

    z_other, e_other, end_other = front(False)
    came = exchange(end_other, 1)
    z_own, e_own, end_own = front(True)
    total, send, gate = call(
        functools.partial(first_kernel, tokens=tokens), (end_own, came, pole, flags), (state, sent, state), "first"
    )
    power, carry = gate, ()
    jobs = [lambda z: middle(True, z), lambda z: middle(False, z), lambda es: (*prepare(True, es[0]), *prepare(False, es[1]))]
    inputs = [z_own, z_other, (e_own, e_other)]
    ready = []
    for k in range(1, rounds):
        last = k == rounds - 1
        met = exchange(send, 1 << k)
        for job, operand in [(jobs.pop(0), inputs.pop(0)) for _ in range(len(jobs) if last else min(1, len(jobs)))]:
            operand, send = lax.optimization_barrier((operand, send))
            met, done = lax.optimization_barrier((met, job(operand)))
            ready.append(done)
        body = functools.partial(round_kernel, k=k, rounds=rounds)
        args = (total, met, flags, power, *carry)
        if last:
            own, send = call(body, args + (gate, end_own, came), (state, sent), "round")
        else:
            total, send, power, *carry = call(body, args, (state, sent, state, state, state), "round")
    other = exchange(send, 1)
    out = back(True, (own, *ready[2][:3], *ready[0]), None)
    return back(False, (other, *ready[2][3:], *ready[1]), out)


def solution(mesh):
    return jax.shard_map(
        per_device,
        mesh=mesh,
        in_specs=(P(None, ("groups", "seq"), None), P(), P(), P(), P(), P(), P("groups")),
        out_specs=P(("groups", "seq"), None),
        check_vma=False,
    )
```
